32 devices in a mesh: shard: 4 (over z), ctx: 8 (over y, x, core).
Axes of the slice: x: 2, y: 2, z: 4, core: 2. Of those that a mesh axis runs over, the one named last changes fastest.
Arguments:
- tokens: bfloat16 [2, 4096, 1024], P(None, ('shard', 'ctx')), may hold values from -6 to 6
- doc_starts: int32 [2, 4, 4], P(None, 'shard'), may hold values from 0 to 1023, as said below
- w_qkv: bfloat16 [1024, 3072], P('shard'), may hold values from -0.1875 to 0.1875
- w_out: bfloat16 [1024, 1024], P('shard'), may hold values from -0.1875 to 0.1875
- w_up: bfloat16 [1024, 4096], P('shard'), may hold values from -0.1875 to 0.1875
- w_down: bfloat16 [4096, 1024], P('shard'), may hold values from -0.09375 to 0.09375
- gains: bfloat16 [1024, 4], P('shard'), may hold values from 0.099609375 to 1.8984375
- cotangent: bfloat16 [2, 4096, 1024], P(None, ('shard', 'ctx')), may hold values from -6 to 6
Outputs:
- layer_out: bfloat16 [2, 4096, 1024], P(None, ('shard', 'ctx'))
- grad_tokens: float32 [2, 4096, 1024], P(None, ('shard', 'ctx'))
- grad_qkv: float32 [1024, 3072], P(('shard', 'ctx'))
- grad_out: float32 [1024, 1024], P(('shard', 'ctx'))
- grad_up: float32 [1024, 4096], P(('shard', 'ctx'))
- grad_down: float32 [4096, 1024], P(('shard', 'ctx'))
- grad_gains: float32 [1024, 4], P(('shard', 'ctx'))
The draws below stay inside these ranges and needn't reach their ends.
Inputs may be any that keep to these rules, and one draw needn't show every extreme that they name: `doc_starts`: in each stream the starts rise strictly and the first is 0; for every stream index s, in at least one micro-batch the last start of stream s is 1023.
All inputs are finite; a program needn't handle non-finite values.
Results may differ from the reference program's by a relative error of at most 0.017.
Values may be sent and summed in bfloat16 or wider, within the bound.
No kernel may reach another device: no remote copies, remote signals or barrier semaphores. Data moves between devices by JAX's collectives and lax.ppermute only.
A program may use at most 256 MiB of HBM per device.

```python
import math
import jax
import jax.numpy as jnp
from jax import lax

D = 1024
HEADS = 16
HDIM = 64
FF = 4096
MB = 2
DOCS = 4
STREAM = 1024
TOKENS = 4096
N_SHARD = 4


def draw_doc_starts(key, part):
    stream_keys = jax.random.split(jax.random.fold_in(key, 17), MB * N_SHARD)
    chosen = jax.random.randint(jax.random.fold_in(key, 29), (N_SHARD,), 0, MB).astype(jnp.int32)
    batch_ids = jnp.repeat(jnp.arange(MB, dtype=jnp.int32), N_SHARD)
    shard_ids = jnp.tile(jnp.arange(N_SHARD, dtype=jnp.int32), MB)
    spanning = batch_ids == chosen[shard_ids]
    tail = jnp.arange(DOCS - 1, dtype=jnp.int32) + (STREAM - DOCS + 1)

    def one_stream(stream_key, span_flag):
        picks = jax.random.permutation(stream_key, STREAM - 1)[:DOCS - 1]
        later = jnp.sort(picks).astype(jnp.int32) + 1
        later = jnp.where(span_flag, tail, later).astype(jnp.int32)
        return jnp.concatenate([jnp.zeros((1,), jnp.int32), later])
    return jax.vmap(one_stream)(stream_keys, spanning).reshape(MB, N_SHARD, DOCS).astype(jnp.int32)


def strengthened(result, key, source, target, shards_of, factor):
    owner, partner = [(jnp.arange(result.shape[position]) // (result.shape[position] // shards_of)).reshape([-1 if axis == position else 1 for axis in range(result.ndim)]) for position in (source, target)]
    chosen = jax.random.permutation(key, shards_of)[partner]
    strong = (owner == chosen) | (owner == (partner + shards_of // 2) % shards_of)
    return jnp.where(strong, factor * result, result)


def steps_of(key, extent, pieces, low, top_value):
    level, own = 1.0, jax.random.fold_in(key, 6)
    for dim, shards_of in pieces:
        heights = jnp.exp(jax.random.uniform(jax.random.fold_in(own, dim), (shards_of,), jnp.float32, low / len(pieces), top_value / len(pieces)))
        level = level * jnp.repeat(heights, extent[dim] // shards_of).reshape([-1 if axis == dim else 1 for axis in range(len(extent))])
    return level


def noise(own_key, dims, deviation, bound, shards=(), held_as=jnp.bfloat16):
    loudness = steps_of(own_key, dims, shards, -0.22, 0.18) if shards else 1.0
    result = jax.random.normal(own_key, dims, jnp.float32) * deviation * loudness
    return jnp.minimum(jnp.maximum(result, -bound), bound).astype(held_as)


def bell_draw_with(key, shape, scale, bound, cuts, heavy, kind=jnp.bfloat16):
    values = scale * jax.random.normal(key, shape, jnp.float32)
    if cuts:
        values = values * steps_of(key, shape, cuts, -0.22, 0.18)
    return jnp.clip(strengthened(values, jax.random.fold_in(key, 3), *heavy), -bound, bound).astype(kind)


def setup_inputs(seed: int = 0) -> dict:
    key_list = jax.random.split(jax.random.key(seed), 9)
    tokens = noise(key_list[0], (MB, TOKENS, D), 1.0, 6.0, ((1, 32),))
    doc_starts = draw_doc_starts(jax.random.fold_in(key_list[8], 71), 0)
    w_qkv = noise(key_list[2], (D, 3 * D), D ** -0.5, 0.1875, ((0, 4),))
    w_out = noise(key_list[3], (D, D), D ** -0.5, 0.1875, ((0, 4),))
    w_up = noise(key_list[4], (D, FF), D ** -0.5, 0.1875, ((0, 4),))
    w_down = noise(key_list[5], (FF, D), FF ** -0.5, 0.09375, ((0, 4),))
    gains = jnp.clip(1.0 + 0.18 * jax.random.normal(key_list[6], (D, 4), jnp.float32), 0.099609375, 1.8984375).astype(jnp.bfloat16)
    cotangent = bell_draw_with(key_list[7], (MB, TOKENS, D), 1.0, 6.0, ((1, 32),), (1, 2, 32, 2.75))
    return {"tokens": tokens, "doc_starts": doc_starts, "w_qkv": w_qkv, "w_out": w_out, "w_up": w_up, "w_down": w_down, "gains": gains, "cotangent": cotangent}


@jax.custom_vjp
def low(v):
    return lax.optimization_barrier(v.astype(jnp.bfloat16)).astype(jnp.float32)

@jax.custom_vjp
def low_back(v):
    return v

def low_keep(v):
    return (low(v), None)

def low_pass(kept, grad):
    return (grad,)

def back_keep(v):
    return (v, None)

def back_low(kept, grad):
    return (low(grad),)
low.defvjp(low_keep, low_pass)
low_back.defvjp(back_keep, back_low)
EPSILON = 1e-05
ROPE_BASE = 10000.0
MASKED = -1e+30

def layer_norm(values, gain):
    center = lax.optimization_barrier(jnp.mean(values, axis=-1, keepdims=True))
    shifted = values - center
    spread = lax.optimization_barrier(jnp.mean(shifted * shifted, axis=-1, keepdims=True))
    return shifted * lax.rsqrt(spread + EPSILON) * gain

def rotate(values, offsets):
    half_dim = values.shape[-1] // 2
    freqs = ROPE_BASE ** (-jnp.arange(half_dim, dtype=jnp.float32) / half_dim)
    angles = offsets.astype(jnp.float32)[:, None] * freqs[None, :]
    cosine = jnp.cos(angles)[:, None, :]
    sine = jnp.sin(angles)[:, None, :]
    first_half = values[..., :half_dim]
    second_half = values[..., half_dim:]
    return jnp.concatenate([first_half * cosine - second_half * sine, second_half * cosine + first_half * sine], axis=-1)

def doc_layout(doc_starts, positions):
    begun = doc_starts[None, :] <= positions[:, None]
    segment_ids = lax.optimization_barrier(jnp.sum(begun.astype(jnp.int32), axis=1)) - 1
    latest = lax.optimization_barrier(jnp.max(jnp.where(begun, doc_starts[None, :], 0), axis=1))
    return (segment_ids, positions - latest)

def stream_forward(rows_in, params, positions, segment_ids, offsets):
    w_qkv_f, w_out_f, w_up_f, w_down_f, gain_f = params
    precise = lax.Precision.HIGHEST
    count = rows_in.shape[0]
    normed = low(layer_norm(rows_in, gain_f[:, 0]))
    projected = low_back(jnp.dot(normed, w_qkv_f, precision=precise))
    queries = projected[:, :D].reshape(count, HEADS, HDIM)
    keys = projected[:, D:2 * D].reshape(count, HEADS, HDIM)
    values = projected[:, 2 * D:].reshape(count, HEADS, HDIM)
    queries = low(rotate(queries, offsets) * HDIM ** (-0.5))
    keys = low(rotate(keys, offsets))
    values = low(values)
    block_rows = math.gcd(count, 512)

    def attend(block_index):
        first_row = block_index * block_rows
        query_block = lax.dynamic_slice_in_dim(queries, first_row, block_rows, 0)
        query_pos = lax.dynamic_slice_in_dim(positions, first_row, block_rows, 0)
        query_seg = lax.dynamic_slice_in_dim(segment_ids, first_row, block_rows, 0)
        scores = jnp.einsum('qhd,khd->hqk', query_block, keys, precision=precise)
        allowed = ((query_seg[:, None] == segment_ids[None, :]) & (positions[None, :] <= query_pos[:, None]))[None]
        scores = low_back(scores)
        masked = jnp.where(allowed, scores, MASKED)
        peak = lax.optimization_barrier(jnp.max(masked, axis=-1, keepdims=True))
        weights = jnp.exp(masked - peak)
        weights = low(weights / lax.optimization_barrier(jnp.sum(weights, axis=-1, keepdims=True)))
        return jnp.einsum('hqk,khd->qhd', weights, values, precision=precise)
    attended = lax.map(jax.checkpoint(attend), jnp.arange(count // block_rows, dtype=jnp.int32))
    attended = low_back(low(attended.reshape(count, D)))
    attn_proj = low_back(jnp.dot(attended, w_out_f, precision=precise))
    hidden_state = rows_in + layer_norm(attn_proj, gain_f[:, 1])
    normed_two = low(layer_norm(hidden_state, gain_f[:, 2]))
    up_proj = low_back(jnp.dot(normed_two, w_up_f, precision=precise))
    activated = low(jax.nn.gelu(up_proj, approximate=True))
    down_proj = low_back(jnp.dot(activated, w_down_f, precision=precise))
    return hidden_state + layer_norm(down_proj, gain_f[:, 3])

def reference(tokens, doc_starts, w_qkv, w_out, w_up, w_down, gains, cotangent):
    params = (w_qkv.astype(jnp.float32), w_out.astype(jnp.float32), w_up.astype(jnp.float32), w_down.astype(jnp.float32), gains.astype(jnp.float32))
    streams = tokens.astype(jnp.float32).reshape(MB * N_SHARD, STREAM, D)
    cotangents = cotangent.astype(jnp.float32).reshape(MB * N_SHARD, STREAM, D)
    starts_all = doc_starts.reshape(MB * N_SHARD, DOCS)
    positions = jnp.arange(STREAM, dtype=jnp.int32)

    def per_stream(totals, items):
        stream_rows, stream_cot, stream_starts = items
        segment_ids, offsets = doc_layout(stream_starts, positions)

        def forward(rows_in, w_one, w_two, w_three, w_four, gain_in):
            return stream_forward(rows_in, (w_one, w_two, w_three, w_four, gain_in), positions, segment_ids, offsets)
        outputs, backward = jax.vjp(forward, stream_rows, params[0], params[1], params[2], params[3], params[4])
        grads = backward(stream_cot)
        new_totals = tuple((total + grad for total, grad in zip(totals, grads[1:])))
        return (new_totals, (outputs, grads[0]))
    zero_grads = tuple((jnp.zeros(param.shape, jnp.float32) for param in params))
    totals, (outputs, input_grads) = lax.scan(per_stream, zero_grads, (streams, cotangents, starts_all))
    return (outputs.reshape(MB, TOKENS, D).astype(jnp.bfloat16), input_grads.reshape(MB, TOKENS, D), totals[0], totals[1], totals[2], totals[3], totals[4])
```

```python
import functools
import math

import jax
import jax.numpy as jnp
from jax import lax
from jax.experimental import pallas as pl
from jax.experimental.pallas import tpu as pltpu
from jax.sharding import PartitionSpec as P

HEADS = 16
HDIM = 64
EPSILON = 1e-05
ROPE_BASE = 10000.0
MASKED = -1e30
ALL = ("shard", "ctx")
BF = jnp.bfloat16
F32 = jnp.float32
VMEM_LIMIT = 56 * 1024 * 1024


def layer_norm(values, gain):
    center = jnp.mean(values, axis=-1, keepdims=True)
    shifted = values - center
    spread = jnp.mean(shifted * shifted, axis=-1, keepdims=True)
    return shifted * lax.rsqrt(spread + EPSILON) * gain


def gelu_tanh(values):
    return jax.nn.gelu(values, approximate=True)


def dot(left, right):
    return jnp.dot(left, right, preferred_element_type=F32)


def contract_rows(left, right):
    return lax.dot_general(left, right, (((0,), (0,)), ((), ())), preferred_element_type=F32)


def contract_cols(left, right):
    return lax.dot_general(left, right, (((1,), (1,)), ((), ())), preferred_element_type=F32)


def latest_start(doc_starts, positions):
    begun = doc_starts[:, None, :] <= positions[None, :, None]
    return jnp.max(jnp.where(begun, doc_starts[:, None, :], 0), axis=2)


def rope_tables(doc_starts, positions):
    half = HDIM // 2
    freqs = ROPE_BASE ** (-jnp.arange(half, dtype=F32) / half)
    offsets = positions[None, :] - latest_start(doc_starts, positions)
    angles = offsets.astype(F32)[:, :, None] * freqs
    cosine, sine = jnp.cos(angles), jnp.sin(angles)
    cos_row = jnp.concatenate([cosine] * 4, axis=-1)
    sin_row = jnp.concatenate([-sine, sine, -sine, sine], axis=-1)
    return cos_row, sin_row


def turned(values, cos_row, sin_row):
    width = values.shape[1]
    half = HDIM // 2
    if width == HDIM:
        swapped = jnp.concatenate([values[:, half:], values[:, :half]], axis=1)
    else:
        lane = lax.broadcasted_iota(jnp.int32, values.shape, 1)
        swapped = jnp.where(
            lane % HDIM < half, pltpu.roll(values, width - half, 1), pltpu.roll(values, half, 1)
        )
    return values * cos_row[:, :width] + swapped * sin_row[:, :width]


def qkv_kernel(lanes, u_ref, wq_ref, wk_ref, wv_ref, cos_ref, sin_ref, out_ref):
    groups, _, batch, rows, _ = out_ref.shape
    cos_row, sin_row = cos_ref[...], sin_ref[...]
    u = u_ref[...]
    for slot, w_ref in enumerate((wq_ref, wk_ref, wv_ref)):
        full = dot(u, w_ref[...])
        for g in range(groups):
            part = full[:, g * lanes : (g + 1) * lanes]
            if slot < 2:
                part = turned(part, cos_row, sin_row)
            if slot == 0:
                part = part * HDIM ** (-0.5)
            out_ref[g, slot] = part.reshape(batch, rows, lanes).astype(BF)


def project_qkv(u, w_qkv, cos_row, sin_row, group_count, batch):
    count, width = u.shape
    lanes = width // group_count
    step = max(1, min(group_count, 256 // lanes))
    columns = step * lanes
    blocks = width // columns
    w_spec = lambda part: pl.BlockSpec((width, columns), lambda i: (0, part * blocks + i))
    whole = lambda a: pl.BlockSpec(a.shape, lambda i: (0, 0))
    return pl.pallas_call(
        functools.partial(qkv_kernel, lanes),
        out_shape=jax.ShapeDtypeStruct((group_count, 3, batch, count // batch, lanes), BF),
        grid=(blocks,),
        in_specs=[whole(u), w_spec(0), w_spec(1), w_spec(2), whole(cos_row), whole(sin_row)],
        out_specs=pl.BlockSpec(
            (step, 3, batch, count // batch, lanes), lambda i: (i, 0, 0, 0, 0)
        ),
        compiler_params=pltpu.CompilerParams(vmem_limit_bytes=VMEM_LIMIT),
        name="project_qkv",
    )(u, w_qkv, w_qkv, w_qkv, cos_row, sin_row)


def starts_row(info_ref, mb, docs, positions):
    latest = jnp.zeros_like(positions)
    for d in range(docs):
        start = info_ref[mb, d]
        latest = jnp.where(positions >= start, jnp.maximum(latest, start), latest)
    return latest


def start_scalar(info_ref, mb, docs, position):
    latest = jnp.int32(0)
    for d in range(docs):
        start = info_ref[mb, d]
        latest = jnp.where(position >= start, jnp.maximum(latest, start), latest)
    return latest


def attend_kernel(docs, heads, info_ref, q_ref, k_ref, v_ref, o_ref, ob_ref, lse_ref):
    mb, i = pl.program_id(0), pl.program_id(1)
    per, rows, lanes = q_ref.shape
    block = per * rows
    first = info_ref[mb, docs] + i * block
    low = start_scalar(info_ref, mb, docs, first) // block
    diag = first // block
    q_pos = first + lax.broadcasted_iota(jnp.int32, (1, block), 1)
    q_start = starts_row(info_ref, mb, docs, q_pos)
    q_all = q_ref[...].reshape(block, lanes)
    queries = [q_all[:, h * HDIM : (h + 1) * HDIM] for h in range(heads)]

    def visit(step, state):
        j = diag - step
        k_all = k_ref[pl.ds(j * per, per)].reshape(block, lanes)
        v_flip = v_ref[pl.ds(j * per, per)].reshape(block, lanes).astype(F32).T.astype(BF)
        k_pos = j * block + lax.broadcasted_iota(jnp.int32, (block, 1), 0)
        allowed = (k_pos >= q_start) & (k_pos <= q_pos)
        out = []
        for h in range(heads):
            peak, total, acc = state[h]
            scores = contract_cols(k_all[:, h * HDIM : (h + 1) * HDIM], queries[h])
            scores = jnp.where(allowed, scores, MASKED)
            new_peak = jnp.maximum(peak, jnp.max(scores, axis=0, keepdims=True))
            decay = jnp.exp(peak - new_peak)
            weights = jnp.exp(scores - new_peak)
            total = total * decay + jnp.sum(weights, axis=0, keepdims=True)
            acc = acc * decay + dot(v_flip[h * HDIM : (h + 1) * HDIM], weights.astype(BF))
            out.append((new_peak, total, acc))
        return tuple(out)

    start = tuple(
        (
            jnp.full((1, block), MASKED, F32),
            jnp.zeros((1, block), F32),
            jnp.zeros((HDIM, block), F32),
        )
        for _ in range(heads)
    )
    state = lax.fori_loop(0, diag - low + 1, visit, start)
    flipped = jnp.concatenate([acc / total for _, total, acc in state], axis=0)
    attended = flipped.T
    o_ref[...] = attended.reshape(per, rows, lanes)
    ob_ref[...] = attended.astype(BF).reshape(per, rows, lanes)
    lse_ref[...] = jnp.concatenate([peak + jnp.log(total) for peak, total, _ in state], axis=0)


def attend(info, docs, queries, q_slot, keys, k_slot, v_slot):
    group_count, _, batch, rows, lanes = queries.shape
    blocks_all = keys.shape[0]
    heads = lanes // HDIM
    per = math.gcd(group_count, max(1, 256 // rows))
    q_blocks = group_count // per
    spec = lambda slot: pl.BlockSpec(
        (per, None, None, rows, lanes), lambda b, i, info: (i, slot, b, 0, 0)
    )
    kv_spec = lambda slot: pl.BlockSpec(
        (blocks_all, None, None, rows, lanes), lambda b, i, info: (0, slot, b, 0, 0)
    )
    o_spec = pl.BlockSpec((per, None, rows, lanes), lambda b, i, info: (i, b, 0, 0))
    return pl.pallas_call(
        functools.partial(attend_kernel, docs, heads),
        out_shape=(
            jax.ShapeDtypeStruct((group_count, batch, rows, lanes), F32),
            jax.ShapeDtypeStruct((group_count, batch, rows, lanes), BF),
            jax.ShapeDtypeStruct((batch, heads, group_count * rows), F32),
        ),
        grid_spec=pltpu.PrefetchScalarGridSpec(
            num_scalar_prefetch=1,
            grid=(batch, q_blocks),
            in_specs=[spec(q_slot), kv_spec(k_slot), kv_spec(v_slot)],
            out_specs=(
                o_spec,
                o_spec,
                pl.BlockSpec((None, heads, per * rows), lambda b, i, info: (b, 0, i)),
            ),
        ),
        compiler_params=pltpu.CompilerParams(vmem_limit_bytes=VMEM_LIMIT),
        name="attend",
    )(info, queries, keys, keys)


def attend_back_kernel(
    docs, heads, per, merged, info_ref, q_ref, k_ref, v_ref, do_ref, o_ref, lse_ref, cosq_ref,
    sinq_ref, cosk_ref, sink_ref, *rest
):
    mb, j = pl.program_id(0), pl.program_id(1)
    if merged:
        out_ref, dq_acc, delta_ref = rest
    else:
        dq_ref, out_ref, dq_acc, delta_ref = rest
    group_count, rows, lanes = q_ref.shape
    block = per * rows
    q_blocks = group_count // per
    base = info_ref[mb, docs] // block

    def lanes_of(i):
        return pl.ds(pl.multiple_of(i * block, block), block)

    @pl.when(j == 0)
    def _():
        dq_acc[...] = jnp.zeros_like(dq_acc)

        def fill(i, carry):
            here = pl.ds(i * per, per)
            prod = do_ref[here].reshape(block, lanes).astype(F32) * o_ref[here].reshape(
                block, lanes
            )
            flipped = prod.T
            delta_ref[:, lanes_of(i)] = jnp.concatenate(
                [
                    jnp.sum(flipped[h * HDIM : (h + 1) * HDIM], axis=0, keepdims=True)
                    for h in range(heads)
                ],
                axis=0,
            )
            return carry

        lax.fori_loop(0, q_blocks, fill, 0)

    k_first = j * block
    last = k_first + block - 1
    end = base * block + group_count * rows
    for d in range(docs):
        start = info_ref[mb, d]
        end = jnp.where(start > last, jnp.minimum(end, start), end)
    i_low = jnp.maximum(j - base, 0)
    i_high = jnp.maximum((end - base * block + block - 1) // block, i_low)
    k_pos = k_first + lax.broadcasted_iota(jnp.int32, (block, 1), 0)
    k_all = k_ref[...].reshape(block, lanes)
    v_all = v_ref[...].reshape(block, lanes)
    k_flip = k_all.astype(F32).T.astype(BF)
    heads_of = lambda a: [a[:, h * HDIM : (h + 1) * HDIM] for h in range(heads)]
    k_heads, v_heads = heads_of(k_all), heads_of(v_all)

    def visit(i, state):
        here = pl.ds(i * per, per)
        q_heads = heads_of(q_ref[here].reshape(block, lanes))
        do_heads = heads_of(do_ref[here].reshape(block, lanes))
        q_pos = (base + i) * block + lax.broadcasted_iota(jnp.int32, (1, block), 1)
        q_start = starts_row(info_ref, mb, docs, q_pos)
        allowed = (k_pos >= q_start) & (k_pos <= q_pos)
        lse = lse_ref[:, lanes_of(i)]
        delta = delta_ref[:, lanes_of(i)]
        out = []
        for h in range(heads):
            dk, dv = state[h]
            scores = contract_cols(k_heads[h], q_heads[h])
            weights = jnp.exp(jnp.where(allowed, scores - lse[h : h + 1], MASKED))
            grad_weights = contract_cols(v_heads[h], do_heads[h])
            grad_scores = (weights * (grad_weights - delta[h : h + 1])).astype(BF)
            dv = dv + dot(weights.astype(BF), do_heads[h])
            dk = dk + dot(grad_scores, q_heads[h])
            at = slice(h * HDIM, (h + 1) * HDIM)
            dq_acc[at, lanes_of(i)] += dot(k_flip[at], grad_scores)
            out.append((dk, dv))
        return tuple(out)

    zero = jnp.zeros((block, HDIM), F32)
    state = lax.fori_loop(i_low, i_high, visit, tuple((zero, zero) for _ in range(heads)))
    dk = jnp.concatenate([dk for dk, _ in state], axis=1) if heads > 1 else state[0][0]
    dv = jnp.concatenate([dv for _, dv in state], axis=1) if heads > 1 else state[0][1]
    dk = turned(dk, cosk_ref[...], -sink_ref[...])
    there = pl.ds(j * per, per)
    k_slot = 1 if merged else 0
    out_ref[there, k_slot] = dk.reshape(per, rows, lanes).astype(out_ref.dtype)
    out_ref[there, k_slot + 1] = dv.reshape(per, rows, lanes).astype(out_ref.dtype)

    @pl.when(j == pl.num_programs(1) - 1)
    def _():
        def finish(i, carry):
            dq = dq_acc[:, lanes_of(i)].T
            at = pl.ds(pl.multiple_of(i * block, block), block)
            dq = turned(dq, cosq_ref[at, :], -sinq_ref[at, :]) * HDIM ** (-0.5)
            dq = dq.reshape(per, rows, lanes).astype(BF)
            if merged:
                out_ref[pl.ds(i * per, per), 0] = dq
            else:
                dq_ref[pl.ds(i * per, per)] = dq
            return carry

        lax.fori_loop(0, q_blocks, finish, 0)


def attend_back(info, docs, queries, q_slot, keys, k_slot, v_slot, grad, attended, lse, cos_all,
                sin_all, cos_here, sin_here):
    group_count, _, batch, rows, lanes = queries.shape
    blocks_all = keys.shape[0]
    merged = blocks_all == group_count
    heads = lanes // HDIM
    per = math.gcd(group_count, max(1, 256 // rows))
    k_blocks = blocks_all // per
    full = lambda slot: pl.BlockSpec(
        (group_count, None, None, rows, lanes), lambda b, j, info: (0, slot, b, 0, 0)
    )
    part = lambda slot: pl.BlockSpec(
        (per, None, None, rows, lanes), lambda b, j, info: (j, slot, b, 0, 0)
    )
    rows_full = pl.BlockSpec((group_count, None, rows, lanes), lambda b, j, info: (0, b, 0, 0))
    length = group_count * rows
    table_q = pl.BlockSpec((None, length, 2 * HDIM), lambda b, j, info: (b, 0, 0))
    table_k = pl.BlockSpec((None, per * rows, 2 * HDIM), lambda b, j, info: (b, j, 0))
    if merged:
        out_shape = [jax.ShapeDtypeStruct((group_count, 3, batch, rows, lanes), BF)]
        out_specs = [
            pl.BlockSpec((group_count, 3, None, rows, lanes), lambda b, j, info: (0, 0, b, 0, 0))
        ]
    else:
        out_shape = [
            jax.ShapeDtypeStruct((group_count, batch, rows, lanes), BF),
            jax.ShapeDtypeStruct((blocks_all, 2, batch, rows, lanes), F32),
        ]
        out_specs = [
            rows_full,
            pl.BlockSpec((blocks_all, 2, None, rows, lanes), lambda b, j, info: (0, 0, b, 0, 0)),
        ]
    return pl.pallas_call(
        functools.partial(attend_back_kernel, docs, heads, per, merged),
        out_shape=out_shape,
        grid_spec=pltpu.PrefetchScalarGridSpec(
            num_scalar_prefetch=1,
            grid=(batch, k_blocks),
            in_specs=[
                full(q_slot), part(k_slot), part(v_slot), rows_full, rows_full,
                pl.BlockSpec((None, heads, length), lambda b, j, info: (b, 0, 0)),
                table_q, table_q, table_k, table_k,
            ],
            out_specs=out_specs,
            scratch_shapes=[pltpu.VMEM((lanes, length), F32), pltpu.VMEM((heads, length), F32)],
        ),
        compiler_params=pltpu.CompilerParams(vmem_limit_bytes=VMEM_LIMIT),
        name="attend_back",
    )(info, queries, keys, keys, grad, attended, lse, cos_here, sin_here, cos_all, sin_all)


def gathered(weight):
    pieces = lax.axis_size("ctx")
    size = weight.shape[0] // pieces
    piece = lax.dynamic_slice_in_dim(weight, lax.axis_index("ctx") * size, size, 0)
    return lax.all_gather(piece, ALL, axis=0, tiled=True)


def scattered(total):
    return lax.psum_scatter(total.astype(BF), ALL, scatter_dimension=0, tiled=True).astype(F32)


def swapped(values, groups):
    return lax.all_to_all(
        values, "ctx", split_axis=0, concat_axis=0, tiled=True, axis_index_groups=groups
    )


def per_device(tokens, doc_starts, w_qkv, w_out, w_up, w_down, gains, cotangent):
    ctx_size = lax.axis_size("ctx")
    place = lax.axis_index("ctx")
    batch, rows, width = tokens.shape
    count = batch * rows
    docs = doc_starts.shape[2]
    group_count = math.gcd(HEADS, ctx_size)
    runs = ctx_size // group_count
    if runs == 1:
        near = far = None
    else:
        near = [[r * group_count + g for g in range(group_count)] for r in range(runs)]
        far = [[r * group_count + g for r in range(runs)] for g in range(group_count)]
    lanes = width // group_count

    full_qkv = gathered(w_qkv)
    full_out = gathered(w_out)
    full_up = gathered(w_up)
    full_down = gathered(w_down)
    gain_all = lax.all_gather(gains, "shard", axis=0, tiled=True).astype(F32)

    starts = doc_starts[:, 0, :]
    here = place * rows + jnp.arange(rows, dtype=jnp.int32)
    cos_row, sin_row = (t.reshape(count, 2 * HDIM) for t in rope_tables(starts, here))
    stream = jnp.arange(ctx_size * rows, dtype=jnp.int32)
    cos_all, sin_all = rope_tables(starts, stream)
    run_first = (place // group_count) * group_count * rows
    run_length = group_count * rows
    cos_here, sin_here = (
        lax.dynamic_slice_in_dim(t, run_first, run_length, 1) for t in (cos_all, sin_all)
    )
    info = jnp.concatenate(
        [starts, jnp.broadcast_to(run_first, (batch, 1)).astype(jnp.int32)], axis=1
    )

    x = tokens.reshape(count, width).astype(F32)
    out_grad = cotangent.reshape(count, width).astype(F32)
    normed, norm_one_back = jax.vjp(layer_norm, x, gain_all[:, 0])
    u = normed.astype(BF)
    qkv = swapped(project_qkv(u, full_qkv, cos_row, sin_row, group_count, batch), near)
    if runs == 1:
        keys, k_slot = qkv, 1
    else:
        keys, k_slot = (
            lax.all_gather(qkv[:, 1:], "ctx", axis=0, tiled=True, axis_index_groups=far),
            0,
        )
    attended, attended_low, lse = attend(info, docs, qkv, 0, keys, k_slot, k_slot + 1)
    ob = swapped(attended_low, near).transpose(1, 2, 0, 3).reshape(count, width)
    attn_proj = dot(ob, full_out)
    attn_branch, norm_two_back = jax.vjp(layer_norm, attn_proj, gain_all[:, 1])
    hidden = x + attn_branch
    normed_two, norm_three_back = jax.vjp(layer_norm, hidden, gain_all[:, 2])
    u2 = normed_two.astype(BF)
    up_proj = dot(u2, full_up)
    activated, gelu_back = jax.vjp(gelu_tanh, up_proj)
    g = activated.astype(BF)
    down_proj = dot(g, full_down)
    mlp_branch, norm_four_back = jax.vjp(layer_norm, down_proj, gain_all[:, 3])
    layer_out = (hidden + mlp_branch).astype(BF)

    down_grad, gain_four = norm_four_back(out_grad)
    dmb = down_grad.astype(BF)
    grad_down = scattered(contract_rows(g, dmb))
    (up_grad,) = gelu_back(contract_cols(dmb, full_down))
    dfb = up_grad.astype(BF)
    grad_up = scattered(contract_rows(u2, dfb))
    hidden_add, gain_three = norm_three_back(contract_cols(dfb, full_up))
    dh = out_grad + hidden_add
    attn_grad, gain_two = norm_two_back(dh)
    dab = attn_grad.astype(BF)
    grad_out = scattered(contract_rows(ob, dab))
    dob = contract_cols(dab, full_out).astype(BF)
    dob = swapped(dob.reshape(batch, rows, group_count, lanes).transpose(2, 0, 1, 3), near)
    back = attend_back(
        info, docs, qkv, 0, keys, k_slot, k_slot + 1, dob, attended, lse, cos_all, sin_all,
        cos_here, sin_here,
    )
    if runs == 1:
        grads = back[0]
    else:
        dkv = lax.psum_scatter(
            back[1], "ctx", scatter_dimension=0, tiled=True, axis_index_groups=far
        )
        grads = jnp.concatenate([back[0][:, None], dkv.astype(BF)], axis=1)
    dqkv = swapped(grads, near).transpose(2, 3, 1, 0, 4).reshape(count, 3 * width)
    grad_qkv = scattered(contract_rows(u, dqkv))
    input_add, gain_one = norm_one_back(contract_cols(dqkv, full_qkv))
    grad_tokens = dh + input_add
    grad_gains = lax.psum_scatter(
        jnp.stack([gain_one, gain_two, gain_three, gain_four], axis=1),
        ALL,
        scatter_dimension=0,
        tiled=True,
    )
    return (
        layer_out.reshape(batch, rows, width),
        grad_tokens.reshape(batch, rows, width),
        grad_qkv,
        grad_out,
        grad_up,
        grad_down,
        grad_gains,
    )


def solution(mesh):
    return jax.shard_map(
        per_device,
        mesh=mesh,
        in_specs=(
            P(None, ALL, None),
            P(None, "shard", None),
            P("shard", None),
            P("shard", None),
            P("shard", None),
            P("shard", None),
            P("shard", None),
            P(None, ALL, None),
        ),
        out_specs=(
            P(None, ALL, None),
            P(None, ALL, None),
            P(ALL, None),
            P(ALL, None),
            P(ALL, None),
            P(ALL, None),
            P(ALL, None),
        ),
        check_vma=False,
    )
```

```python
import functools
import math

import jax
import jax.numpy as jnp
from jax import lax
from jax.experimental import pallas as pl
from jax.experimental.pallas import tpu as pltpu
from jax.sharding import PartitionSpec as P

HEADS = 16
HDIM = 64
EPSILON = 1e-05
ROPE_BASE = 10000.0
MASKED = -1e30
ALL = ("shard", "ctx")
BF = jnp.bfloat16
F32 = jnp.float32
VMEM_LIMIT = 56 * 1024 * 1024


def layer_norm(values, gain):
    center = jnp.mean(values, axis=-1, keepdims=True)
    shifted = values - center
    spread = jnp.mean(shifted * shifted, axis=-1, keepdims=True)
    return shifted * lax.rsqrt(spread + EPSILON) * gain


def gelu_tanh(values):
    return jax.nn.gelu(values, approximate=True)


def dot(left, right):
    return jnp.dot(left, right, preferred_element_type=F32)


def contract_rows(left, right):
    return lax.dot_general(left, right, (((0,), (0,)), ((), ())), preferred_element_type=F32)


def contract_cols(left, right):
    return lax.dot_general(left, right, (((1,), (1,)), ((), ())), preferred_element_type=F32)


def latest_start(doc_starts, positions):
    begun = doc_starts[:, None, :] <= positions[None, :, None]
    return jnp.max(jnp.where(begun, doc_starts[:, None, :], 0), axis=2)


def rope_tables(doc_starts, positions):
    half = HDIM // 2
    freqs = ROPE_BASE ** (-jnp.arange(half, dtype=F32) / half)
    offsets = positions[None, :] - latest_start(doc_starts, positions)
    angles = offsets.astype(F32)[:, :, None] * freqs
    cosine, sine = jnp.cos(angles), jnp.sin(angles)
    cos_row = jnp.concatenate([cosine] * 4, axis=-1)
    sin_row = jnp.concatenate([-sine, sine, -sine, sine], axis=-1)
    return cos_row, sin_row


def turned(values, cos_row, sin_row):
    width = values.shape[1]
    half = HDIM // 2
    if width == HDIM:
        swapped = jnp.concatenate([values[:, half:], values[:, :half]], axis=1)
    else:
        lane = lax.broadcasted_iota(jnp.int32, values.shape, 1)
        swapped = jnp.where(
            lane % HDIM < half, pltpu.roll(values, width - half, 1), pltpu.roll(values, half, 1)
        )
    return values * cos_row[:, :width] + swapped * sin_row[:, :width]


def qkv_kernel(lanes, u_ref, wq_ref, wk_ref, wv_ref, cos_ref, sin_ref, out_ref):
    groups, _, batch, rows, _ = out_ref.shape
    cos_row, sin_row = cos_ref[...], sin_ref[...]
    u = u_ref[...]
    for slot, w_ref in enumerate((wq_ref, wk_ref, wv_ref)):
        full = dot(u, w_ref[...])
        for g in range(groups):
            part = full[:, g * lanes : (g + 1) * lanes]
            if slot < 2:
                part = turned(part, cos_row, sin_row)
            if slot == 0:
                part = part * HDIM ** (-0.5)
            out_ref[g, slot] = part.reshape(batch, rows, lanes).astype(BF)


def project_qkv(u, w_qkv, cos_row, sin_row, group_count, batch):
    count, width = u.shape
    lanes = width // group_count
    step = max(1, min(group_count, 256 // lanes))
    columns = step * lanes
    blocks = width // columns
    w_spec = lambda part: pl.BlockSpec((width, columns), lambda i: (0, part * blocks + i))
    whole = lambda a: pl.BlockSpec(a.shape, lambda i: (0, 0))
    return pl.pallas_call(
        functools.partial(qkv_kernel, lanes),
        out_shape=jax.ShapeDtypeStruct((group_count, 3, batch, count // batch, lanes), BF),
        grid=(blocks,),
        in_specs=[whole(u), w_spec(0), w_spec(1), w_spec(2), whole(cos_row), whole(sin_row)],
        out_specs=pl.BlockSpec(
            (step, 3, batch, count // batch, lanes), lambda i: (i, 0, 0, 0, 0)
        ),
        compiler_params=pltpu.CompilerParams(vmem_limit_bytes=VMEM_LIMIT),
        name="project_qkv",
    )(u, w_qkv, w_qkv, w_qkv, cos_row, sin_row)


def starts_row(info_ref, mb, docs, positions):
    latest = jnp.zeros_like(positions)
    for d in range(docs):
        start = info_ref[mb, d]
        latest = jnp.where(positions >= start, jnp.maximum(latest, start), latest)
    return latest


def start_scalar(info_ref, mb, docs, position):
    latest = jnp.int32(0)
    for d in range(docs):
        start = info_ref[mb, d]
        latest = jnp.where(position >= start, jnp.maximum(latest, start), latest)
    return latest


def attend_kernel(docs, heads, info_ref, q_ref, k_ref, v_ref, o_ref, ob_ref, lse_ref):
    mb, i = pl.program_id(0), pl.program_id(1)
    per, rows, lanes = q_ref.shape
    block = per * rows
    first = info_ref[mb, docs] + i * block
    low = start_scalar(info_ref, mb, docs, first) // block
    diag = first // block
    q_pos = first + lax.broadcasted_iota(jnp.int32, (1, block), 1)
    q_start = starts_row(info_ref, mb, docs, q_pos)
    q_all = q_ref[...].reshape(block, lanes)
    queries = [q_all[:, h * HDIM : (h + 1) * HDIM] for h in range(heads)]

    def visit(step, state):
        j = diag - step
        k_all = k_ref[pl.ds(j * per, per)].reshape(block, lanes)
        v_flip = v_ref[pl.ds(j * per, per)].reshape(block, lanes).astype(F32).T.astype(BF)
        k_pos = j * block + lax.broadcasted_iota(jnp.int32, (block, 1), 0)
        allowed = (k_pos >= q_start) & (k_pos <= q_pos)
        out = []
        for h in range(heads):
            peak, total, acc = state[h]
            scores = contract_cols(k_all[:, h * HDIM : (h + 1) * HDIM], queries[h])
            scores = jnp.where(allowed, scores, MASKED)
            new_peak = jnp.maximum(peak, jnp.max(scores, axis=0, keepdims=True))
            decay = jnp.exp(peak - new_peak)
            weights = jnp.exp(scores - new_peak)
            total = total * decay + jnp.sum(weights, axis=0, keepdims=True)
            acc = acc * decay + dot(v_flip[h * HDIM : (h + 1) * HDIM], weights.astype(BF))
            out.append((new_peak, total, acc))
        return tuple(out)

    start = tuple(
        (
            jnp.full((1, block), MASKED, F32),
            jnp.zeros((1, block), F32),
            jnp.zeros((HDIM, block), F32),
        )
        for _ in range(heads)
    )
    state = lax.fori_loop(0, diag - low + 1, visit, start)
    flipped = jnp.concatenate([acc / total for _, total, acc in state], axis=0)
    attended = flipped.T
    o_ref[...] = attended.reshape(per, rows, lanes)
    ob_ref[...] = attended.astype(BF).reshape(per, rows, lanes)
    lse_ref[...] = jnp.concatenate([peak + jnp.log(total) for peak, total, _ in state], axis=0)


def attend(info, docs, queries, q_slot, keys, k_slot, v_slot):
    group_count, _, batch, rows, lanes = queries.shape
    blocks_all = keys.shape[0]
    heads = lanes // HDIM
    per = math.gcd(group_count, max(1, 256 // rows))
    q_blocks = group_count // per
    spec = lambda slot: pl.BlockSpec(
        (per, None, None, rows, lanes), lambda b, i, info: (i, slot, b, 0, 0)
    )
    kv_spec = lambda slot: pl.BlockSpec(
        (blocks_all, None, None, rows, lanes), lambda b, i, info: (0, slot, b, 0, 0)
    )
    o_spec = pl.BlockSpec((per, None, rows, lanes), lambda b, i, info: (i, b, 0, 0))
    return pl.pallas_call(
        functools.partial(attend_kernel, docs, heads),
        out_shape=(
            jax.ShapeDtypeStruct((group_count, batch, rows, lanes), F32),
            jax.ShapeDtypeStruct((group_count, batch, rows, lanes), BF),
            jax.ShapeDtypeStruct((batch, heads, group_count * rows), F32),
        ),
        grid_spec=pltpu.PrefetchScalarGridSpec(
            num_scalar_prefetch=1,
            grid=(batch, q_blocks),
            in_specs=[spec(q_slot), kv_spec(k_slot), kv_spec(v_slot)],
            out_specs=(
                o_spec,
                o_spec,
                pl.BlockSpec((None, heads, per * rows), lambda b, i, info: (b, 0, i)),
            ),
        ),
        compiler_params=pltpu.CompilerParams(vmem_limit_bytes=VMEM_LIMIT),
        name="attend",
    )(info, queries, keys, keys)


def attend_back_kernel(
    docs, heads, per, merged, info_ref, q_ref, k_ref, v_ref, do_ref, o_ref, lse_ref, cosq_ref,
    sinq_ref, cosk_ref, sink_ref, *rest
):
    mb, j = pl.program_id(0), pl.program_id(1)
    if merged:
        out_ref, dq_acc, delta_ref = rest
    else:
        dq_ref, out_ref, dq_acc, delta_ref = rest
    group_count, rows, lanes = q_ref.shape
    block = per * rows
    q_blocks = group_count // per
    base = info_ref[mb, docs] // block

    def lanes_of(i):
        return pl.ds(pl.multiple_of(i * block, block), block)

    @pl.when(j == 0)
    def _():
        dq_acc[...] = jnp.zeros_like(dq_acc)

        def fill(i, carry):
            here = pl.ds(i * per, per)
            prod = do_ref[here].reshape(block, lanes).astype(F32) * o_ref[here].reshape(
                block, lanes
            )
            flipped = prod.T
            delta_ref[:, lanes_of(i)] = jnp.concatenate(
                [
                    jnp.sum(flipped[h * HDIM : (h + 1) * HDIM], axis=0, keepdims=True)
                    for h in range(heads)
                ],
                axis=0,
            )
            return carry

        lax.fori_loop(0, q_blocks, fill, 0)

    k_first = j * block
    last = k_first + block - 1
    end = base * block + group_count * rows
    for d in range(docs):
        start = info_ref[mb, d]
        end = jnp.where(start > last, jnp.minimum(end, start), end)
    i_low = jnp.maximum(j - base, 0)
    i_high = jnp.maximum((end - base * block + block - 1) // block, i_low)
    k_pos = k_first + lax.broadcasted_iota(jnp.int32, (block, 1), 0)
    k_all = k_ref[...].reshape(block, lanes)
    v_all = v_ref[...].reshape(block, lanes)
    k_flip = k_all.astype(F32).T.astype(BF)
    heads_of = lambda a: [a[:, h * HDIM : (h + 1) * HDIM] for h in range(heads)]
    k_heads, v_heads = heads_of(k_all), heads_of(v_all)

    def visit(i, state):
        here = pl.ds(i * per, per)
        q_heads = heads_of(q_ref[here].reshape(block, lanes))
        do_heads = heads_of(do_ref[here].reshape(block, lanes))
        q_pos = (base + i) * block + lax.broadcasted_iota(jnp.int32, (1, block), 1)
        q_start = starts_row(info_ref, mb, docs, q_pos)
        allowed = (k_pos >= q_start) & (k_pos <= q_pos)
        lse = lse_ref[:, lanes_of(i)]
        delta = delta_ref[:, lanes_of(i)]
        out = []
        for h in range(heads):
            dk, dv = state[h]
            scores = contract_cols(k_heads[h], q_heads[h])
            weights = jnp.exp(jnp.where(allowed, scores - lse[h : h + 1], MASKED))
            grad_weights = contract_cols(v_heads[h], do_heads[h])
            grad_scores = (weights * (grad_weights - delta[h : h + 1])).astype(BF)
            dv = dv + dot(weights.astype(BF), do_heads[h])
            dk = dk + dot(grad_scores, q_heads[h])
            at = slice(h * HDIM, (h + 1) * HDIM)
            dq_acc[at, lanes_of(i)] += dot(k_flip[at], grad_scores)
            out.append((dk, dv))
        return tuple(out)

    zero = jnp.zeros((block, HDIM), F32)
    state = lax.fori_loop(i_low, i_high, visit, tuple((zero, zero) for _ in range(heads)))
    dk = jnp.concatenate([dk for dk, _ in state], axis=1) if heads > 1 else state[0][0]
    dv = jnp.concatenate([dv for _, dv in state], axis=1) if heads > 1 else state[0][1]
    dk = turned(dk, cosk_ref[...], -sink_ref[...])
    there = pl.ds(j * per, per)
    k_slot = 1 if merged else 0
    out_ref[there, k_slot] = dk.reshape(per, rows, lanes).astype(out_ref.dtype)
    out_ref[there, k_slot + 1] = dv.reshape(per, rows, lanes).astype(out_ref.dtype)

    @pl.when(j == pl.num_programs(1) - 1)
    def _():
        def finish(i, carry):
            dq = dq_acc[:, lanes_of(i)].T
            at = pl.ds(pl.multiple_of(i * block, block), block)
            dq = turned(dq, cosq_ref[at, :], -sinq_ref[at, :]) * HDIM ** (-0.5)
            dq = dq.reshape(per, rows, lanes).astype(BF)
            if merged:
                out_ref[pl.ds(i * per, per), 0] = dq
            else:
                dq_ref[pl.ds(i * per, per)] = dq
            return carry

        lax.fori_loop(0, q_blocks, finish, 0)


def attend_back(info, docs, queries, q_slot, keys, k_slot, v_slot, grad, attended, lse, cos_all,
                sin_all, cos_here, sin_here):
    group_count, _, batch, rows, lanes = queries.shape
    blocks_all = keys.shape[0]
    merged = blocks_all == group_count
    heads = lanes // HDIM
    per = math.gcd(group_count, max(1, 256 // rows))
    k_blocks = blocks_all // per
    full = lambda slot: pl.BlockSpec(
        (group_count, None, None, rows, lanes), lambda b, j, info: (0, slot, b, 0, 0)
    )
    part = lambda slot: pl.BlockSpec(
        (per, None, None, rows, lanes), lambda b, j, info: (j, slot, b, 0, 0)
    )
    rows_full = pl.BlockSpec((group_count, None, rows, lanes), lambda b, j, info: (0, b, 0, 0))
    length = group_count * rows
    table_q = pl.BlockSpec((None, length, 2 * HDIM), lambda b, j, info: (b, 0, 0))
    table_k = pl.BlockSpec((None, per * rows, 2 * HDIM), lambda b, j, info: (b, j, 0))
    if merged:
        out_shape = [jax.ShapeDtypeStruct((group_count, 3, batch, rows, lanes), BF)]
        out_specs = [
            pl.BlockSpec((group_count, 3, None, rows, lanes), lambda b, j, info: (0, 0, b, 0, 0))
        ]
    else:
        out_shape = [
            jax.ShapeDtypeStruct((group_count, batch, rows, lanes), BF),
            jax.ShapeDtypeStruct((blocks_all, 2, batch, rows, lanes), F32),
        ]
        out_specs = [
            rows_full,
            pl.BlockSpec((blocks_all, 2, None, rows, lanes), lambda b, j, info: (0, 0, b, 0, 0)),
        ]
    return pl.pallas_call(
        functools.partial(attend_back_kernel, docs, heads, per, merged),
        out_shape=out_shape,
        grid_spec=pltpu.PrefetchScalarGridSpec(
            num_scalar_prefetch=1,
            grid=(batch, k_blocks),
            in_specs=[
                full(q_slot), part(k_slot), part(v_slot), rows_full, rows_full,
                pl.BlockSpec((None, heads, length), lambda b, j, info: (b, 0, 0)),
                table_q, table_q, table_k, table_k,
            ],
            out_specs=out_specs,
            scratch_shapes=[pltpu.VMEM((lanes, length), F32), pltpu.VMEM((heads, length), F32)],
        ),
        compiler_params=pltpu.CompilerParams(vmem_limit_bytes=VMEM_LIMIT),
        name="attend_back",
    )(info, queries, keys, keys, grad, attended, lse, cos_here, sin_here, cos_all, sin_all)


def flips(mask):
    count = lax.axis_size("shard") * lax.axis_size("ctx")
    return [(i, i ^ mask) for i in range(count)]


def turns(by):
    shards, places = lax.axis_size("shard"), lax.axis_size("ctx")
    return [
        (a * places + b, ((a + by) % shards) * places + b)
        for a in range(shards)
        for b in range(places)
    ]


def sent(values, pairs):
    return lax.ppermute(values, ALL, pairs)


def picked(values, index, axis):
    return lax.dynamic_index_in_dim(values, index, axis, keepdims=False)


def cube():
    return lax.axis_size("ctx") == 8


def bits():
    place = lax.axis_index("ctx")
    return lax.axis_index("shard"), place // 4, place // 2 % 2, place % 2


def put_kernel(shards, where, own_ref, a0, a1, b0, b1, out_ref, sem):
    z, y, x, c = (where[i] for i in range(4))
    half = a0.shape[-1]
    copies = [pltpu.make_async_copy(own_ref, out_ref.at[z], sem.at[0])]
    for side, (a, b) in enumerate(((a0, b0), (a1, b1))):
        for p in range(2):
            for q in range(2):
                for k in range(1, shards):
                    source = lax.rem(z - k + shards, shards)
                    core = c ^ side
                    at_a = ((y ^ p) * 2 + (x ^ q)) * 2 + core
                    at_b = ((y ^ q) * 2 + (x ^ p)) * 2 + core
                    for part, at, first in ((a, at_a, 0), (b, at_b, half)):
                        copies.append(
                            pltpu.make_async_copy(
                                part.at[p, q, k - 1],
                                out_ref.at[source, at, :, pl.ds(first, half)],
                                sem.at[len(copies)],
                            )
                        )
    for copy in copies:
        copy.start()
    for copy in copies:
        copy.wait()


def put_together(own, parts):
    shards = lax.axis_size("shard")
    pieces, rows, columns = own.shape
    anywhere = pl.BlockSpec(memory_space=pl.ANY)
    full = (shards, pieces, rows, columns)
    return pl.pallas_call(
        functools.partial(put_kernel, shards),
        out_shape=jax.ShapeDtypeStruct(full, BF),
        grid_spec=pltpu.PrefetchScalarGridSpec(
            num_scalar_prefetch=1,
            grid=(1,),
            in_specs=[anywhere] * 5,
            out_specs=pl.BlockSpec(full, lambda i, where: (0, 0, 0, 0)),
            scratch_shapes=[pltpu.SemaphoreType.DMA((1 + 16 * (shards - 1),))],
        ),
        compiler_params=pltpu.CompilerParams(vmem_limit_bytes=VMEM_LIMIT),
        name="put_together",
    )(jnp.stack(bits()).astype(jnp.int32), own, *parts)


def gathered(weight, after):
    pieces = lax.axis_size("ctx")
    rows, columns = weight.shape
    size = rows // pieces
    own = weight.reshape(pieces, size, columns)
    piece = picked(own, lax.axis_index("ctx"), 0)
    if not cube():
        return lax.all_gather(piece, ALL, axis=0, tiled=True), after
    shards = lax.axis_size("shard")
    if after is not None:
        piece, _ = lax.optimization_barrier((piece, after))
    far = jnp.stack([sent(piece, turns(k)) for k in range(1, shards)])
    a, b = far[:, :, : columns // 2], far[:, :, columns // 2 :]
    a = jnp.stack([a, sent(a, flips(2))])
    b = jnp.stack([b, sent(b, flips(4))])
    a = jnp.stack([a, sent(a, flips(4))])
    b = jnp.stack([b, sent(b, flips(2))])
    full = put_together(own, (a, sent(a, flips(1)), b, sent(b, flips(1))))
    return full.reshape(shards * rows, columns), far


def gathered_gains(gains):
    if not cube():
        return lax.all_gather(gains, "shard", axis=0, tiled=True).T
    shards = lax.axis_size("shard")
    flat = gains.T
    parts = [flat] + [sent(flat, turns(-k)) for k in range(1, shards)]
    ring = jnp.stack(parts + parts)
    start = lax.rem(shards - lax.axis_index("shard"), shards)
    ring = lax.dynamic_slice_in_dim(ring, start, shards, 0)
    return ring.transpose(1, 0, 2).reshape(flat.shape[0], -1)


def summed(left, right):
    return (left.astype(F32) + right.astype(F32)).astype(BF)


def scattered(left, right):
    if not cube():
        total = contract_rows(left, right).astype(BF)
        return lax.psum_scatter(total, ALL, scatter_dimension=0, tiled=True).astype(F32)
    shards = lax.axis_size("shard")
    z, y, x, c = bits()
    tokens, rows = left.shape
    columns = right.shape[1]
    size = rows // (8 * shards)
    flat = left.T.reshape(shards * 4, 2, size, tokens)
    half = lambda core: dot(picked(flat, core, 1).reshape(rows // 2, tokens), right).astype(BF)
    away = sent(half(1 - c), flips(1))
    total = summed(half(c), away).reshape(shards, 2, 2, size, columns)
    a, b = total[..., : columns // 2], total[..., columns // 2 :]
    a_in = sent(picked(a, 1 - y, 1), flips(4))
    b_in = sent(picked(b, 1 - x, 2), flips(2))
    a = summed(picked(a, y, 1), a_in)
    b = summed(picked(b, x, 2), b_in)
    a_in = sent(picked(a, 1 - x, 1), flips(2))
    b_in = sent(picked(b, 1 - y, 1), flips(4))
    a = summed(picked(a, x, 1), a_in)
    b = summed(picked(b, y, 1), b_in)
    total = jnp.concatenate([a, b], axis=-1)
    kept = picked(total, z, 0).astype(F32)
    for k in range(1, shards):
        part = picked(total, lax.rem(z + k, shards), 0)
        kept = kept + sent(part, turns(k)).astype(F32)
    return kept


def scattered_gains(grads):
    count = lax.axis_size("shard") * lax.axis_size("ctx")
    kinds = grads.shape[0]
    parts = grads.reshape(kinds, count, -1).transpose(1, 0, 2)
    parts = lax.all_to_all(parts, ALL, split_axis=0, concat_axis=0, tiled=True)
    return jnp.sum(parts, axis=0).T


def swapped(values, groups):
    return lax.all_to_all(
        values, "ctx", split_axis=0, concat_axis=0, tiled=True, axis_index_groups=groups
    )


def per_device(tokens, doc_starts, w_qkv, w_out, w_up, w_down, gains, cotangent):
    ctx_size = lax.axis_size("ctx")
    place = lax.axis_index("ctx")
    batch, rows, width = tokens.shape
    count = batch * rows
    docs = doc_starts.shape[2]
    group_count = math.gcd(HEADS, ctx_size)
    runs = ctx_size // group_count
    if runs == 1:
        near = far = None
    else:
        near = [[r * group_count + g for g in range(group_count)] for r in range(runs)]
        far = [[r * group_count + g for r in range(runs)] for g in range(group_count)]
    lanes = width // group_count

    gain_all = gathered_gains(gains).astype(F32)
    full_qkv, order = gathered(w_qkv, None)
    full_out, order = gathered(w_out, order)
    full_up, order = gathered(w_up, order)
    full_down, order = gathered(w_down, order)

    starts = doc_starts[:, 0, :]
    here = place * rows + jnp.arange(rows, dtype=jnp.int32)
    cos_row, sin_row = (t.reshape(count, 2 * HDIM) for t in rope_tables(starts, here))
    stream = jnp.arange(ctx_size * rows, dtype=jnp.int32)
    cos_all, sin_all = rope_tables(starts, stream)
    run_first = (place // group_count) * group_count * rows
    run_length = group_count * rows
    cos_here, sin_here = (
        lax.dynamic_slice_in_dim(t, run_first, run_length, 1) for t in (cos_all, sin_all)
    )
    info = jnp.concatenate(
        [starts, jnp.broadcast_to(run_first, (batch, 1)).astype(jnp.int32)], axis=1
    )

    x = tokens.reshape(count, width).astype(F32)
    out_grad = cotangent.reshape(count, width).astype(F32)
    normed, norm_one_back = jax.vjp(layer_norm, x, gain_all[0])
    u = normed.astype(BF)
    qkv = swapped(project_qkv(u, full_qkv, cos_row, sin_row, group_count, batch), near)
    if runs == 1:
        keys, k_slot = qkv, 1
    else:
        keys, k_slot = (
            lax.all_gather(qkv[:, 1:], "ctx", axis=0, tiled=True, axis_index_groups=far),
            0,
        )
    attended, attended_low, lse = attend(info, docs, qkv, 0, keys, k_slot, k_slot + 1)
    ob = swapped(attended_low, near).transpose(1, 2, 0, 3).reshape(count, width)
    attn_proj = dot(ob, full_out)
    attn_branch, norm_two_back = jax.vjp(layer_norm, attn_proj, gain_all[1])
    hidden = x + attn_branch
    normed_two, norm_three_back = jax.vjp(layer_norm, hidden, gain_all[2])
    u2 = normed_two.astype(BF)
    up_proj = dot(u2, full_up)
    activated, gelu_back = jax.vjp(gelu_tanh, up_proj)
    g = activated.astype(BF)
    down_proj = dot(g, full_down)
    mlp_branch, norm_four_back = jax.vjp(layer_norm, down_proj, gain_all[3])
    layer_out = (hidden + mlp_branch).astype(BF)

    down_grad, gain_four = norm_four_back(out_grad)
    dmb = down_grad.astype(BF)
    grad_down = scattered(g, dmb)
    (up_grad,) = gelu_back(contract_cols(dmb, full_down))
    dfb = up_grad.astype(BF)
    grad_up = scattered(u2, dfb)
    hidden_add, gain_three = norm_three_back(contract_cols(dfb, full_up))
    dh = out_grad + hidden_add
    attn_grad, gain_two = norm_two_back(dh)
    dab = attn_grad.astype(BF)
    grad_out = scattered(ob, dab)
    dob = contract_cols(dab, full_out).astype(BF)
    dob = swapped(dob.reshape(batch, rows, group_count, lanes).transpose(2, 0, 1, 3), near)
    back = attend_back(
        info, docs, qkv, 0, keys, k_slot, k_slot + 1, dob, attended, lse, cos_all, sin_all,
        cos_here, sin_here,
    )
    if runs == 1:
        grads = back[0]
    else:
        dkv = lax.psum_scatter(
            back[1], "ctx", scatter_dimension=0, tiled=True, axis_index_groups=far
        )
        grads = jnp.concatenate([back[0][:, None], dkv.astype(BF)], axis=1)
    dqkv = swapped(grads, near).transpose(2, 3, 1, 0, 4).reshape(count, 3 * width)
    grad_qkv = scattered(u, dqkv)
    input_add, gain_one = norm_one_back(contract_cols(dqkv, full_qkv))
    grad_tokens = dh + input_add
    grad_gains = scattered_gains(jnp.stack([gain_one, gain_two, gain_three, gain_four]))
    return (
        layer_out.reshape(batch, rows, width),
        grad_tokens.reshape(batch, rows, width),
        grad_qkv,
        grad_out,
        grad_up,
        grad_down,
        grad_gains,
    )


def solution(mesh):
    return jax.shard_map(
        per_device,
        mesh=mesh,
        in_specs=(
            P(None, ALL, None),
            P(None, "shard", None),
            P("shard", None),
            P("shard", None),
            P("shard", None),
            P("shard", None),
            P("shard", None),
            P(None, ALL, None),
        ),
        out_specs=(
            P(None, ALL, None),
            P(None, ALL, None),
            P(ALL, None),
            P(ALL, None),
            P(ALL, None),
            P(ALL, None),
            P(ALL, None),
        ),
        check_vma=False,
    )
```

```python
import functools
import math

import jax
import jax.numpy as jnp
from jax import lax
from jax.experimental import pallas as pl
from jax.experimental.pallas import tpu as pltpu
from jax.sharding import PartitionSpec as P

HEADS = 16
HDIM = 64
EPSILON = 1e-05
ROPE_BASE = 10000.0
MASKED = -1e30
ALL = ("shard", "ctx")
BF = jnp.bfloat16
F32 = jnp.float32
VMEM_LIMIT = 56 * 1024 * 1024


def layer_norm(values, gain):
    center = jnp.mean(values, axis=-1, keepdims=True)
    shifted = values - center
    spread = jnp.mean(shifted * shifted, axis=-1, keepdims=True)
    return shifted * lax.rsqrt(spread + EPSILON) * gain


def gelu_tanh(values):
    return jax.nn.gelu(values, approximate=True)


def dot(left, right):
    return jnp.dot(left, right, preferred_element_type=F32)


def contract_rows(left, right):
    return lax.dot_general(left, right, (((0,), (0,)), ((), ())), preferred_element_type=F32)


def contract_cols(left, right):
    return lax.dot_general(left, right, (((1,), (1,)), ((), ())), preferred_element_type=F32)


def rope_tables(doc_starts, blocks, rows):
    half = HDIM // 2
    lane = jnp.arange(2 * HDIM, dtype=jnp.int32)
    freqs = ROPE_BASE ** (-(lane % half).astype(F32) / half)
    sign = jnp.where(lane % HDIM < half, -1.0, 1.0).astype(F32)
    positions = jnp.arange(blocks * rows, dtype=jnp.int32).reshape(blocks, 1, rows)
    latest = jnp.zeros((blocks, doc_starts.shape[0], rows), jnp.int32)
    for d in range(doc_starts.shape[1]):
        start = doc_starts[None, :, d, None]
        latest = jnp.where(positions >= start, jnp.maximum(latest, start), latest)
    angles = (positions - latest).astype(F32)[..., None] * freqs
    return jnp.cos(angles), jnp.sin(angles) * sign


def turned(values, cos_row, sin_row):
    width = values.shape[1]
    half = HDIM // 2
    if width == HDIM:
        swapped = jnp.concatenate([values[:, half:], values[:, :half]], axis=1)
    else:
        lane = lax.broadcasted_iota(jnp.int32, values.shape, 1)
        swapped = jnp.where(
            lane % HDIM < half, pltpu.roll(values, width - half, 1), pltpu.roll(values, half, 1)
        )
    return values * cos_row[:, :width] + swapped * sin_row[:, :width]


def project_rows(u, weight, cos_row, sin_row, lanes):
    full = dot(u, weight)
    parts = [full[:, slot * lanes : (slot + 1) * lanes] for slot in range(3)]
    query = turned(parts[0], cos_row, sin_row) * HDIM ** (-0.5)
    return query, turned(parts[1], cos_row, sin_row), parts[2]


def project_kernel(where, a0, a1, b0, b1, w_ref, cos_ref, sin_ref, out_ref, u_ref):
    _, _, batch, rows, lanes = out_ref.shape
    count = batch * rows
    for side, (a, b) in enumerate(((a0, b0), (a1, b1))):
        core = where[3] ^ side
        u = jnp.concatenate([a[...], b[...]], axis=1)
        u_ref[core] = u
        cos_row = cos_ref[core].reshape(count, -1)
        sin_row = sin_ref[core].reshape(count, -1)
        for slot, part in enumerate(project_rows(u, w_ref[...], cos_row, sin_row, lanes)):
            out_ref[core, slot] = part.reshape(batch, rows, lanes).astype(BF)


def project(parts, weight, cos_all, sin_all):
    a, b = parts[0], parts[2]
    count, half = a.shape[2:]
    width, columns = weight.shape
    lanes = columns // 3
    blocks, batch, rows, _ = cos_all.shape
    a_spec = pl.BlockSpec(
        (None, None, count, half), lambda t, w: ((t // 2) ^ w[1], (t % 2) ^ w[2], 0, 0)
    )
    b_spec = pl.BlockSpec(
        (None, None, count, half), lambda t, w: ((t % 2) ^ w[2], (t // 2) ^ w[1], 0, 0)
    )
    table = pl.BlockSpec((2, batch, rows, 2 * HDIM), lambda t, w: (t, 0, 0, 0))
    return pl.pallas_call(
        project_kernel,
        out_shape=(
            jax.ShapeDtypeStruct((blocks, 3, batch, rows, lanes), BF),
            jax.ShapeDtypeStruct((blocks, count, width), BF),
        ),
        grid_spec=pltpu.PrefetchScalarGridSpec(
            num_scalar_prefetch=1,
            grid=(4,),
            in_specs=[
                a_spec, a_spec, b_spec, b_spec,
                pl.BlockSpec((width, columns), lambda t, w: (0, 0)),
                table, table,
            ],
            out_specs=(
                pl.BlockSpec((2, 3, batch, rows, lanes), lambda t, w: (t, 0, 0, 0, 0)),
                pl.BlockSpec((2, count, width), lambda t, w: (t, 0, 0)),
            ),
        ),
        compiler_params=pltpu.CompilerParams(vmem_limit_bytes=VMEM_LIMIT),
        name="project",
    )(where(), *parts, weight, cos_all, sin_all)


def project_plain(u_run, weight, cos_run, sin_run):
    blocks, batch, rows, _ = cos_run.shape
    lanes = weight.shape[1] // 3
    full = dot(u_run.reshape(-1, weight.shape[0]), weight).reshape(blocks, batch, rows, 3, -1, HDIM)
    half = HDIM // 2
    cosine, sine = (t[..., None, half:HDIM] for t in (cos_run, sin_run))

    def turn(values):
        first, second = values[..., :half], values[..., half:]
        return jnp.concatenate(
            [first * cosine - second * sine, second * cosine + first * sine], axis=-1
        )

    parts = [turn(full[..., 0, :, :]) * HDIM ** (-0.5), turn(full[..., 1, :, :]), full[..., 2, :, :]]
    return jnp.stack([p.reshape(blocks, batch, rows, lanes).astype(BF) for p in parts], axis=1)


def starts_row(info_ref, mb, docs, positions):
    latest = jnp.zeros_like(positions)
    for d in range(docs):
        start = info_ref[mb, d]
        latest = jnp.where(positions >= start, jnp.maximum(latest, start), latest)
    return latest


def start_scalar(info_ref, mb, docs, position):
    latest = jnp.int32(0)
    for d in range(docs):
        start = info_ref[mb, d]
        latest = jnp.where(position >= start, jnp.maximum(latest, start), latest)
    return latest


def attend_kernel(docs, heads, info_ref, q_ref, k_ref, v_ref, o_ref, ob_ref, lse_ref):
    mb, i = pl.program_id(0), pl.program_id(1)
    per, rows, lanes = q_ref.shape
    block = per * rows
    first = info_ref[mb, docs] + i * block
    low = start_scalar(info_ref, mb, docs, first) // block
    diag = first // block
    q_pos = first + lax.broadcasted_iota(jnp.int32, (1, block), 1)
    q_start = starts_row(info_ref, mb, docs, q_pos)
    q_all = q_ref[...].reshape(block, lanes)
    queries = [q_all[:, h * HDIM : (h + 1) * HDIM] for h in range(heads)]

    def visit(step, state):
        j = diag - step
        k_all = k_ref[pl.ds(j * per, per)].reshape(block, lanes)
        v_flip = v_ref[pl.ds(j * per, per)].reshape(block, lanes).astype(F32).T.astype(BF)
        k_pos = j * block + lax.broadcasted_iota(jnp.int32, (block, 1), 0)
        allowed = (k_pos >= q_start) & (k_pos <= q_pos)
        out = []
        for h in range(heads):
            peak, total, acc = state[h]
            scores = contract_cols(k_all[:, h * HDIM : (h + 1) * HDIM], queries[h])
            scores = jnp.where(allowed, scores, MASKED)
            new_peak = jnp.maximum(peak, jnp.max(scores, axis=0, keepdims=True))
            decay = jnp.exp(peak - new_peak)
            weights = jnp.exp(scores - new_peak)
            total = total * decay + jnp.sum(weights, axis=0, keepdims=True)
            acc = acc * decay + dot(v_flip[h * HDIM : (h + 1) * HDIM], weights.astype(BF))
            out.append((new_peak, total, acc))
        return tuple(out)

    start = tuple(
        (
            jnp.full((1, block), MASKED, F32),
            jnp.zeros((1, block), F32),
            jnp.zeros((HDIM, block), F32),
        )
        for _ in range(heads)
    )
    state = lax.fori_loop(0, diag - low + 1, visit, start)
    flipped = jnp.concatenate([acc / total for _, total, acc in state], axis=0)
    attended = flipped.T
    o_ref[...] = attended.reshape(per, rows, lanes)
    ob_ref[...] = attended.astype(BF).reshape(per, rows, lanes)
    lse_ref[...] = jnp.concatenate([peak + jnp.log(total) for peak, total, _ in state], axis=0)


def attend(info, docs, queries, q_slot, keys, k_slot, v_slot):
    group_count, _, batch, rows, lanes = queries.shape
    blocks_all = keys.shape[0]
    heads = lanes // HDIM
    per = math.gcd(group_count, max(1, 256 // rows))
    q_blocks = group_count // per
    spec = lambda slot: pl.BlockSpec(
        (per, None, None, rows, lanes), lambda b, i, info: (i, slot, b, 0, 0)
    )
    kv_spec = lambda slot: pl.BlockSpec(
        (blocks_all, None, None, rows, lanes), lambda b, i, info: (0, slot, b, 0, 0)
    )
    o_spec = pl.BlockSpec((per, None, rows, lanes), lambda b, i, info: (i, b, 0, 0))
    return pl.pallas_call(
        functools.partial(attend_kernel, docs, heads),
        out_shape=(
            jax.ShapeDtypeStruct((group_count, batch, rows, lanes), F32),
            jax.ShapeDtypeStruct((group_count, batch, rows, lanes), BF),
            jax.ShapeDtypeStruct((batch, heads, group_count * rows), F32),
        ),
        grid_spec=pltpu.PrefetchScalarGridSpec(
            num_scalar_prefetch=1,
            grid=(batch, q_blocks),
            in_specs=[spec(q_slot), kv_spec(k_slot), kv_spec(v_slot)],
            out_specs=(
                o_spec,
                o_spec,
                pl.BlockSpec((None, heads, per * rows), lambda b, i, info: (b, 0, i)),
            ),
        ),
        compiler_params=pltpu.CompilerParams(vmem_limit_bytes=VMEM_LIMIT),
        name="attend",
    )(info, queries, keys, keys)


def attend_back_kernel(
    docs, heads, per, merged, info_ref, q_ref, k_ref, v_ref, do_ref, o_ref, lse_ref, cosq_ref,
    sinq_ref, cosk_ref, sink_ref, *rest
):
    mb, j = pl.program_id(0), pl.program_id(1)
    if merged:
        out_ref, dq_acc, delta_ref = rest
    else:
        dq_ref, out_ref, dq_acc, delta_ref = rest
    group_count, rows, lanes = q_ref.shape
    block = per * rows
    q_blocks = group_count // per
    base = info_ref[mb, docs] // block

    def lanes_of(i):
        return pl.ds(pl.multiple_of(i * block, block), block)

    @pl.when(j == 0)
    def _():
        dq_acc[...] = jnp.zeros_like(dq_acc)

        def fill(i, carry):
            here = pl.ds(i * per, per)
            prod = do_ref[here].reshape(block, lanes).astype(F32) * o_ref[here].reshape(
                block, lanes
            )
            flipped = prod.T
            delta_ref[:, lanes_of(i)] = jnp.concatenate(
                [
                    jnp.sum(flipped[h * HDIM : (h + 1) * HDIM], axis=0, keepdims=True)
                    for h in range(heads)
                ],
                axis=0,
            )
            return carry

        lax.fori_loop(0, q_blocks, fill, 0)

    k_first = j * block
    last = k_first + block - 1
    end = base * block + group_count * rows
    for d in range(docs):
        start = info_ref[mb, d]
        end = jnp.where(start > last, jnp.minimum(end, start), end)
    i_low = jnp.maximum(j - base, 0)
    i_high = jnp.maximum((end - base * block + block - 1) // block, i_low)
    k_pos = k_first + lax.broadcasted_iota(jnp.int32, (block, 1), 0)
    k_all = k_ref[...].reshape(block, lanes)
    v_all = v_ref[...].reshape(block, lanes)
    k_flip = k_all.astype(F32).T.astype(BF)
    heads_of = lambda a: [a[:, h * HDIM : (h + 1) * HDIM] for h in range(heads)]
    k_heads, v_heads = heads_of(k_all), heads_of(v_all)

    def visit(i, state):
        here = pl.ds(i * per, per)
        q_heads = heads_of(q_ref[here].reshape(block, lanes))
        do_heads = heads_of(do_ref[here].reshape(block, lanes))
        q_pos = (base + i) * block + lax.broadcasted_iota(jnp.int32, (1, block), 1)
        q_start = starts_row(info_ref, mb, docs, q_pos)
        allowed = (k_pos >= q_start) & (k_pos <= q_pos)
        lse = lse_ref[:, lanes_of(i)]
        delta = delta_ref[:, lanes_of(i)]
        out = []
        for h in range(heads):
            dk, dv = state[h]
            scores = contract_cols(k_heads[h], q_heads[h])
            weights = jnp.exp(jnp.where(allowed, scores - lse[h : h + 1], MASKED))
            grad_weights = contract_cols(v_heads[h], do_heads[h])
            grad_scores = (weights * (grad_weights - delta[h : h + 1])).astype(BF)
            dv = dv + dot(weights.astype(BF), do_heads[h])
            dk = dk + dot(grad_scores, q_heads[h])
            at = slice(h * HDIM, (h + 1) * HDIM)
            dq_acc[at, lanes_of(i)] += dot(k_flip[at], grad_scores)
            out.append((dk, dv))
        return tuple(out)

    zero = jnp.zeros((block, HDIM), F32)
    state = lax.fori_loop(i_low, i_high, visit, tuple((zero, zero) for _ in range(heads)))
    dk = jnp.concatenate([dk for dk, _ in state], axis=1) if heads > 1 else state[0][0]
    dv = jnp.concatenate([dv for _, dv in state], axis=1) if heads > 1 else state[0][1]
    dk = turned(dk, cosk_ref[...].reshape(block, -1), -sink_ref[...].reshape(block, -1))
    there = pl.ds(j * per, per)
    first = lanes if merged else 0
    out_ref[there, :, first : first + lanes] = dk.reshape(per, rows, lanes).astype(out_ref.dtype)
    out_ref[there, :, first + lanes : first + 2 * lanes] = dv.reshape(per, rows, lanes).astype(
        out_ref.dtype
    )

    @pl.when(j == pl.num_programs(1) - 1)
    def _():
        def finish(i, carry):
            dq = dq_acc[:, lanes_of(i)].T
            at = pl.ds(i * per, per)
            cos_row = cosq_ref[at].reshape(block, -1)
            sin_row = sinq_ref[at].reshape(block, -1)
            dq = turned(dq, cos_row, -sin_row) * HDIM ** (-0.5)
            dq = dq.reshape(per, rows, lanes).astype(BF)
            if merged:
                out_ref[at, :, :lanes] = dq
            else:
                dq_ref[at] = dq
            return carry

        lax.fori_loop(0, q_blocks, finish, 0)


def attend_back(info, docs, queries, q_slot, keys, k_slot, v_slot, grad, attended, lse, cos_all,
                sin_all, cos_here, sin_here):
    group_count, _, batch, rows, lanes = queries.shape
    blocks_all = keys.shape[0]
    merged = blocks_all == group_count
    heads = lanes // HDIM
    per = math.gcd(group_count, max(1, 256 // rows))
    k_blocks = blocks_all // per
    full = lambda slot: pl.BlockSpec(
        (group_count, None, None, rows, lanes), lambda b, j, info: (0, slot, b, 0, 0)
    )
    part = lambda slot: pl.BlockSpec(
        (per, None, None, rows, lanes), lambda b, j, info: (j, slot, b, 0, 0)
    )
    rows_full = pl.BlockSpec((group_count, None, rows, lanes), lambda b, j, info: (0, b, 0, 0))
    length = group_count * rows
    table_q = pl.BlockSpec(
        (group_count, None, rows, 2 * HDIM), lambda b, j, info: (0, b, 0, 0)
    )
    table_k = pl.BlockSpec((per, None, rows, 2 * HDIM), lambda b, j, info: (j, b, 0, 0))
    if merged:
        out_shape = [jax.ShapeDtypeStruct((group_count, batch, rows, 3 * lanes), BF)]
        out_specs = [
            pl.BlockSpec((group_count, None, rows, 3 * lanes), lambda b, j, info: (0, b, 0, 0))
        ]
    else:
        out_shape = [
            jax.ShapeDtypeStruct((group_count, batch, rows, lanes), BF),
            jax.ShapeDtypeStruct((blocks_all, batch, rows, 2 * lanes), F32),
        ]
        out_specs = [
            rows_full,
            pl.BlockSpec((blocks_all, None, rows, 2 * lanes), lambda b, j, info: (0, b, 0, 0)),
        ]
    return pl.pallas_call(
        functools.partial(attend_back_kernel, docs, heads, per, merged),
        out_shape=out_shape,
        grid_spec=pltpu.PrefetchScalarGridSpec(
            num_scalar_prefetch=1,
            grid=(batch, k_blocks),
            in_specs=[
                full(q_slot), part(k_slot), part(v_slot), rows_full, rows_full,
                pl.BlockSpec((None, heads, length), lambda b, j, info: (b, 0, 0)),
                table_q, table_q, table_k, table_k,
            ],
            out_specs=out_specs,
            scratch_shapes=[pltpu.VMEM((lanes, length), F32), pltpu.VMEM((heads, length), F32)],
        ),
        compiler_params=pltpu.CompilerParams(vmem_limit_bytes=VMEM_LIMIT),
        name="attend_back",
    )(info, queries, keys, keys, grad, attended, lse, cos_here, sin_here, cos_all, sin_all)


def flips(mask):
    count = lax.axis_size("shard") * lax.axis_size("ctx")
    return [(i, i ^ mask) for i in range(count)]


def turns(by):
    shards, places = lax.axis_size("shard"), lax.axis_size("ctx")
    return [
        (a * places + b, ((a + by) % shards) * places + b)
        for a in range(shards)
        for b in range(places)
    ]


def sent(values, pairs):
    return lax.ppermute(values, ALL, pairs)


def picked(values, index, axis):
    return lax.dynamic_index_in_dim(values, index, axis, keepdims=False)


def cube():
    return lax.axis_size("ctx") == 8


def bits():
    place = lax.axis_index("ctx")
    return lax.axis_index("shard"), place // 4, place // 2 % 2, place % 2


def where():
    return jnp.stack(bits()).astype(jnp.int32)


def spread(values):
    half = values.shape[1] // 2
    a, b = values[:, :half], values[:, half:]
    a = jnp.stack([a, sent(a, flips(2))])
    b = jnp.stack([b, sent(b, flips(4))])
    a = jnp.stack([a, sent(a, flips(4))])
    b = jnp.stack([b, sent(b, flips(2))])
    return a, sent(a, flips(1)), b, sent(b, flips(1))


def ringed(values):
    if not cube():
        return lax.all_gather(values, "shard", axis=0)
    shards = lax.axis_size("shard")
    parts = [values] + [sent(values, turns(-k)) for k in range(1, shards)]
    start = lax.rem(shards - lax.axis_index("shard"), shards)
    return lax.dynamic_slice_in_dim(jnp.stack(parts + parts), start, shards, 0)


def ring_sum(values):
    shards = lax.axis_size("shard")
    z = lax.axis_index("shard")
    kept = picked(values, z, 0).astype(F32)
    for k in range(1, shards):
        part = picked(values, lax.rem(z + k, shards), 0)
        kept = kept + sent(part, turns(k)).astype(F32)
    return kept


def put_kernel(shards, where, own_ref, a0, a1, b0, b1, out_ref, sem):
    z, y, x, c = (where[i] for i in range(4))
    half = a0.shape[-1]
    copies = [pltpu.make_async_copy(own_ref, out_ref.at[z], sem.at[0])]
    for side, (a, b) in enumerate(((a0, b0), (a1, b1))):
        for p in range(2):
            for q in range(2):
                for k in range(1, shards):
                    source = lax.rem(z - k + shards, shards)
                    core = c ^ side
                    at_a = ((y ^ p) * 2 + (x ^ q)) * 2 + core
                    at_b = ((y ^ q) * 2 + (x ^ p)) * 2 + core
                    for part, at, first in ((a, at_a, 0), (b, at_b, half)):
                        copies.append(
                            pltpu.make_async_copy(
                                part.at[p, q, k - 1],
                                out_ref.at[source, at, :, pl.ds(first, half)],
                                sem.at[len(copies)],
                            )
                        )
    for copy in copies:
        copy.start()
    for copy in copies:
        copy.wait()


def put_together(own, parts):
    shards = lax.axis_size("shard")
    pieces, rows, columns = own.shape
    anywhere = pl.BlockSpec(memory_space=pl.ANY)
    full = (shards, pieces, rows, columns)
    return pl.pallas_call(
        functools.partial(put_kernel, shards),
        out_shape=jax.ShapeDtypeStruct(full, BF),
        grid_spec=pltpu.PrefetchScalarGridSpec(
            num_scalar_prefetch=1,
            grid=(1,),
            in_specs=[anywhere] * 5,
            out_specs=pl.BlockSpec(full, lambda i, where: (0, 0, 0, 0)),
            scratch_shapes=[pltpu.SemaphoreType.DMA((1 + 16 * (shards - 1),))],
        ),
        compiler_params=pltpu.CompilerParams(vmem_limit_bytes=VMEM_LIMIT),
        name="put_together",
    )(where(), own, *parts)


def gathered(weight, after):
    pieces = lax.axis_size("ctx")
    rows, columns = weight.shape
    size = rows // pieces
    own = weight.reshape(pieces, size, columns)
    piece = picked(own, lax.axis_index("ctx"), 0)
    if not cube():
        return lax.all_gather(piece, ALL, axis=0, tiled=True), after
    shards = lax.axis_size("shard")
    if after is not None:
        piece, _ = lax.optimization_barrier((piece, after))
    far = jnp.stack([sent(piece, turns(k)) for k in range(1, shards)])
    a, b = far[:, :, : columns // 2], far[:, :, columns // 2 :]
    a = jnp.stack([a, sent(a, flips(2))])
    b = jnp.stack([b, sent(b, flips(4))])
    a = jnp.stack([a, sent(a, flips(4))])
    b = jnp.stack([b, sent(b, flips(2))])
    full = put_together(own, (a, sent(a, flips(1)), b, sent(b, flips(1))))
    return full.reshape(shards * rows, columns), far


def summed(left, right):
    return (left.astype(F32) + right.astype(F32)).astype(BF)


def scattered(left, right):
    if not cube():
        total = contract_rows(left, right).astype(BF)
        return lax.psum_scatter(total, ALL, scatter_dimension=0, tiled=True).astype(F32)
    shards = lax.axis_size("shard")
    c = bits()[3]
    tokens, rows = left.shape
    columns = right.shape[1]
    size = rows // (8 * shards)
    flat = left.T.reshape(shards * 4, 2, size, tokens)
    half = lambda core: dot(picked(flat, core, 1).reshape(rows // 2, tokens), right).astype(BF)
    away = sent(half(1 - c), flips(1))
    total = summed(half(c), away).reshape(shards, 2, 2, size, columns)
    return ring_sum(jnp.concatenate(folded(total), axis=-1))


def folded(total):
    _, y, x, _ = bits()
    columns = total.shape[-1]
    axis = total.ndim - 4
    a, b = total[..., : columns // 2], total[..., columns // 2 :]
    a_in = sent(picked(a, 1 - y, axis), flips(4))
    b_in = sent(picked(b, 1 - x, axis + 1), flips(2))
    a = summed(picked(a, y, axis), a_in)
    b = summed(picked(b, x, axis + 1), b_in)
    a_in = sent(picked(a, 1 - x, axis), flips(2))
    b_in = sent(picked(b, 1 - y, axis), flips(4))
    return summed(picked(a, x, axis), a_in), summed(picked(b, y, axis), b_in)


def scattered_gains(grads):
    count = lax.axis_size("shard") * lax.axis_size("ctx")
    kinds = grads.shape[0]
    parts = grads.reshape(kinds, count, -1).transpose(1, 0, 2)
    parts = lax.all_to_all(parts, ALL, split_axis=0, concat_axis=0, tiled=True)
    return jnp.sum(parts, axis=0).T


def swapped(values, groups):
    return lax.all_to_all(
        values, "ctx", split_axis=0, concat_axis=0, tiled=True, axis_index_groups=groups
    )


def per_device(tokens, doc_starts, w_qkv, w_out, w_up, w_down, gains, cotangent):
    ctx_size = lax.axis_size("ctx")
    place = lax.axis_index("ctx")
    batch, rows, width = tokens.shape
    count = batch * rows
    docs = doc_starts.shape[2]
    group_count = math.gcd(HEADS, ctx_size)
    runs = ctx_size // group_count
    if runs == 1:
        near = far = None
    else:
        near = [[r * group_count + g for g in range(group_count)] for r in range(runs)]
        far = [[r * group_count + g for r in range(runs)] for g in range(group_count)]
    lanes = width // group_count

    gain_all = ringed(gains.T).transpose(1, 0, 2).reshape(gains.shape[1], width).astype(F32)
    columns = picked(w_qkv.reshape(-1, 3, group_count, lanes), lax.rem(place, group_count), 2)
    w_heads = ringed(columns.reshape(-1, 3 * lanes))
    order = w_heads
    w_heads = w_heads.reshape(width, 3 * lanes)
    full_out, order = gathered(w_out, order)
    full_up, order = gathered(w_up, order)
    full_down, order = gathered(w_down, order)

    starts = doc_starts[:, 0, :]
    cos_all, sin_all = rope_tables(starts, ctx_size, rows)
    run_first = (place // group_count) * group_count
    info = jnp.concatenate(
        [starts, jnp.broadcast_to(run_first * rows, (batch, 1)).astype(jnp.int32)], axis=1
    )

    x = tokens.reshape(count, width).astype(F32)
    out_grad = cotangent.reshape(count, width).astype(F32)
    normed, norm_one_back = jax.vjp(layer_norm, x, gain_all[0])
    u = normed.astype(BF)
    if cube():
        cos_here, sin_here = cos_all, sin_all
        qkv, u_run = project(spread(u), w_heads, cos_all, sin_all)
    else:
        cos_here, sin_here = (
            lax.dynamic_slice_in_dim(t, run_first, group_count, 0) for t in (cos_all, sin_all)
        )
        u_run = lax.all_gather(u, "ctx", axis=0, axis_index_groups=near)
        qkv = project_plain(u_run, w_heads, cos_here, sin_here)
    if runs == 1:
        keys, k_slot = qkv, 1
    else:
        keys, k_slot = (
            lax.all_gather(qkv[:, 1:], "ctx", axis=0, tiled=True, axis_index_groups=far),
            0,
        )
    attended, attended_low, lse = attend(info, docs, qkv, 0, keys, k_slot, k_slot + 1)
    ob = swapped(attended_low, near).transpose(1, 2, 0, 3).reshape(count, width)
    attn_proj = dot(ob, full_out)
    attn_branch, norm_two_back = jax.vjp(layer_norm, attn_proj, gain_all[1])
    hidden = x + attn_branch
    normed_two, norm_three_back = jax.vjp(layer_norm, hidden, gain_all[2])
    u2 = normed_two.astype(BF)
    up_proj = dot(u2, full_up)
    activated, gelu_back = jax.vjp(gelu_tanh, up_proj)
    g = activated.astype(BF)
    down_proj = dot(g, full_down)
    mlp_branch, norm_four_back = jax.vjp(layer_norm, down_proj, gain_all[3])
    layer_out = (hidden + mlp_branch).astype(BF)

    down_grad, gain_four = norm_four_back(out_grad)
    dmb = down_grad.astype(BF)
    grad_down = scattered(g, dmb)
    (up_grad,) = gelu_back(contract_cols(dmb, full_down))
    dfb = up_grad.astype(BF)
    grad_up = scattered(u2, dfb)
    hidden_add, gain_three = norm_three_back(contract_cols(dfb, full_up))
    dh = out_grad + hidden_add
    attn_grad, gain_two = norm_two_back(dh)
    dab = attn_grad.astype(BF)
    grad_out = scattered(ob, dab)
    dob = contract_cols(dab, full_out).astype(BF)
    dob = swapped(dob.reshape(batch, rows, group_count, lanes).transpose(2, 0, 1, 3), near)
    back = attend_back(
        info, docs, qkv, 0, keys, k_slot, k_slot + 1, dob, attended, lse, cos_all, sin_all,
        cos_here, sin_here,
    )
    if runs == 1:
        dqkv = back[0]
    else:
        dkv = lax.psum_scatter(
            back[1], "ctx", scatter_dimension=0, tiled=True, axis_index_groups=far
        )
        dqkv = jnp.concatenate([back[0], dkv.astype(BF)], axis=-1)
    dqkv = dqkv.reshape(group_count * count, 3 * lanes)
    du = contract_cols(dqkv, w_heads)
    qkv_part = contract_rows(u_run.reshape(group_count * count, width), dqkv)
    if cube():
        du = du.astype(BF).reshape(2, 2, 2, count, width)
        c = bits()[3]
        away = sent(picked(du, 1 - c, 2), flips(1))
        du = jnp.concatenate(folded(summed(picked(du, c, 2), away)), axis=-1).astype(F32)
        qkv_part = qkv_part.astype(BF).reshape(lax.axis_size("shard"), -1, 3 * lanes)
        qkv_part = ring_sum(qkv_part).reshape(ctx_size, -1, 3 * lanes)
        qkv_part = swapped(qkv_part, None)
        grad_qkv = qkv_part.reshape(ctx_size, -1, 3, lanes).transpose(1, 2, 0, 3)
        grad_qkv = grad_qkv.reshape(-1, 3 * width)
    else:
        du = lax.psum_scatter(
            du, "ctx", scatter_dimension=0, tiled=True, axis_index_groups=near
        )
        whole = jnp.zeros((width, 3, group_count, lanes), F32)
        whole = lax.dynamic_update_slice_in_dim(
            whole, qkv_part.reshape(width, 3, 1, lanes), lax.rem(place, group_count), 2
        )
        grad_qkv = lax.psum_scatter(
            whole.reshape(width, 3 * width), ALL, scatter_dimension=0, tiled=True
        )
    input_add, gain_one = norm_one_back(du)
    grad_tokens = dh + input_add
    grad_gains = scattered_gains(jnp.stack([gain_one, gain_two, gain_three, gain_four]))
    return (
        layer_out.reshape(batch, rows, width),
        grad_tokens.reshape(batch, rows, width),
        grad_qkv,
        grad_out,
        grad_up,
        grad_down,
        grad_gains,
    )


def solution(mesh):
    return jax.shard_map(
        per_device,
        mesh=mesh,
        in_specs=(
            P(None, ALL, None),
            P(None, "shard", None),
            P("shard", None),
            P("shard", None),
            P("shard", None),
            P("shard", None),
            P("shard", None),
            P(None, ALL, None),
        ),
        out_specs=(
            P(None, ALL, None),
            P(None, ALL, None),
            P(ALL, None),
            P(ALL, None),
            P(ALL, None),
            P(ALL, None),
            P(ALL, None),
        ),
        check_vma=False,
    )
```

```python
import functools
import math

import jax
import jax.numpy as jnp
from jax import lax
from jax.experimental import pallas as pl
from jax.experimental.pallas import tpu as pltpu
from jax.sharding import PartitionSpec as P

HEADS = 16
HDIM = 64
EPSILON = 1e-05
ROPE_BASE = 10000.0
MASKED = -1e30
ALL = ("shard", "ctx")
BF = jnp.bfloat16
F32 = jnp.float32
VMEM_LIMIT = 56 * 1024 * 1024


def layer_norm(values, gain):
    center = jnp.mean(values, axis=-1, keepdims=True)
    shifted = values - center
    spread = jnp.mean(shifted * shifted, axis=-1, keepdims=True)
    return shifted * lax.rsqrt(spread + EPSILON) * gain


def gelu_tanh(values):
    return jax.nn.gelu(values, approximate=True)


def dot(left, right):
    return jnp.dot(left, right, preferred_element_type=F32)


def contract_rows(left, right):
    return lax.dot_general(left, right, (((0,), (0,)), ((), ())), preferred_element_type=F32)


def contract_cols(left, right):
    return lax.dot_general(left, right, (((1,), (1,)), ((), ())), preferred_element_type=F32)


def rope_tables(doc_starts, blocks, rows):
    half = HDIM // 2
    lane = jnp.arange(2 * HDIM, dtype=jnp.int32)
    freqs = ROPE_BASE ** (-(lane % half).astype(F32) / half)
    sign = jnp.where(lane % HDIM < half, -1.0, 1.0).astype(F32)
    positions = jnp.arange(blocks * rows, dtype=jnp.int32).reshape(blocks, 1, rows)
    latest = jnp.zeros((blocks, doc_starts.shape[0], rows), jnp.int32)
    for d in range(doc_starts.shape[1]):
        start = doc_starts[None, :, d, None]
        latest = jnp.where(positions >= start, jnp.maximum(latest, start), latest)
    angles = (positions - latest).astype(F32)[..., None] * freqs
    return jnp.cos(angles), jnp.sin(angles) * sign


def turned(values, cos_row, sin_row):
    width = values.shape[1]
    half = HDIM // 2
    if width == HDIM:
        swapped = jnp.concatenate([values[:, half:], values[:, :half]], axis=1)
    else:
        lane = lax.broadcasted_iota(jnp.int32, values.shape, 1)
        swapped = jnp.where(
            lane % HDIM < half, pltpu.roll(values, width - half, 1), pltpu.roll(values, half, 1)
        )
    return values * cos_row[:, :width] + swapped * sin_row[:, :width]


def project_rows(u, weight, cos_row, sin_row, lanes):
    full = dot(u, weight)
    parts = [full[:, slot * lanes : (slot + 1) * lanes] for slot in range(3)]
    query = turned(parts[0], cos_row, sin_row) * HDIM ** (-0.5)
    return query, turned(parts[1], cos_row, sin_row), parts[2]


def norm_parts(values):
    shifted = values - jnp.mean(values, axis=-1, keepdims=True)
    scale = lax.rsqrt(jnp.mean(shifted * shifted, axis=-1, keepdims=True) + EPSILON)
    return shifted * scale, scale


def norm_back(grad, normed, scale, gain):
    scaled = grad * gain
    return scale * (
        scaled
        - jnp.mean(scaled, axis=-1, keepdims=True)
        - normed * jnp.mean(scaled * normed, axis=-1, keepdims=True)
    )


def project_kernel(
    shards, where, a0, a1, b0, b1, cos_ref, sin_ref, *rest
):
    part_refs, (out_ref, u_ref, w_ref, gain_ref) = rest[:shards], rest[shards:]
    _, _, batch, rows, lanes = out_ref.shape
    count = batch * rows
    size = w_ref.shape[0] // shards

    @pl.when(pl.program_id(0) == 0)
    def _():
        for k, part_ref in enumerate(part_refs):
            at = pl.multiple_of(lax.rem(where[0] - k + shards, shards) * size, size)
            w_ref[pl.ds(at, size), :] = part_ref[:size, :]
            gain_ref[:, pl.ds(at, size)] = part_ref[size:, :size].astype(F32)

    gain = gain_ref[0:1, :]
    for side, (a, b) in enumerate(((a0, b0), (a1, b1))):
        core = where[3] ^ side
        x = jnp.concatenate([a[...], b[...]], axis=1).astype(F32)
        u = (norm_parts(x)[0] * gain).astype(BF)
        u_ref[core] = u
        cos_row = cos_ref[core].reshape(count, -1)
        sin_row = sin_ref[core].reshape(count, -1)
        for slot, part in enumerate(project_rows(u, w_ref[...], cos_row, sin_row, lanes)):
            out_ref[core, slot] = part.reshape(batch, rows, lanes).astype(BF)


def project(parts, weight_parts, cos_all, sin_all):
    a, b = parts[0], parts[2]
    count, half = a.shape[2:]
    shards = len(weight_parts)
    size, columns = weight_parts[0].shape
    width = 2 * half
    kinds = size - width // shards
    lanes = columns // 3
    blocks, batch, rows, _ = cos_all.shape
    a_spec = pl.BlockSpec(
        (None, None, count, half), lambda t, w: ((t // 2) ^ w[1], (t % 2) ^ w[2], 0, 0)
    )
    b_spec = pl.BlockSpec(
        (None, None, count, half), lambda t, w: ((t % 2) ^ w[2], (t // 2) ^ w[1], 0, 0)
    )
    table = pl.BlockSpec((2, batch, rows, 2 * HDIM), lambda t, w: (t, 0, 0, 0))
    whole = lambda shape: pl.BlockSpec(shape, lambda t, w: (0, 0))
    return pl.pallas_call(
        functools.partial(project_kernel, shards),
        out_shape=(
            jax.ShapeDtypeStruct((blocks, 3, batch, rows, lanes), BF),
            jax.ShapeDtypeStruct((blocks, count, width), BF),
            jax.ShapeDtypeStruct((width, columns), BF),
            jax.ShapeDtypeStruct((kinds, width), F32),
        ),
        grid_spec=pltpu.PrefetchScalarGridSpec(
            num_scalar_prefetch=1,
            grid=(4,),
            in_specs=[a_spec, a_spec, b_spec, b_spec, table, table]
            + [whole((size, columns))] * shards,
            out_specs=(
                pl.BlockSpec((2, 3, batch, rows, lanes), lambda t, w: (t, 0, 0, 0, 0)),
                pl.BlockSpec((2, count, width), lambda t, w: (t, 0, 0)),
                whole((width, columns)),
                whole((kinds, width)),
            ),
        ),
        compiler_params=pltpu.CompilerParams(vmem_limit_bytes=VMEM_LIMIT),
        name="project",
    )(where(), *parts, cos_all, sin_all, *weight_parts)


def project_plain(u_run, weight, cos_run, sin_run):
    blocks, batch, rows, _ = cos_run.shape
    lanes = weight.shape[1] // 3
    full = dot(u_run.reshape(-1, weight.shape[0]), weight).reshape(blocks, batch, rows, 3, -1, HDIM)
    half = HDIM // 2
    cosine, sine = (t[..., None, half:HDIM] for t in (cos_run, sin_run))

    def turn(values):
        first, second = values[..., :half], values[..., half:]
        return jnp.concatenate(
            [first * cosine - second * sine, second * cosine + first * sine], axis=-1
        )

    parts = [turn(full[..., 0, :, :]) * HDIM ** (-0.5), turn(full[..., 1, :, :]), full[..., 2, :, :]]
    return jnp.stack([p.reshape(blocks, batch, rows, lanes).astype(BF) for p in parts], axis=1)


def starts_row(info_ref, mb, docs, positions):
    latest = jnp.zeros_like(positions)
    for d in range(docs):
        start = info_ref[mb, d]
        latest = jnp.where(positions >= start, jnp.maximum(latest, start), latest)
    return latest


def start_scalar(info_ref, mb, docs, position):
    latest = jnp.int32(0)
    for d in range(docs):
        start = info_ref[mb, d]
        latest = jnp.where(position >= start, jnp.maximum(latest, start), latest)
    return latest


def attend_kernel(docs, heads, mb, info_ref, q_ref, k_ref, v_ref, *rest):
    o_ref, ob_ref, lse_ref = rest[-3:]
    i = pl.program_id(0)
    per, rows, lanes = q_ref.shape
    block = per * rows
    first = info_ref[mb, docs] + i * block
    low = start_scalar(info_ref, mb, docs, first) // block
    diag = first // block
    q_pos = first + lax.broadcasted_iota(jnp.int32, (1, block), 1)
    q_start = starts_row(info_ref, mb, docs, q_pos)
    q_all = q_ref[...].reshape(block, lanes)
    queries = [q_all[:, h * HDIM : (h + 1) * HDIM] for h in range(heads)]

    def visit(step, state):
        j = diag - step
        k_all = k_ref[pl.ds(j * per, per)].reshape(block, lanes)
        v_flip = v_ref[pl.ds(j * per, per)].reshape(block, lanes).astype(F32).T.astype(BF)
        k_pos = j * block + lax.broadcasted_iota(jnp.int32, (block, 1), 0)
        allowed = (k_pos >= q_start) & (k_pos <= q_pos)
        out = []
        for h in range(heads):
            peak, total, acc = state[h]
            scores = contract_cols(k_all[:, h * HDIM : (h + 1) * HDIM], queries[h])
            scores = jnp.where(allowed, scores, MASKED)
            new_peak = jnp.maximum(peak, jnp.max(scores, axis=0, keepdims=True))
            decay = jnp.exp(peak - new_peak)
            weights = jnp.exp(scores - new_peak)
            total = total * decay + jnp.sum(weights, axis=0, keepdims=True)
            acc = acc * decay + dot(v_flip[h * HDIM : (h + 1) * HDIM], weights.astype(BF))
            out.append((new_peak, total, acc))
        return tuple(out)

    start = tuple(
        (
            jnp.full((1, block), MASKED, F32),
            jnp.zeros((1, block), F32),
            jnp.zeros((HDIM, block), F32),
        )
        for _ in range(heads)
    )
    state = lax.fori_loop(0, diag - low + 1, visit, start)
    flipped = jnp.concatenate([acc / total for _, total, acc in state], axis=0)
    attended = flipped.T
    o_ref[...] = attended.reshape(per, rows, lanes)
    ob_ref[...] = attended.astype(BF).reshape(per, rows, lanes)
    lse_ref[...] = jnp.concatenate([peak + jnp.log(total) for peak, total, _ in state], axis=0)


def attend(info, docs, mb, queries, q_slot, keys, k_slot, v_slot, earlier=()):
    group_count, _, batch, rows, lanes = queries.shape
    blocks_all = keys.shape[0]
    heads = lanes // HDIM
    per = math.gcd(group_count, max(1, 256 // rows))
    q_blocks = group_count // per
    spec = pl.BlockSpec((per, None, None, rows, lanes), lambda i, info: (i, q_slot, mb, 0, 0))
    kv_spec = lambda slot: pl.BlockSpec(
        (blocks_all, None, None, rows, lanes), lambda i, info: (0, slot, mb, 0, 0)
    )
    o_spec = pl.BlockSpec((per, None, rows, lanes), lambda i, info: (i, mb, 0, 0))
    return pl.pallas_call(
        functools.partial(attend_kernel, docs, heads, mb),
        out_shape=(
            jax.ShapeDtypeStruct((group_count, batch, rows, lanes), F32),
            jax.ShapeDtypeStruct((group_count, batch, rows, lanes), BF),
            jax.ShapeDtypeStruct((batch, heads, group_count * rows), F32),
        ),
        grid_spec=pltpu.PrefetchScalarGridSpec(
            num_scalar_prefetch=1,
            grid=(q_blocks,),
            in_specs=[spec, kv_spec(k_slot), kv_spec(v_slot)]
            + [pl.BlockSpec(memory_space=pl.ANY)] * len(earlier),
            out_specs=(
                o_spec,
                o_spec,
                pl.BlockSpec((None, heads, per * rows), lambda i, info: (mb, 0, i)),
            ),
        ),
        input_output_aliases={4 + n: n for n in range(len(earlier))},
        compiler_params=pltpu.CompilerParams(vmem_limit_bytes=VMEM_LIMIT),
        name="attend",
    )(info, queries, keys, keys, *earlier)


def attend_back_kernel(
    docs, heads, per, merged, mb, info_ref, q_ref, k_ref, v_ref, do_ref, o_ref, lse_ref, cosq_ref,
    sinq_ref, cosk_ref, sink_ref, *rest
):
    j = pl.program_id(0)
    out_ref, dq_acc, delta_ref = rest[-3:]
    dq_ref = None if merged else rest[-4]
    group_count, rows, lanes = q_ref.shape
    block = per * rows
    q_blocks = group_count // per
    base = info_ref[mb, docs] // block

    def lanes_of(i):
        return pl.ds(pl.multiple_of(i * block, block), block)

    @pl.when(j == 0)
    def _():
        dq_acc[...] = jnp.zeros_like(dq_acc)

        def fill(i, carry):
            here = pl.ds(i * per, per)
            prod = do_ref[here].reshape(block, lanes).astype(F32) * o_ref[here].reshape(
                block, lanes
            )
            flipped = prod.T
            delta_ref[:, lanes_of(i)] = jnp.concatenate(
                [
                    jnp.sum(flipped[h * HDIM : (h + 1) * HDIM], axis=0, keepdims=True)
                    for h in range(heads)
                ],
                axis=0,
            )
            return carry

        lax.fori_loop(0, q_blocks, fill, 0)

    k_first = j * block
    last = k_first + block - 1
    end = base * block + group_count * rows
    for d in range(docs):
        start = info_ref[mb, d]
        end = jnp.where(start > last, jnp.minimum(end, start), end)
    i_low = jnp.maximum(j - base, 0)
    i_high = jnp.maximum((end - base * block + block - 1) // block, i_low)
    k_pos = k_first + lax.broadcasted_iota(jnp.int32, (block, 1), 0)
    k_all = k_ref[...].reshape(block, lanes)
    v_all = v_ref[...].reshape(block, lanes)
    k_flip = k_all.astype(F32).T.astype(BF)
    heads_of = lambda a: [a[:, h * HDIM : (h + 1) * HDIM] for h in range(heads)]
    k_heads, v_heads = heads_of(k_all), heads_of(v_all)

    def visit(i, state):
        here = pl.ds(i * per, per)
        q_heads = heads_of(q_ref[here].reshape(block, lanes))
        do_heads = heads_of(do_ref[here].reshape(block, lanes))
        q_pos = (base + i) * block + lax.broadcasted_iota(jnp.int32, (1, block), 1)
        q_start = starts_row(info_ref, mb, docs, q_pos)
        allowed = (k_pos >= q_start) & (k_pos <= q_pos)
        lse = lse_ref[:, lanes_of(i)]
        delta = delta_ref[:, lanes_of(i)]
        out = []
        for h in range(heads):
            dk, dv = state[h]
            scores = contract_cols(k_heads[h], q_heads[h])
            weights = jnp.exp(jnp.where(allowed, scores - lse[h : h + 1], MASKED))
            grad_weights = contract_cols(v_heads[h], do_heads[h])
            grad_scores = (weights * (grad_weights - delta[h : h + 1])).astype(BF)
            dv = dv + dot(weights.astype(BF), do_heads[h])
            dk = dk + dot(grad_scores, q_heads[h])
            at = slice(h * HDIM, (h + 1) * HDIM)
            dq_acc[at, lanes_of(i)] += dot(k_flip[at], grad_scores)
            out.append((dk, dv))
        return tuple(out)

    zero = jnp.zeros((block, HDIM), F32)
    state = lax.fori_loop(i_low, i_high, visit, tuple((zero, zero) for _ in range(heads)))
    dk = jnp.concatenate([dk for dk, _ in state], axis=1) if heads > 1 else state[0][0]
    dv = jnp.concatenate([dv for _, dv in state], axis=1) if heads > 1 else state[0][1]
    dk = turned(dk, cosk_ref[...].reshape(block, -1), -sink_ref[...].reshape(block, -1))
    there = pl.ds(j * per, per)
    first = lanes if merged else 0
    out_ref[there, :, first : first + lanes] = dk.reshape(per, rows, lanes).astype(out_ref.dtype)
    out_ref[there, :, first + lanes : first + 2 * lanes] = dv.reshape(per, rows, lanes).astype(
        out_ref.dtype
    )

    @pl.when(j == pl.num_programs(0) - 1)
    def _():
        def finish(i, carry):
            dq = dq_acc[:, lanes_of(i)].T
            at = pl.ds(i * per, per)
            cos_row = cosq_ref[at].reshape(block, -1)
            sin_row = sinq_ref[at].reshape(block, -1)
            dq = turned(dq, cos_row, -sin_row) * HDIM ** (-0.5)
            dq = dq.reshape(per, rows, lanes).astype(BF)
            if merged:
                out_ref[at, :, :lanes] = dq
            else:
                dq_ref[at] = dq
            return carry

        lax.fori_loop(0, q_blocks, finish, 0)


def attend_back(info, docs, mb, queries, q_slot, keys, k_slot, v_slot, grad, attended, lse,
                cos_all, sin_all, cos_here, sin_here, earlier=()):
    group_count, _, batch, rows, lanes = queries.shape
    blocks_all = keys.shape[0]
    merged = blocks_all == group_count
    heads = lanes // HDIM
    per = math.gcd(group_count, max(1, 256 // rows))
    length = group_count * rows
    full = pl.BlockSpec(
        (group_count, None, None, rows, lanes), lambda j, info: (0, q_slot, mb, 0, 0)
    )
    part = lambda slot: pl.BlockSpec(
        (per, None, None, rows, lanes), lambda j, info: (j, slot, mb, 0, 0)
    )
    rows_of_mb = lambda count, width: pl.BlockSpec(
        (count, None, rows, width), lambda j, info: (0, mb, 0, 0)
    )
    table_k = pl.BlockSpec((per, None, rows, 2 * HDIM), lambda j, info: (j, mb, 0, 0))
    if merged:
        out_shape = [jax.ShapeDtypeStruct((group_count, batch, rows, 3 * lanes), BF)]
        out_specs = [rows_of_mb(group_count, 3 * lanes)]
    else:
        out_shape = [
            jax.ShapeDtypeStruct((group_count, batch, rows, lanes), BF),
            jax.ShapeDtypeStruct((blocks_all, batch, rows, 2 * lanes), F32),
        ]
        out_specs = [rows_of_mb(group_count, lanes), rows_of_mb(blocks_all, 2 * lanes)]
    table_q = rows_of_mb(group_count, 2 * HDIM)
    return pl.pallas_call(
        functools.partial(attend_back_kernel, docs, heads, per, merged, mb),
        out_shape=out_shape,
        grid_spec=pltpu.PrefetchScalarGridSpec(
            num_scalar_prefetch=1,
            grid=(blocks_all // per,),
            in_specs=[
                full, part(k_slot), part(v_slot), rows_of_mb(group_count, lanes),
                rows_of_mb(group_count, lanes),
                pl.BlockSpec((None, heads, length), lambda j, info: (mb, 0, 0)),
                table_q, table_q, table_k, table_k,
            ]
            + [pl.BlockSpec(memory_space=pl.ANY)] * len(earlier),
            out_specs=out_specs,
            scratch_shapes=[pltpu.VMEM((lanes, length), F32), pltpu.VMEM((heads, length), F32)],
        ),
        input_output_aliases={11 + n: n for n in range(len(earlier))},
        compiler_params=pltpu.CompilerParams(vmem_limit_bytes=VMEM_LIMIT),
        name="attend_back",
    )(info, queries, keys, keys, grad, attended, lse, cos_here, sin_here, cos_all, sin_all,
      *earlier)


def flips(mask):
    count = lax.axis_size("shard") * lax.axis_size("ctx")
    return [(i, i ^ mask) for i in range(count)]


def turns(by):
    shards, places = lax.axis_size("shard"), lax.axis_size("ctx")
    return [
        (a * places + b, ((a + by) % shards) * places + b)
        for a in range(shards)
        for b in range(places)
    ]


def sent(values, pairs):
    return lax.ppermute(values, ALL, pairs)


def picked(values, index, axis):
    return lax.dynamic_index_in_dim(values, index, axis, keepdims=False)


def cube():
    return lax.axis_size("ctx") == 8


def bits():
    place = lax.axis_index("ctx")
    return lax.axis_index("shard"), place // 4, place // 2 % 2, place % 2


def where():
    return jnp.stack(bits()).astype(jnp.int32)


def spread(values, early):
    half = values.shape[1] // 2
    a, b = values[:, :half], values[:, half:]
    a_in, b_in = sent(a, flips(2)), sent(b, flips(4))
    a, b = jnp.stack([a, after(a_in, *early)]), jnp.stack([b, after(b_in, *early)])
    middle = (a, b)
    a = jnp.stack([a, sent(a, flips(4))])
    b = jnp.stack([b, sent(b, flips(2))])
    return (a, sent(a, flips(1)), b, sent(b, flips(1))), middle


def ring_sum(values):
    shards = lax.axis_size("shard")
    z = lax.axis_index("shard")
    kept = picked(values, z, 0).astype(F32)
    for k in range(1, shards):
        part = picked(values, lax.rem(z + k, shards), 0)
        kept = kept + sent(part, turns(k)).astype(F32)
    return kept


def after(values, *earlier):
    return lax.optimization_barrier((values,) + earlier)[0]


def far_rows(piece):
    shards = lax.axis_size("shard")
    return jnp.stack([sent(piece, turns(k)) for k in range(1, shards)])


def copies_in(where, owns, parts, out_ref, sem):
    z, y, x, c = (where[i] for i in range(4))
    shards = out_ref.shape[0]
    half = parts[0].shape[-1]
    groups = [[] for _ in range(shards)]

    def add(k, source, target):
        at = sum(len(group) for group in groups)
        groups[k].append(pltpu.make_async_copy(source, target, sem.at[at]))

    first = 0
    for own in owns:
        add(0, own, out_ref.at[z, :, :, pl.ds(first, own.shape[-1])])
        first += own.shape[-1]
    for k in range(1, shards):
        source = lax.rem(z - k + shards, shards)
        for side in range(2):
            a, b = parts[side], parts[2 + side]
            core = c ^ side
            for p in range(2):
                for q in range(2):
                    at_a = ((y ^ p) * 2 + (x ^ q)) * 2 + core
                    at_b = ((y ^ q) * 2 + (x ^ p)) * 2 + core
                    add(k, a.at[p, q, k - 1], out_ref.at[source, at_a, :, pl.ds(0, half)])
                    add(k, b.at[p, q, k - 1], out_ref.at[source, at_b, :, pl.ds(half, half)])
    for group in groups:
        for copy in group:
            copy.start()
    return groups


def arrived(groups, where):
    shards = len(groups)
    for k, group in enumerate(groups):
        for copy in group:
            copy.wait()
        yield lax.rem(where[0] - k + shards, shards)


def copy_count(shards, owns):
    return owns + 16 * (shards - 1)


def rows_of(w, first, last):
    part = w[:, :, :, first:last]
    return part.reshape(-1, last - first)


def chunk_of(w, z, first, last):
    part = w[z, :, :, first:last]
    return part.reshape(-1, last - first)


def block_at(z, size):
    return pl.ds(pl.multiple_of(z * size, size), size)


def flip_pieces(values, size, out_ref, first):
    tokens, rows = values.shape
    step = max(size, 128)
    for start in range(0, rows, step):
        flip = values[:, start : start + step].astype(F32).T.astype(BF)
        for low in range(0, step, size):
            piece = (start + low) // size
            z, y, x, c = piece // 8, piece // 4 % 2, piece // 2 % 2, piece % 2
            out_ref[c, y, x, z, :, first : first + tokens] = flip[low : low + size]


def mlp_in_kernel(
    where, ob_ref, x_ref, gain_ref, own_out, own_up, a0, a1, b0, b1,
    a_ref, h_ref, g_ref, slope_ref, in_flip, g_flip, w, obl, sem
):
    copies = copies_in(where, (own_out, own_up), (a0, a1, b0, b1), w, sem)
    groups, batch, rows, lanes = ob_ref.shape
    shards = w.shape[0]
    width = x_ref.shape[1]
    count = batch * rows
    size = width // shards
    for mb in range(batch):
        for g in range(groups):
            obl[mb * rows : (mb + 1) * rows, g * lanes : (g + 1) * lanes] = ob_ref[g, mb]
    flip_pieces(obl[...], size // 8, in_flip, count)
    a = None
    for z in arrived(copies, where):
        part = dot(obl[:, block_at(z, size)], chunk_of(w, z, 0, width))
        a = part if a is None else a + part
    a_ref[...] = a
    h = x_ref[...].astype(F32) + norm_parts(a)[0] * gain_ref[1:2, :]
    h_ref[...] = h
    u2 = (norm_parts(h)[0] * gain_ref[2:3, :]).astype(BF)
    flip_pieces(u2, size // 8, in_flip, 0)
    hidden = g_ref.shape[1]
    step = 512
    root = math.sqrt(2.0 / math.pi)
    for first in range(0, hidden, step):
        f = dot(u2, rows_of(w, width + first, width + first + step))
        square = f * f
        bent = jnp.tanh(root * (f + 0.044715 * (square * f)))
        half = 0.5 * (1.0 + bent)
        at = slice(first, first + step)
        g_ref[:, at] = (f * half).astype(BF)
        slope = half + 0.5 * f * (1.0 - bent * bent) * (root * (1.0 + 3 * 0.044715 * square))
        slope_ref[:, at] = slope.astype(BF)
    flip_pieces(g_ref[...], hidden // (8 * shards), g_flip, 0)


def mlp_in(ob, x, gain_all, w_out, w_up, parts):
    shards = lax.axis_size("shard")
    count, width = x.shape
    hidden = w_up.shape[-1]
    pieces, rows = w_out.shape[:2]
    anywhere = pl.BlockSpec(memory_space=pl.ANY)
    local = pl.BlockSpec(memory_space=pltpu.VMEM)
    shape = jax.ShapeDtypeStruct
    return pl.pallas_call(
        mlp_in_kernel,
        out_shape=(
            shape((count, width), F32),
            shape((count, width), F32),
            shape((count, hidden), BF),
            shape((count, hidden), BF),
            shape((2, 2, 2, shards, width // (8 * shards), 2 * count), BF),
            shape((2, 2, 2, shards, hidden // (8 * shards), count), BF),
        ),
        grid_spec=pltpu.PrefetchScalarGridSpec(
            num_scalar_prefetch=1,
            grid=(),
            in_specs=[local] * 3 + [anywhere] * 6,
            out_specs=[local] * 6,
            scratch_shapes=[
                pltpu.VMEM((shards, pieces, rows, width + hidden), BF),
                pltpu.VMEM((count, width), BF),
                pltpu.SemaphoreType.DMA((copy_count(shards, 2),)),
            ],
        ),
        compiler_params=pltpu.CompilerParams(vmem_limit_bytes=VMEM_LIMIT),
        name="mlp_in",
    )(where(), ob, x, gain_all, w_out, w_up, *parts)


def mlp_out_kernel(
    where, g_ref, slope_ref, h_ref, cot_ref, gain_ref, own, a0, a1, b0, b1,
    out_ref, dmb_ref, dfb_ref, gg_ref, w, sem
):
    copies = copies_in(where, (own,), (a0, a1, b0, b1), w, sem)
    shards = w.shape[0]
    width = h_ref.shape[1]
    size = g_ref.shape[1] // shards
    m = None
    for z in arrived(copies, where):
        part = dot(g_ref[:, block_at(z, size)], chunk_of(w, z, 0, width))
        m = part if m is None else m + part
    gain = gain_ref[3:4, :]
    normed, scale = norm_parts(m)
    out_ref[...] = (h_ref[...] + normed * gain).astype(BF)
    dy = cot_ref[...].astype(F32)
    gg_ref[...] = jnp.sum(dy * normed, axis=0, keepdims=True)
    dmb = norm_back(dy, normed, scale, gain).astype(BF)
    dmb_ref[...] = dmb
    for z in range(shards):
        at = slice(z * size, (z + 1) * size)
        dg = contract_cols(dmb, chunk_of(w, z, 0, width))
        dfb_ref[:, at] = (dg * slope_ref[:, at].astype(F32)).astype(BF)


def mlp_out(g, slope, h, cot, gain_all, w_down, parts):
    shards = lax.axis_size("shard")
    count, width = h.shape
    hidden = g.shape[1]
    pieces, rows = w_down.shape[:2]
    anywhere = pl.BlockSpec(memory_space=pl.ANY)
    local = pl.BlockSpec(memory_space=pltpu.VMEM)
    shape = jax.ShapeDtypeStruct
    return pl.pallas_call(
        mlp_out_kernel,
        out_shape=(
            shape((count, width), BF),
            shape((count, width), BF),
            shape((count, hidden), BF),
            shape((1, width), F32),
        ),
        grid_spec=pltpu.PrefetchScalarGridSpec(
            num_scalar_prefetch=1,
            grid=(),
            in_specs=[local] * 5 + [anywhere] * 5,
            out_specs=[local] * 4,
            scratch_shapes=[
                pltpu.VMEM((shards, pieces, rows, width), BF),
                pltpu.SemaphoreType.DMA((copy_count(shards, 1),)),
            ],
        ),
        compiler_params=pltpu.CompilerParams(vmem_limit_bytes=VMEM_LIMIT),
        name="mlp_out",
    )(where(), g, slope, h, cot, gain_all, w_down, *parts)


def mlp_back_kernel(
    where, dfb_ref, h_ref, a_ref, cot_ref, gain_ref, own_out, own_up, a0, a1, b0, b1,
    dh_ref, right_ref, dob_ref, gg_ref, w, du2, sem
):
    copies = copies_in(where, (own_out, own_up), (a0, a1, b0, b1), w, sem)
    shards = w.shape[0]
    count, width = h_ref.shape
    size = width // shards
    groups, batch, rows, lanes = dob_ref.shape
    last = w.shape[-1]
    right_ref[:count, :width] = jnp.zeros((count, width), BF)
    right_ref[count:, width:] = jnp.zeros((count, last - width), BF)
    right_ref[:count, width:] = dfb_ref[...]
    for z in arrived(copies, where):
        du2[:, block_at(z, size)] = contract_cols(dfb_ref[...], chunk_of(w, z, width, last))
    normed, scale = norm_parts(h_ref[...])
    dh = cot_ref[...].astype(F32) + norm_back(du2[...], normed, scale, gain_ref[2:3, :])
    dh_ref[...] = dh
    normed, scale = norm_parts(a_ref[...])
    gg_ref[...] = jnp.sum(dh * normed, axis=0, keepdims=True)
    dab = norm_back(dh, normed, scale, gain_ref[1:2, :]).astype(BF)
    right_ref[count:, :width] = dab
    for z in range(shards):
        dob = contract_cols(dab, chunk_of(w, z, 0, width)).astype(BF)
        for part in range(size // lanes):
            for mb in range(batch):
                dob_ref[z * (size // lanes) + part, mb] = dob[
                    mb * rows : (mb + 1) * rows, part * lanes : (part + 1) * lanes
                ]


def mlp_back(dfb, h, a, cot, gain_all, w_out, w_up, parts, groups, batch):
    shards = lax.axis_size("shard")
    count, width = h.shape
    hidden = dfb.shape[1]
    pieces, rows = w_out.shape[:2]
    anywhere = pl.BlockSpec(memory_space=pl.ANY)
    local = pl.BlockSpec(memory_space=pltpu.VMEM)
    shape = jax.ShapeDtypeStruct
    return pl.pallas_call(
        mlp_back_kernel,
        out_shape=(
            shape((count, width), F32),
            shape((2 * count, width + hidden), BF),
            shape((groups, batch, count // batch, width // groups), BF),
            shape((1, width), F32),
        ),
        grid_spec=pltpu.PrefetchScalarGridSpec(
            num_scalar_prefetch=1,
            grid=(),
            in_specs=[local] * 5 + [anywhere] * 6,
            out_specs=[local] * 4,
            scratch_shapes=[
                pltpu.VMEM((shards, pieces, rows, width + hidden), BF),
                pltpu.VMEM((count, width), F32),
                pltpu.SemaphoreType.DMA((copy_count(shards, 2),)),
            ],
        ),
        compiler_params=pltpu.CompilerParams(vmem_limit_bytes=VMEM_LIMIT),
        name="mlp_back",
    )(where(), dfb, h, a, cot, gain_all, w_out, w_up, *parts)


def product(left, right, *addends):
    total = dot(left.reshape(-1, left.shape[-1]), right)
    total = total.reshape(*left.shape[:-1], right.shape[1])
    for addend in addends:
        total = total + addend.astype(F32)
    return total.astype(BF)


def halves(values):
    half = values.shape[-1] // 2
    return values[..., :half], values[..., half:]


def first_away(left, right):
    return product(picked(left, 1 - bits()[3], 0), right)


def second_away(left, right, core_in):
    _, y, x, c = bits()
    left = picked(left, c, 0)
    (right_a, right_b), (in_a, in_b) = halves(right), halves(core_in)
    return (
        product(picked(left, 1 - y, 0), right_a, picked(in_a, 1 - y, 0)),
        product(picked(left, 1 - x, 1), right_b, picked(in_b, 1 - x, 1)),
    )


def third_away(left, right, core_in, a_in, b_in):
    _, y, x, c = bits()
    left = picked(left, c, 0)
    (right_a, right_b), (in_a, in_b) = halves(right), halves(core_in)
    at = lambda values, y, x: picked(picked(values, y, 0), x, 0)
    return (
        product(at(left, y, 1 - x), right_a, at(in_a, y, 1 - x), picked(a_in, 1 - x, 0)),
        product(at(left, 1 - y, x), right_b, at(in_b, 1 - y, x), picked(b_in, 1 - y, 0)),
    )


def last_total(left, right, core_in, a_in, b_in, a_last, b_last):
    _, y, x, c = bits()
    (right_a, right_b), (in_a, in_b) = halves(right), halves(core_in)
    at = lambda values: picked(picked(values, y, 0), x, 0)
    left = at(picked(left, c, 0))
    a = product(left, right_a, at(in_a), picked(a_in, x, 0), a_last)
    b = product(left, right_b, at(in_b), picked(b_in, y, 0), b_last)
    return jnp.concatenate([a, b], axis=-1)


def summed(left, right):
    return (left.astype(F32) + right.astype(F32)).astype(BF)


def gathered(weight):
    size = weight.shape[0] // lax.axis_size("ctx")
    piece = lax.dynamic_slice_in_dim(weight, lax.axis_index("ctx") * size, size, 0)
    return lax.all_gather(piece, ALL, axis=0, tiled=True)


def scattered(left, right):
    total = contract_rows(left, right).astype(BF)
    return lax.psum_scatter(total, ALL, scatter_dimension=0, tiled=True).astype(F32)


def folded(total):
    _, y, x, _ = bits()
    columns = total.shape[-1]
    axis = total.ndim - 4
    a, b = total[..., : columns // 2], total[..., columns // 2 :]
    a_in = sent(picked(a, 1 - y, axis), flips(4))
    b_in = sent(picked(b, 1 - x, axis + 1), flips(2))
    a = summed(picked(a, y, axis), a_in)
    b = summed(picked(b, x, axis + 1), b_in)
    a_in = sent(picked(a, 1 - x, axis), flips(2))
    b_in = sent(picked(b, 1 - y, axis), flips(4))
    return summed(picked(a, x, axis), a_in), summed(picked(b, y, axis), b_in)


def scattered_gains(grads):
    count = lax.axis_size("shard") * lax.axis_size("ctx")
    kinds = grads.shape[0]
    parts = grads.reshape(kinds, count, -1).transpose(1, 0, 2)
    parts = lax.all_to_all(parts, ALL, split_axis=0, concat_axis=0, tiled=True)
    return jnp.sum(parts, axis=0).T


def swapped(values, groups):
    return lax.all_to_all(
        values, "ctx", split_axis=0, concat_axis=0, tiled=True, axis_index_groups=groups
    )


def plain(tokens, doc_starts, w_qkv, w_out, w_up, w_down, gains, cotangent):
    ctx_size = lax.axis_size("ctx")
    place = lax.axis_index("ctx")
    batch, rows, width = tokens.shape
    count = batch * rows
    docs = doc_starts.shape[2]
    group_count = math.gcd(HEADS, ctx_size)
    runs = ctx_size // group_count
    if runs == 1:
        near = far = None
    else:
        near = [[r * group_count + g for g in range(group_count)] for r in range(runs)]
        far = [[r * group_count + g for r in range(runs)] for g in range(group_count)]
    lanes = width // group_count

    gain_all = lax.all_gather(gains, "shard", axis=0, tiled=True).T.astype(F32)
    columns = picked(w_qkv.reshape(-1, 3, group_count, lanes), lax.rem(place, group_count), 2)
    w_heads = lax.all_gather(columns.reshape(-1, 3 * lanes), "shard", axis=0, tiled=True)
    full_out, full_up, full_down = gathered(w_out), gathered(w_up), gathered(w_down)

    starts = doc_starts[:, 0, :]
    cos_all, sin_all = rope_tables(starts, ctx_size, rows)
    run_first = (place // group_count) * group_count
    info = jnp.concatenate(
        [starts, jnp.broadcast_to(run_first * rows, (batch, 1)).astype(jnp.int32)], axis=1
    )

    x = tokens.reshape(count, width).astype(F32)
    out_grad = cotangent.reshape(count, width).astype(F32)
    normed, norm_one_back = jax.vjp(layer_norm, x, gain_all[0])
    u = normed.astype(BF)
    cos_here, sin_here = (
        lax.dynamic_slice_in_dim(t, run_first, group_count, 0) for t in (cos_all, sin_all)
    )
    u_run = lax.all_gather(u, "ctx", axis=0, axis_index_groups=near)
    qkv = project_plain(u_run, w_heads, cos_here, sin_here)
    if runs == 1:
        keys, k_slot = qkv, 1
    else:
        keys, k_slot = (
            lax.all_gather(qkv[:, 1:], "ctx", axis=0, tiled=True, axis_index_groups=far),
            0,
        )
    held = ()
    for mb in range(batch):
        held = attend(info, docs, mb, qkv, 0, keys, k_slot, k_slot + 1, held)
    attended, attended_low, lse = held
    ob = swapped(attended_low, near).transpose(1, 2, 0, 3).reshape(count, width)
    attn_proj = dot(ob, full_out)
    attn_branch, norm_two_back = jax.vjp(layer_norm, attn_proj, gain_all[1])
    hidden = x + attn_branch
    normed_two, norm_three_back = jax.vjp(layer_norm, hidden, gain_all[2])
    u2 = normed_two.astype(BF)
    up_proj = dot(u2, full_up)
    activated, gelu_back = jax.vjp(gelu_tanh, up_proj)
    g = activated.astype(BF)
    down_proj = dot(g, full_down)
    mlp_branch, norm_four_back = jax.vjp(layer_norm, down_proj, gain_all[3])
    layer_out = (hidden + mlp_branch).astype(BF)

    down_grad, gain_four = norm_four_back(out_grad)
    dmb = down_grad.astype(BF)
    grad_down = scattered(g, dmb)
    (up_grad,) = gelu_back(contract_cols(dmb, full_down))
    dfb = up_grad.astype(BF)
    grad_up = scattered(u2, dfb)
    hidden_add, gain_three = norm_three_back(contract_cols(dfb, full_up))
    dh = out_grad + hidden_add
    attn_grad, gain_two = norm_two_back(dh)
    dab = attn_grad.astype(BF)
    grad_out = scattered(ob, dab)
    dob = contract_cols(dab, full_out).astype(BF)
    dob = swapped(dob.reshape(batch, rows, group_count, lanes).transpose(2, 0, 1, 3), near)
    back = ()
    for mb in range(batch):
        back = attend_back(
            info, docs, mb, qkv, 0, keys, k_slot, k_slot + 1, dob, attended, lse, cos_all, sin_all,
            cos_here, sin_here, back,
        )
    if runs == 1:
        dqkv = back[0]
    else:
        dkv = lax.psum_scatter(
            back[1], "ctx", scatter_dimension=0, tiled=True, axis_index_groups=far
        )
        dqkv = jnp.concatenate([back[0], dkv.astype(BF)], axis=-1)
    dqkv = dqkv.reshape(group_count * count, 3 * lanes)
    du = contract_cols(dqkv, w_heads)
    qkv_part = contract_rows(u_run.reshape(group_count * count, width), dqkv)
    du = lax.psum_scatter(du, "ctx", scatter_dimension=0, tiled=True, axis_index_groups=near)
    own = jnp.zeros((width, 3, group_count, lanes), F32)
    own = lax.dynamic_update_slice_in_dim(
        own, qkv_part.reshape(width, 3, 1, lanes), lax.rem(place, group_count), 2
    )
    grad_qkv = lax.psum_scatter(
        own.reshape(width, 3 * width), ALL, scatter_dimension=0, tiled=True
    )
    input_add, gain_one = norm_one_back(du)
    grad_tokens = dh + input_add
    grad_gains = scattered_gains(jnp.stack([gain_one, gain_two, gain_three, gain_four]))
    return (
        layer_out.reshape(batch, rows, width),
        grad_tokens.reshape(batch, rows, width),
        grad_qkv,
        grad_out,
        grad_up,
        grad_down,
        grad_gains,
    )


def staged(tokens, doc_starts, w_qkv, w_out, w_up, w_down, gains, cotangent):
    ctx_size, shards = lax.axis_size("ctx"), lax.axis_size("shard")
    place = lax.axis_index("ctx")
    batch, rows, width = tokens.shape
    count = batch * rows
    docs = doc_starts.shape[2]
    lanes = width // ctx_size
    kinds = gains.shape[1]
    x = tokens.reshape(count, width)
    cot = cotangent.reshape(count, width)
    split = lambda w: w.reshape(ctx_size, -1, w.shape[1])
    own_out, own_up, own_down = split(w_out), split(w_up), split(w_down)

    starts = doc_starts[:, 0, :]
    cos_all, sin_all = rope_tables(starts, ctx_size, rows)
    x_parts, middle = spread(x, (cos_all, sin_all))
    columns = picked(w_qkv.reshape(-1, 3, ctx_size, lanes), place, 2).reshape(-1, 3 * lanes)
    gain_rows = jnp.pad(gains.T, ((0, 8 - kinds), (0, 3 * lanes - gains.shape[0])))
    piece = jnp.concatenate([columns, gain_rows])
    head_parts = [piece] + [sent(piece, turns(k)) for k in range(1, shards)]

    piece = jnp.concatenate([picked(own_out, place, 0), picked(own_up, place, 0)], axis=1)
    far_in = far_rows(after(piece, *middle, *head_parts))
    far_out = far_rows(after(picked(own_down, place, 0), far_in))

    info = jnp.concatenate([starts, jnp.zeros((batch, 1), jnp.int32)], axis=1)
    qkv, u_run, w_heads, gain_all = project(x_parts, head_parts, cos_all, sin_all)

    half = far_in.shape[2] // 2
    a, b = (after(t, qkv) for t in (far_in[:, :, :half], far_in[:, :, half:]))
    a_in, b_in = sent(a, flips(2)), sent(b, flips(4))
    held = ()
    for mb in range(batch):
        held = attend(after(info, far_in, *held), docs, mb, qkv, 0, qkv, 1, 2, held)
        if mb == 0:
            a, b = jnp.stack([a, after(a_in, held[2])]), jnp.stack([b, after(b_in, held[2])])
            info = after(info, a, b)
    attended, attended_low, lse = held
    a_in, b_in = sent(a, flips(4)), sent(b, flips(2))
    ob = swapped(attended_low, None)
    a = jnp.stack([a, after(a_in, ob, far_out)])
    b = jnp.stack([b, after(b_in, ob, far_out)])
    in_parts = (a, sent(a, flips(1)), b, sent(b, flips(1)))
    half = far_out.shape[2] // 2
    c, d = (after(t, ob) for t in (far_out[:, :, :half], far_out[:, :, half:]))
    c_in, d_in = sent(c, flips(2)), sent(d, flips(4))
    c, d = jnp.stack([c, c_in]), jnp.stack([d, d_in])
    c_in, d_in = sent(c, flips(4)), sent(d, flips(2))

    attn, h, g, slope, in_flip, g_flip = mlp_in(
        after(ob, c, d), x, gain_all, own_out, own_up, in_parts
    )
    c, d = jnp.stack([c, after(c_in, h)]), jnp.stack([d, after(d_in, h)])
    out_parts = (c, sent(c, flips(1)), d, sent(d, flips(1)))
    layer_out, dmb, dfb, gain_four = mlp_out(g, slope, h, cot, gain_all, own_down, out_parts)

    away = first_away(g_flip, dmb)
    down_in = sent(away, flips(1))
    dh, right, dob, gain_two = mlp_back(
        after(dfb, away), h, attn, cot, gain_all, own_out, own_up, in_parts, ctx_size, batch
    )
    dob = swapped(dob, None)
    away = first_away(in_flip, right)
    up_in = sent(away, flips(1))
    a, b = second_away(g_flip, after(dmb, away), down_in)
    a_in, b_in = sent(a, flips(4)), sent(b, flips(2))
    back = ()
    for mb in range(batch):
        back = attend_back(
            after(info, a, b, *back), docs, mb, qkv, 0, qkv, 1, 2, dob, attended, lse, cos_all,
            sin_all, cos_all, sin_all, back,
        )
        if mb == 0:
            c, d = second_away(in_flip, after(right, *back), up_in)
            c_in, d_in = sent(c, flips(4)), sent(d, flips(2))
            a, b = third_away(g_flip, after(dmb, c, d), down_in, a_in, b_in)
            a_last, b_last = sent(a, flips(2)), sent(b, flips(4))
    (dqkv,) = back
    dqkv = dqkv.reshape(ctx_size * count, 3 * lanes)
    du = contract_cols(dqkv, w_heads).astype(BF).reshape(2, 2, 2, count, width)
    core = bits()[3]
    du_in = sent(picked(du, 1 - core, 2), flips(1))
    qkv_part = contract_rows(u_run.reshape(ctx_size * count, width), dqkv)
    grad_qkv = ring_sum(qkv_part.astype(BF).reshape(shards, -1, 3 * lanes))
    grad_down = ring_sum(
        last_total(g_flip, after(dmb, qkv_part), down_in, a_in, b_in, a_last, b_last)
    )
    du = jnp.concatenate(folded(summed(picked(du, core, 2), du_in)), axis=-1).astype(F32)
    c, d = third_away(in_flip, right, up_in, c_in, d_in)
    c_last, d_last = sent(c, flips(2)), sent(d, flips(4))
    grad_in = ring_sum(last_total(in_flip, right, up_in, c_in, d_in, c_last, d_last))
    grad_out, grad_up = grad_in[:, :width], grad_in[:, width:]

    grad_qkv = swapped(grad_qkv.reshape(ctx_size, -1, 3 * lanes), None)
    grad_qkv = grad_qkv.reshape(ctx_size, -1, 3, lanes).transpose(1, 2, 0, 3)
    grad_qkv = grad_qkv.reshape(-1, 3 * width)
    normed, scale = norm_parts(x.astype(F32))
    grad_tokens = dh + norm_back(du, normed, scale, gain_all[0:1, :])

    own_gains = picked(gains.reshape(ctx_size, -1, kinds), place, 0).astype(F32)
    row_sum = lambda weight, grad: jnp.sum(
        picked(split(weight), place, 0).astype(F32) * grad, axis=1
    )
    gain_one = row_sum(w_qkv, grad_qkv) / own_gains[:, 0]
    gain_three = row_sum(w_up, grad_up) / own_gains[:, 2]
    gain_pair = scattered_gains(after(jnp.concatenate([gain_two, gain_four]), dqkv))
    grad_gains = jnp.stack([gain_one, gain_pair[:, 0], gain_three, gain_pair[:, 1]], axis=1)
    return (
        layer_out.reshape(batch, rows, width),
        grad_tokens.reshape(batch, rows, width),
        grad_qkv,
        grad_out,
        grad_up,
        grad_down,
        grad_gains,
    )


def per_device(*args):
    return staged(*args) if cube() else plain(*args)


def solution(mesh):
    return jax.shard_map(
        per_device,
        mesh=mesh,
        in_specs=(
            P(None, ALL, None),
            P(None, "shard", None),
            P("shard", None),
            P("shard", None),
            P("shard", None),
            P("shard", None),
            P("shard", None),
            P(None, ALL, None),
        ),
        out_specs=(
            P(None, ALL, None),
            P(None, ALL, None),
            P(ALL, None),
            P(ALL, None),
            P(ALL, None),
            P(ALL, None),
            P(ALL, None),
        ),
        check_vma=False,
    )
```

```python
import functools
import math

import jax
import jax.numpy as jnp
from jax import lax
from jax.experimental import pallas as pl
from jax.experimental.pallas import tpu as pltpu
from jax.sharding import PartitionSpec as P

HEADS = 16
HDIM = 64
EPSILON = 1e-05
ROPE_BASE = 10000.0
MASKED = -1e30
ALL = ("shard", "ctx")
BF = jnp.bfloat16
F32 = jnp.float32
VMEM_LIMIT = 56 * 1024 * 1024
GAIN_ROWS = 16


def layer_norm(values, gain):
    center = jnp.mean(values, axis=-1, keepdims=True)
    shifted = values - center
    spread = jnp.mean(shifted * shifted, axis=-1, keepdims=True)
    return shifted * lax.rsqrt(spread + EPSILON) * gain


def gelu_tanh(values):
    return jax.nn.gelu(values, approximate=True)


def dot(left, right):
    return jnp.dot(left, right, preferred_element_type=F32)


def contract_rows(left, right):
    return lax.dot_general(left, right, (((0,), (0,)), ((), ())), preferred_element_type=F32)


def contract_cols(left, right):
    return lax.dot_general(left, right, (((1,), (1,)), ((), ())), preferred_element_type=F32)


def rope_tables(doc_starts, blocks, rows):
    half = HDIM // 2
    lane = jnp.arange(2 * HDIM, dtype=jnp.int32)
    freqs = ROPE_BASE ** (-(lane % half).astype(F32) / half)
    sign = jnp.where(lane % HDIM < half, -1.0, 1.0).astype(F32)
    positions = jnp.arange(blocks * rows, dtype=jnp.int32).reshape(blocks, 1, rows)
    latest = jnp.zeros((blocks, doc_starts.shape[0], rows), jnp.int32)
    for d in range(doc_starts.shape[1]):
        start = doc_starts[None, :, d, None]
        latest = jnp.where(positions >= start, jnp.maximum(latest, start), latest)
    angles = (positions - latest).astype(F32)[..., None] * freqs
    return jnp.cos(angles), jnp.sin(angles) * sign


def turned(values, cos_row, sin_row):
    width = values.shape[1]
    half = HDIM // 2
    if width == HDIM:
        swapped = jnp.concatenate([values[:, half:], values[:, :half]], axis=1)
    else:
        lane = lax.broadcasted_iota(jnp.int32, values.shape, 1)
        swapped = jnp.where(
            lane % HDIM < half, pltpu.roll(values, width - half, 1), pltpu.roll(values, half, 1)
        )
    return values * cos_row[:, :width] + swapped * sin_row[:, :width]


def project_rows(u, weight, cos_row, sin_row, lanes):
    full = dot(u, weight)
    parts = [full[:, slot * lanes : (slot + 1) * lanes] for slot in range(3)]
    query = turned(parts[0], cos_row, sin_row) * HDIM ** (-0.5)
    return query, turned(parts[1], cos_row, sin_row), parts[2]


def norm_parts(values):
    shifted = values - jnp.mean(values, axis=-1, keepdims=True)
    scale = lax.rsqrt(jnp.mean(shifted * shifted, axis=-1, keepdims=True) + EPSILON)
    return shifted * scale, scale


def norm_back(grad, normed, scale, gain):
    scaled = grad * gain
    return scale * (
        scaled
        - jnp.mean(scaled, axis=-1, keepdims=True)
        - normed * jnp.mean(scaled * normed, axis=-1, keepdims=True)
    )


def project_kernel(
    shards, where, a0, a1, b0, b1, cos_ref, sin_ref, *rest
):
    part_refs, (out_ref, u_ref, w_ref, gain_ref) = rest[:shards], rest[shards:]
    _, _, batch, rows, lanes = out_ref.shape
    count = batch * rows
    size = w_ref.shape[0] // shards

    @pl.when(pl.program_id(0) == 0)
    def _():
        for k, part_ref in enumerate(part_refs):
            at = pl.multiple_of(lax.rem(where[0] - k + shards, shards) * size, size)
            w_ref[pl.ds(at, size), :] = part_ref[:size, :]
            gain_ref[:, pl.ds(at, size)] = part_ref[size:, :size].astype(F32)

    gain = gain_ref[0:1, :]
    for side, (a, b) in enumerate(((a0, b0), (a1, b1))):
        core = where[3] ^ side
        x = jnp.concatenate([a[...], b[...]], axis=1).astype(F32)
        u = (norm_parts(x)[0] * gain).astype(BF)
        u_ref[core] = u
        cos_row = cos_ref[core].reshape(count, -1)
        sin_row = sin_ref[core].reshape(count, -1)
        for slot, part in enumerate(project_rows(u, w_ref[...], cos_row, sin_row, lanes)):
            out_ref[core, slot] = part.reshape(batch, rows, lanes).astype(BF)


def project(parts, weight_parts, cos_all, sin_all):
    a, b = parts[0], parts[2]
    count, half = a.shape[2:]
    shards = len(weight_parts)
    size, columns = weight_parts[0].shape
    width = 2 * half
    kinds = size - width // shards
    lanes = columns // 3
    blocks, batch, rows, _ = cos_all.shape
    a_spec = pl.BlockSpec(
        (None, None, count, half), lambda t, w: ((t // 2) ^ w[1], (t % 2) ^ w[2], 0, 0)
    )
    b_spec = pl.BlockSpec(
        (None, None, count, half), lambda t, w: ((t % 2) ^ w[2], (t // 2) ^ w[1], 0, 0)
    )
    table = pl.BlockSpec((2, batch, rows, 2 * HDIM), lambda t, w: (t, 0, 0, 0))
    whole = lambda shape: pl.BlockSpec(shape, lambda t, w: (0, 0))
    return pl.pallas_call(
        functools.partial(project_kernel, shards),
        out_shape=(
            jax.ShapeDtypeStruct((blocks, 3, batch, rows, lanes), BF),
            jax.ShapeDtypeStruct((blocks, count, width), BF),
            jax.ShapeDtypeStruct((width, columns), BF),
            jax.ShapeDtypeStruct((kinds, width), F32),
        ),
        grid_spec=pltpu.PrefetchScalarGridSpec(
            num_scalar_prefetch=1,
            grid=(4,),
            in_specs=[a_spec, a_spec, b_spec, b_spec, table, table]
            + [whole((size, columns))] * shards,
            out_specs=(
                pl.BlockSpec((2, 3, batch, rows, lanes), lambda t, w: (t, 0, 0, 0, 0)),
                pl.BlockSpec((2, count, width), lambda t, w: (t, 0, 0)),
                whole((width, columns)),
                whole((kinds, width)),
            ),
        ),
        compiler_params=pltpu.CompilerParams(vmem_limit_bytes=VMEM_LIMIT),
        name="project",
    )(where(), *parts, cos_all, sin_all, *weight_parts)


def project_plain(u_run, weight, cos_run, sin_run):
    blocks, batch, rows, _ = cos_run.shape
    lanes = weight.shape[1] // 3
    full = dot(u_run.reshape(-1, weight.shape[0]), weight).reshape(blocks, batch, rows, 3, -1, HDIM)
    half = HDIM // 2
    cosine, sine = (t[..., None, half:HDIM] for t in (cos_run, sin_run))

    def turn(values):
        first, second = values[..., :half], values[..., half:]
        return jnp.concatenate(
            [first * cosine - second * sine, second * cosine + first * sine], axis=-1
        )

    parts = [turn(full[..., 0, :, :]) * HDIM ** (-0.5), turn(full[..., 1, :, :]), full[..., 2, :, :]]
    return jnp.stack([p.reshape(blocks, batch, rows, lanes).astype(BF) for p in parts], axis=1)


def starts_row(info_ref, mb, docs, positions):
    latest = jnp.zeros_like(positions)
    for d in range(docs):
        start = info_ref[mb, d]
        latest = jnp.where(positions >= start, jnp.maximum(latest, start), latest)
    return latest


def start_scalar(info_ref, mb, docs, position):
    latest = jnp.int32(0)
    for d in range(docs):
        start = info_ref[mb, d]
        latest = jnp.where(position >= start, jnp.maximum(latest, start), latest)
    return latest


def attend_kernel(docs, heads, mb, info_ref, q_ref, k_ref, v_ref, *rest):
    o_ref, ob_ref, lse_ref = rest[-3:]
    i = pl.program_id(0)
    per, rows, lanes = q_ref.shape
    block = per * rows
    first = info_ref[mb, docs] + i * block
    low = start_scalar(info_ref, mb, docs, first) // block
    diag = first // block
    q_pos = first + lax.broadcasted_iota(jnp.int32, (1, block), 1)
    q_start = starts_row(info_ref, mb, docs, q_pos)
    q_all = q_ref[...].reshape(block, lanes)
    queries = [q_all[:, h * HDIM : (h + 1) * HDIM] for h in range(heads)]

    def visit(step, state):
        j = diag - step
        k_all = k_ref[pl.ds(j * per, per)].reshape(block, lanes)
        v_flip = v_ref[pl.ds(j * per, per)].reshape(block, lanes).astype(F32).T.astype(BF)
        k_pos = j * block + lax.broadcasted_iota(jnp.int32, (block, 1), 0)
        allowed = (k_pos >= q_start) & (k_pos <= q_pos)
        out = []
        for h in range(heads):
            peak, total, acc = state[h]
            scores = contract_cols(k_all[:, h * HDIM : (h + 1) * HDIM], queries[h])
            scores = jnp.where(allowed, scores, MASKED)
            new_peak = jnp.maximum(peak, jnp.max(scores, axis=0, keepdims=True))
            decay = jnp.exp(peak - new_peak)
            weights = jnp.exp(scores - new_peak)
            total = total * decay + jnp.sum(weights, axis=0, keepdims=True)
            acc = acc * decay + dot(v_flip[h * HDIM : (h + 1) * HDIM], weights.astype(BF))
            out.append((new_peak, total, acc))
        return tuple(out)

    start = tuple(
        (
            jnp.full((1, block), MASKED, F32),
            jnp.zeros((1, block), F32),
            jnp.zeros((HDIM, block), F32),
        )
        for _ in range(heads)
    )
    state = lax.fori_loop(0, diag - low + 1, visit, start)
    flipped = jnp.concatenate([acc / total for _, total, acc in state], axis=0)
    attended = flipped.T
    o_ref[...] = attended.reshape(per, rows, lanes)
    ob_ref[...] = attended.astype(BF).reshape(per, rows, lanes)
    lse_ref[...] = jnp.concatenate([peak + jnp.log(total) for peak, total, _ in state], axis=0)


def attend(info, docs, mb, queries, q_slot, keys, k_slot, v_slot, earlier=()):
    group_count, _, batch, rows, lanes = queries.shape
    blocks_all = keys.shape[0]
    heads = lanes // HDIM
    per = math.gcd(group_count, max(1, 256 // rows))
    q_blocks = group_count // per
    spec = pl.BlockSpec((per, None, None, rows, lanes), lambda i, info: (i, q_slot, mb, 0, 0))
    kv_spec = lambda slot: pl.BlockSpec(
        (blocks_all, None, None, rows, lanes), lambda i, info: (0, slot, mb, 0, 0)
    )
    o_spec = pl.BlockSpec((per, None, rows, lanes), lambda i, info: (i, mb, 0, 0))
    return pl.pallas_call(
        functools.partial(attend_kernel, docs, heads, mb),
        out_shape=(
            jax.ShapeDtypeStruct((group_count, batch, rows, lanes), F32),
            jax.ShapeDtypeStruct((group_count, batch, rows, lanes), BF),
            jax.ShapeDtypeStruct((batch, heads, group_count * rows), F32),
        ),
        grid_spec=pltpu.PrefetchScalarGridSpec(
            num_scalar_prefetch=1,
            grid=(q_blocks,),
            in_specs=[spec, kv_spec(k_slot), kv_spec(v_slot)]
            + [pl.BlockSpec(memory_space=pl.ANY)] * len(earlier),
            out_specs=(
                o_spec,
                o_spec,
                pl.BlockSpec((None, heads, per * rows), lambda i, info: (mb, 0, i)),
            ),
        ),
        input_output_aliases={4 + n: n for n in range(len(earlier))},
        compiler_params=pltpu.CompilerParams(vmem_limit_bytes=VMEM_LIMIT),
        name="attend",
    )(info, queries, keys, keys, *earlier)


def attend_back_kernel(
    docs, heads, per, merged, mb, info_ref, q_ref, k_ref, v_ref, do_ref, o_ref, lse_ref, cosq_ref,
    sinq_ref, cosk_ref, sink_ref, *rest
):
    j = pl.program_id(0)
    out_ref, dq_acc, delta_ref = rest[-3:]
    dq_ref = None if merged else rest[-4]
    group_count, rows, lanes = q_ref.shape
    block = per * rows
    q_blocks = group_count // per
    base = info_ref[mb, docs] // block

    def lanes_of(i):
        return pl.ds(pl.multiple_of(i * block, block), block)

    @pl.when(j == 0)
    def _():
        dq_acc[...] = jnp.zeros_like(dq_acc)

        def fill(i, carry):
            here = pl.ds(i * per, per)
            prod = do_ref[here].reshape(block, lanes).astype(F32) * o_ref[here].reshape(
                block, lanes
            )
            flipped = prod.T
            delta_ref[:, lanes_of(i)] = jnp.concatenate(
                [
                    jnp.sum(flipped[h * HDIM : (h + 1) * HDIM], axis=0, keepdims=True)
                    for h in range(heads)
                ],
                axis=0,
            )
            return carry

        lax.fori_loop(0, q_blocks, fill, 0)

    k_first = j * block
    last = k_first + block - 1
    end = base * block + group_count * rows
    for d in range(docs):
        start = info_ref[mb, d]
        end = jnp.where(start > last, jnp.minimum(end, start), end)
    i_low = jnp.maximum(j - base, 0)
    i_high = jnp.maximum((end - base * block + block - 1) // block, i_low)
    k_pos = k_first + lax.broadcasted_iota(jnp.int32, (block, 1), 0)
    k_all = k_ref[...].reshape(block, lanes)
    v_all = v_ref[...].reshape(block, lanes)
    k_flip = k_all.astype(F32).T.astype(BF)
    heads_of = lambda a: [a[:, h * HDIM : (h + 1) * HDIM] for h in range(heads)]
    k_heads, v_heads = heads_of(k_all), heads_of(v_all)

    def visit(i, state):
        here = pl.ds(i * per, per)
        q_heads = heads_of(q_ref[here].reshape(block, lanes))
        do_heads = heads_of(do_ref[here].reshape(block, lanes))
        q_pos = (base + i) * block + lax.broadcasted_iota(jnp.int32, (1, block), 1)
        q_start = starts_row(info_ref, mb, docs, q_pos)
        allowed = (k_pos >= q_start) & (k_pos <= q_pos)
        lse = lse_ref[:, lanes_of(i)]
        delta = delta_ref[:, lanes_of(i)]
        out = []
        for h in range(heads):
            dk, dv = state[h]
            scores = contract_cols(k_heads[h], q_heads[h])
            weights = jnp.exp(jnp.where(allowed, scores - lse[h : h + 1], MASKED))
            grad_weights = contract_cols(v_heads[h], do_heads[h])
            grad_scores = (weights * (grad_weights - delta[h : h + 1])).astype(BF)
            dv = dv + dot(weights.astype(BF), do_heads[h])
            dk = dk + dot(grad_scores, q_heads[h])
            at = slice(h * HDIM, (h + 1) * HDIM)
            dq_acc[at, lanes_of(i)] += dot(k_flip[at], grad_scores)
            out.append((dk, dv))
        return tuple(out)

    zero = jnp.zeros((block, HDIM), F32)
    state = lax.fori_loop(i_low, i_high, visit, tuple((zero, zero) for _ in range(heads)))
    dk = jnp.concatenate([dk for dk, _ in state], axis=1) if heads > 1 else state[0][0]
    dv = jnp.concatenate([dv for _, dv in state], axis=1) if heads > 1 else state[0][1]
    dk = turned(dk, cosk_ref[...].reshape(block, -1), -sink_ref[...].reshape(block, -1))
    there = pl.ds(j * per, per)
    first = lanes if merged else 0
    out_ref[there, :, first : first + lanes] = dk.reshape(per, rows, lanes).astype(out_ref.dtype)
    out_ref[there, :, first + lanes : first + 2 * lanes] = dv.reshape(per, rows, lanes).astype(
        out_ref.dtype
    )

    @pl.when(j == pl.num_programs(0) - 1)
    def _():
        def finish(i, carry):
            dq = dq_acc[:, lanes_of(i)].T
            at = pl.ds(i * per, per)
            cos_row = cosq_ref[at].reshape(block, -1)
            sin_row = sinq_ref[at].reshape(block, -1)
            dq = turned(dq, cos_row, -sin_row) * HDIM ** (-0.5)
            dq = dq.reshape(per, rows, lanes).astype(BF)
            if merged:
                out_ref[at, :, :lanes] = dq
            else:
                dq_ref[at] = dq
            return carry

        lax.fori_loop(0, q_blocks, finish, 0)


def attend_back(info, docs, mb, queries, q_slot, keys, k_slot, v_slot, grad, attended, lse,
                cos_all, sin_all, cos_here, sin_here, earlier=()):
    group_count, _, batch, rows, lanes = queries.shape
    blocks_all = keys.shape[0]
    merged = blocks_all == group_count
    heads = lanes // HDIM
    per = math.gcd(group_count, max(1, 256 // rows))
    length = group_count * rows
    full = pl.BlockSpec(
        (group_count, None, None, rows, lanes), lambda j, info: (0, q_slot, mb, 0, 0)
    )
    part = lambda slot: pl.BlockSpec(
        (per, None, None, rows, lanes), lambda j, info: (j, slot, mb, 0, 0)
    )
    rows_of_mb = lambda count, width: pl.BlockSpec(
        (count, None, rows, width), lambda j, info: (0, mb, 0, 0)
    )
    table_k = pl.BlockSpec((per, None, rows, 2 * HDIM), lambda j, info: (j, mb, 0, 0))
    if merged:
        out_shape = [jax.ShapeDtypeStruct((group_count, batch, rows, 3 * lanes), BF)]
        out_specs = [rows_of_mb(group_count, 3 * lanes)]
    else:
        out_shape = [
            jax.ShapeDtypeStruct((group_count, batch, rows, lanes), BF),
            jax.ShapeDtypeStruct((blocks_all, batch, rows, 2 * lanes), F32),
        ]
        out_specs = [rows_of_mb(group_count, lanes), rows_of_mb(blocks_all, 2 * lanes)]
    table_q = rows_of_mb(group_count, 2 * HDIM)
    return pl.pallas_call(
        functools.partial(attend_back_kernel, docs, heads, per, merged, mb),
        out_shape=out_shape,
        grid_spec=pltpu.PrefetchScalarGridSpec(
            num_scalar_prefetch=1,
            grid=(blocks_all // per,),
            in_specs=[
                full, part(k_slot), part(v_slot), rows_of_mb(group_count, lanes),
                rows_of_mb(group_count, lanes),
                pl.BlockSpec((None, heads, length), lambda j, info: (mb, 0, 0)),
                table_q, table_q, table_k, table_k,
            ]
            + [pl.BlockSpec(memory_space=pl.ANY)] * len(earlier),
            out_specs=out_specs,
            scratch_shapes=[pltpu.VMEM((lanes, length), F32), pltpu.VMEM((heads, length), F32)],
        ),
        input_output_aliases={11 + n: n for n in range(len(earlier))},
        compiler_params=pltpu.CompilerParams(vmem_limit_bytes=VMEM_LIMIT),
        name="attend_back",
    )(info, queries, keys, keys, grad, attended, lse, cos_here, sin_here, cos_all, sin_all,
      *earlier)


def flips(mask):
    count = lax.axis_size("shard") * lax.axis_size("ctx")
    return [(i, i ^ mask) for i in range(count)]


def turns(by):
    shards, places = lax.axis_size("shard"), lax.axis_size("ctx")
    return [
        (a * places + b, ((a + by) % shards) * places + b)
        for a in range(shards)
        for b in range(places)
    ]


def sent(values, pairs):
    return lax.ppermute(values, ALL, pairs)


def picked(values, index, axis):
    return lax.dynamic_index_in_dim(values, index, axis, keepdims=False)


def cube():
    return lax.axis_size("ctx") == 8


def bits():
    place = lax.axis_index("ctx")
    return lax.axis_index("shard"), place // 4, place // 2 % 2, place % 2


def where():
    return jnp.stack(bits()).astype(jnp.int32)


def spread(values, early):
    half = values.shape[1] // 2
    a, b = values[:, :half], values[:, half:]
    a_in, b_in = sent(a, flips(2)), sent(b, flips(4))
    a, b = jnp.stack([a, after(a_in, *early)]), jnp.stack([b, after(b_in, *early)])
    a = jnp.stack([a, sent(a, flips(4))])
    b = jnp.stack([b, sent(b, flips(2))])
    return a, sent(a, flips(1)), b, sent(b, flips(1))


def ring_parts(values):
    shards = lax.axis_size("shard")
    z = lax.axis_index("shard")
    return [picked(values, lax.rem(z + k, shards), 0) for k in range(shards)]


def ring_sent(parts):
    return [sent(part, turns(k)) for k, part in enumerate(parts) if k]


def ring_total(own, received):
    total = own.astype(F32)
    for part in received:
        total = total + part.astype(F32)
    return total


def after(values, *earlier):
    return lax.optimization_barrier((values,) + earlier)[0]


def far_rows(piece, *earlier):
    shards = lax.axis_size("shard")
    every = after(lax.all_gather(piece, "shard", axis=0), *earlier)
    twice = jnp.concatenate([every[::-1], every[::-1]])
    first = shards - lax.axis_index("shard")
    return lax.dynamic_slice_in_dim(twice, first, shards - 1, 0)


def copies_in(where, owns, parts, out_ref, sem):
    z, y, x, c = (where[i] for i in range(4))
    shards = out_ref.shape[0]
    half = parts[0].shape[-1]
    groups = [[] for _ in range(shards)]

    def add(k, source, target):
        at = sum(len(group) for group in groups)
        groups[k].append(pltpu.make_async_copy(source, target, sem.at[at]))

    first = 0
    for own in owns:
        add(0, own, out_ref.at[z, :, :, pl.ds(first, own.shape[-1])])
        first += own.shape[-1]
    for k in range(1, shards):
        source = lax.rem(z - k + shards, shards)
        for side in range(2):
            a, b = parts[side], parts[2 + side]
            core = c ^ side
            for p in range(2):
                for q in range(2):
                    at_a = ((y ^ p) * 2 + (x ^ q)) * 2 + core
                    at_b = ((y ^ q) * 2 + (x ^ p)) * 2 + core
                    add(k, a.at[p, q, k - 1], out_ref.at[source, at_a, :, pl.ds(0, half)])
                    add(k, b.at[p, q, k - 1], out_ref.at[source, at_b, :, pl.ds(half, half)])
    for group in groups:
        for copy in group:
            copy.start()
    return groups


def arrived(groups, where):
    shards = len(groups)
    for k, group in enumerate(groups):
        for copy in group:
            copy.wait()
        yield lax.rem(where[0] - k + shards, shards)


def copy_count(shards, owns):
    return owns + 16 * (shards - 1)


def rows_of(w, first, last):
    part = w[:, :, :, first:last]
    return part.reshape(-1, last - first)


def chunk_of(w, z, first, last):
    part = w[z, :, :, first:last]
    return part.reshape(-1, last - first)


def block_at(z, size):
    return pl.ds(pl.multiple_of(z * size, size), size)


def flip_pieces(values, size, out_ref, first):
    tokens, rows = values.shape
    step = max(size, 128)
    for start in range(0, rows, step):
        flip = values[:, start : start + step].astype(F32).T.astype(BF)
        for low in range(0, step, size):
            piece = (start + low) // size
            z, y, x, c = piece // 8, piece // 4 % 2, piece // 2 % 2, piece % 2
            out_ref[c, y, x, z, :, first : first + tokens] = flip[low : low + size]


def mlp_in_kernel(
    where, ob_ref, x_ref, gain_ref, own_out, own_up, a0, a1, b0, b1,
    a_ref, h_ref, g_ref, slope_ref, in_flip, g_flip, w, obl, sem
):
    copies = copies_in(where, (own_out, own_up), (a0, a1, b0, b1), w, sem)
    groups, batch, rows, lanes = ob_ref.shape
    shards = w.shape[0]
    width = x_ref.shape[1]
    count = batch * rows
    size = width // shards
    for mb in range(batch):
        for g in range(groups):
            obl[mb * rows : (mb + 1) * rows, g * lanes : (g + 1) * lanes] = ob_ref[g, mb]
    flip_pieces(obl[...], size // 8, in_flip, count)
    a = None
    for z in arrived(copies, where):
        part = dot(obl[:, block_at(z, size)], chunk_of(w, z, 0, width))
        a = part if a is None else a + part
    a_ref[...] = a
    h = x_ref[...].astype(F32) + norm_parts(a)[0] * gain_ref[1:2, :]
    h_ref[...] = h
    u2 = (norm_parts(h)[0] * gain_ref[2:3, :]).astype(BF)
    flip_pieces(u2, size // 8, in_flip, 0)
    hidden = g_ref.shape[1]
    step = 512
    root = math.sqrt(2.0 / math.pi)
    for first in range(0, hidden, step):
        f = dot(u2, rows_of(w, width + first, width + first + step))
        square = f * f
        bent = jnp.tanh(root * (f + 0.044715 * (square * f)))
        half = 0.5 * (1.0 + bent)
        at = slice(first, first + step)
        g_ref[:, at] = (f * half).astype(BF)
        slope = half + 0.5 * f * (1.0 - bent * bent) * (root * (1.0 + 3 * 0.044715 * square))
        slope_ref[:, at] = slope.astype(BF)
    flip_pieces(g_ref[...], hidden // (8 * shards), g_flip, 0)


def mlp_in(ob, x, gain_all, w_out, w_up, parts):
    shards = lax.axis_size("shard")
    count, width = x.shape
    hidden = w_up.shape[-1]
    pieces, rows = w_out.shape[:2]
    anywhere = pl.BlockSpec(memory_space=pl.ANY)
    local = pl.BlockSpec(memory_space=pltpu.VMEM)
    shape = jax.ShapeDtypeStruct
    return pl.pallas_call(
        mlp_in_kernel,
        out_shape=(
            shape((count, width), F32),
            shape((count, width), F32),
            shape((count, hidden), BF),
            shape((count, hidden), BF),
            shape((2, 2, 2, shards, width // (8 * shards), 2 * count), BF),
            shape((2, 2, 2, shards, hidden // (8 * shards), count), BF),
        ),
        grid_spec=pltpu.PrefetchScalarGridSpec(
            num_scalar_prefetch=1,
            grid=(),
            in_specs=[local] * 3 + [anywhere] * 6,
            out_specs=[local] * 6,
            scratch_shapes=[
                pltpu.VMEM((shards, pieces, rows, width + hidden), BF),
                pltpu.VMEM((count, width), BF),
                pltpu.SemaphoreType.DMA((copy_count(shards, 2),)),
            ],
        ),
        compiler_params=pltpu.CompilerParams(vmem_limit_bytes=VMEM_LIMIT),
        name="mlp_in",
    )(where(), ob, x, gain_all, w_out, w_up, *parts)


def mlp_out_kernel(
    where, g_ref, slope_ref, h_ref, cot_ref, gain_ref, own, a0, a1, b0, b1,
    out_ref, dmb_ref, dfb_ref, gg_ref, w, sem
):
    copies = copies_in(where, (own,), (a0, a1, b0, b1), w, sem)
    shards = w.shape[0]
    width = h_ref.shape[1]
    size = g_ref.shape[1] // shards
    m = None
    for z in arrived(copies, where):
        part = dot(g_ref[:, block_at(z, size)], chunk_of(w, z, 0, width))
        m = part if m is None else m + part
    gain = gain_ref[3:4, :]
    normed, scale = norm_parts(m)
    out_ref[...] = (h_ref[...] + normed * gain).astype(BF)
    dy = cot_ref[...].astype(F32)
    gg_ref[...] = jnp.sum(dy * normed, axis=0, keepdims=True)
    dmb = norm_back(dy, normed, scale, gain).astype(BF)
    dmb_ref[...] = dmb
    for z in range(shards):
        at = slice(z * size, (z + 1) * size)
        dg = contract_cols(dmb, chunk_of(w, z, 0, width))
        dfb_ref[:, at] = (dg * slope_ref[:, at].astype(F32)).astype(BF)


def mlp_out(g, slope, h, cot, gain_all, w_down, parts):
    shards = lax.axis_size("shard")
    count, width = h.shape
    hidden = g.shape[1]
    pieces, rows = w_down.shape[:2]
    anywhere = pl.BlockSpec(memory_space=pl.ANY)
    local = pl.BlockSpec(memory_space=pltpu.VMEM)
    shape = jax.ShapeDtypeStruct
    return pl.pallas_call(
        mlp_out_kernel,
        out_shape=(
            shape((count, width), BF),
            shape((count, width), BF),
            shape((count, hidden), BF),
            shape((1, width), F32),
        ),
        grid_spec=pltpu.PrefetchScalarGridSpec(
            num_scalar_prefetch=1,
            grid=(),
            in_specs=[local] * 5 + [anywhere] * 5,
            out_specs=[local] * 4,
            scratch_shapes=[
                pltpu.VMEM((shards, pieces, rows, width), BF),
                pltpu.SemaphoreType.DMA((copy_count(shards, 1),)),
            ],
        ),
        compiler_params=pltpu.CompilerParams(vmem_limit_bytes=VMEM_LIMIT),
        name="mlp_out",
    )(where(), g, slope, h, cot, gain_all, w_down, *parts)


def mlp_back_kernel(
    where, dfb_ref, h_ref, a_ref, cot_ref, gain_ref, gain_four_ref, own_out, own_up, a0, a1, b0, b1,
    dh_ref, right_a, right_b, dob_ref, w, du2, sem
):
    copies = copies_in(where, (own_out, own_up), (a0, a1, b0, b1), w, sem)
    shards = w.shape[0]
    count, width = h_ref.shape
    size = width // shards
    groups, batch, rows, lanes = dob_ref.shape
    rows -= GAIN_ROWS
    last = w.shape[-1]
    middle = last // 2
    right_a[:count, :width] = jnp.zeros((count, width), BF)
    right_a[count:, width:] = jnp.zeros((count, middle - width), BF)
    right_a[:count, width:] = dfb_ref[:, : middle - width]
    right_b[count:, :] = jnp.zeros((count, middle), BF)
    right_b[:count, :] = dfb_ref[:, middle - width :]
    for z in arrived(copies, where):
        du2[:, block_at(z, size)] = contract_cols(dfb_ref[...], chunk_of(w, z, width, last))
    normed, scale = norm_parts(h_ref[...])
    dh = cot_ref[...].astype(F32) + norm_back(du2[...], normed, scale, gain_ref[2:3, :])
    dh_ref[...] = dh
    normed, scale = norm_parts(a_ref[...])
    gains = (jnp.sum(dh * normed, axis=0, keepdims=True), gain_four_ref[...])
    step = lanes // shards
    blank = jnp.zeros((GAIN_ROWS - len(gains), lanes), F32)
    for g in range(groups):
        lines = [
            jnp.concatenate(
                [line[:, z * size + g * step : z * size + (g + 1) * step] for z in range(shards)],
                axis=1,
            )
            for line in gains
        ]
        block = jnp.concatenate(lines + [blank], axis=0).astype(BF)
        for mb in range(batch):
            dob_ref[g, mb, rows:, :] = block
    dab = norm_back(dh, normed, scale, gain_ref[1:2, :]).astype(BF)
    right_a[count:, :width] = dab
    for z in range(shards):
        dob = contract_cols(dab, chunk_of(w, z, 0, width)).astype(BF)
        for part in range(size // lanes):
            for mb in range(batch):
                dob_ref[z * (size // lanes) + part, mb, :rows] = dob[
                    mb * rows : (mb + 1) * rows, part * lanes : (part + 1) * lanes
                ]


def mlp_back(dfb, h, a, cot, gain_all, gain_four, w_out, w_up, parts, groups, batch):
    shards = lax.axis_size("shard")
    count, width = h.shape
    hidden = dfb.shape[1]
    pieces, rows = w_out.shape[:2]
    anywhere = pl.BlockSpec(memory_space=pl.ANY)
    local = pl.BlockSpec(memory_space=pltpu.VMEM)
    shape = jax.ShapeDtypeStruct
    return pl.pallas_call(
        mlp_back_kernel,
        out_shape=(
            shape((count, width), F32),
            shape((2 * count, (width + hidden) // 2), BF),
            shape((2 * count, (width + hidden) // 2), BF),
            shape((groups, batch, count // batch + GAIN_ROWS, width // groups), BF),
        ),
        grid_spec=pltpu.PrefetchScalarGridSpec(
            num_scalar_prefetch=1,
            grid=(),
            in_specs=[local] * 6 + [anywhere] * 6,
            out_specs=[local] * 4,
            scratch_shapes=[
                pltpu.VMEM((shards, pieces, rows, width + hidden), BF),
                pltpu.VMEM((count, width), F32),
                pltpu.SemaphoreType.DMA((copy_count(shards, 2),)),
            ],
        ),
        compiler_params=pltpu.CompilerParams(vmem_limit_bytes=VMEM_LIMIT),
        name="mlp_back",
    )(where(), dfb, h, a, cot, gain_all, gain_four, w_out, w_up, *parts)


def tail_kernel(where, dqkv_ref, u_ref, w_ref, gain_ref, keep_ref, away_ref, grad_ref):
    core = where[3]
    shards = grad_ref.shape[0]
    size = w_ref.shape[0] // shards
    step = gain_ref.shape[1] // shards
    total = None
    for pair in range(dqkv_ref.shape[0] // 2):
        for side, out_ref in enumerate((keep_ref, away_ref)):
            block = 2 * pair + (core ^ side)
            dqkv = dqkv_ref[block]
            out_ref[pair] = contract_cols(dqkv, w_ref[...]).astype(BF)
            part = dot(dqkv.astype(F32).T.astype(BF), u_ref[block])
            total = part if total is None else total + part
    blank = jnp.zeros((gain_ref.shape[0], grad_ref.shape[2] - step), F32)
    for z in range(shards):
        grad_ref[z, :size] = total[:, z * size : (z + 1) * size].T.astype(BF)
        gains = gain_ref[:, z * step : (z + 1) * step]
        grad_ref[z, size:] = jnp.concatenate([gains, blank], axis=1).astype(BF)


def tail_products(dqkv, u_run, w_heads, gain_part):
    blocks, count, columns = dqkv.shape
    width = w_heads.shape[0]
    shards = lax.axis_size("shard")
    local = pl.BlockSpec(memory_space=pltpu.VMEM)
    rows = jax.ShapeDtypeStruct((blocks // 2, count, width), BF)
    return pl.pallas_call(
        tail_kernel,
        out_shape=(
            rows,
            rows,
            jax.ShapeDtypeStruct((shards, width // shards + gain_part.shape[0], columns), BF),
        ),
        grid_spec=pltpu.PrefetchScalarGridSpec(
            num_scalar_prefetch=1, grid=(), in_specs=[local] * 4, out_specs=[local] * 3
        ),
        compiler_params=pltpu.CompilerParams(vmem_limit_bytes=VMEM_LIMIT),
        name="tail_products",
    )(where(), dqkv, u_run, w_heads, gain_part)


def finish_kernel(keep_a, keep_b, got_a, got_b, x_ref, dh_ref, gain_ref, out_ref):
    parts = ((keep_a, got_a), (keep_b, got_b))
    du = jnp.concatenate([k[...].astype(F32) + g[...].astype(F32) for k, g in parts], axis=1)
    normed, scale = norm_parts(x_ref[...].astype(F32))
    out_ref[...] = dh_ref[...] + norm_back(du, normed, scale, gain_ref[0:1, :])


def finish_tokens(kept, got, x, dh, gain_all):
    local = pl.BlockSpec(memory_space=pltpu.VMEM)
    return pl.pallas_call(
        finish_kernel,
        out_shape=jax.ShapeDtypeStruct(x.shape, F32),
        in_specs=[local] * 7,
        out_specs=local,
        compiler_params=pltpu.CompilerParams(vmem_limit_bytes=VMEM_LIMIT),
        name="finish_tokens",
    )(*kept, *got, x, dh, gain_all)


def product(left, right, *addends):
    total = dot(left.reshape(-1, left.shape[-1]), right)
    total = total.reshape(*left.shape[:-1], right.shape[1])
    for addend in addends:
        total = total + addend.astype(F32)
    return total.astype(BF)


def halves(values):
    half = values.shape[-1] // 2
    return values[..., :half], values[..., half:]


def at(values, y, x):
    return picked(picked(values, y, 0), x, 0)


def first_away(left, rights):
    left = picked(left, 1 - bits()[3], 0)
    return [product(left, right) for right in rights]


def second_away(left, rights, core_in):
    _, y, x, c = bits()
    left = picked(left, c, 0)
    return (
        product(picked(left, 1 - y, 0), rights[0], picked(core_in[0], 1 - y, 0)),
        product(picked(left, 1 - x, 1), rights[1], picked(core_in[1], 1 - x, 1)),
    )


def third_away(left, rights, core_in, first_in):
    _, y, x, c = bits()
    left = picked(left, c, 0)
    return (
        product(
            at(left, y, 1 - x), rights[0], at(core_in[0], y, 1 - x), picked(first_in[0], 1 - x, 0)
        ),
        product(
            at(left, 1 - y, x), rights[1], at(core_in[1], 1 - y, x), picked(first_in[1], 1 - y, 0)
        ),
    )


def last_total(left, rights, core_in, first_in, second_in):
    _, y, x, c = bits()
    left = at(picked(left, c, 0), y, x)
    own = (x, y)
    parts = [
        product(left, rights[n], at(core_in[n], y, x), picked(first_in[n], own[n], 0), second_in[n])
        for n in range(2)
    ]
    return jnp.concatenate(parts, axis=-1)


def pair_sent(parts, first, second):
    return sent(parts[0], flips(first)), sent(parts[1], flips(second))


def pair_after(parts, *earlier):
    return tuple(after(part, *earlier) for part in parts)


def summed(left, right):
    return (left.astype(F32) + right.astype(F32)).astype(BF)


def gathered(weight):
    size = weight.shape[0] // lax.axis_size("ctx")
    piece = lax.dynamic_slice_in_dim(weight, lax.axis_index("ctx") * size, size, 0)
    return lax.all_gather(piece, ALL, axis=0, tiled=True)


def scattered(left, right):
    total = contract_rows(left, right).astype(BF)
    return lax.psum_scatter(total, ALL, scatter_dimension=0, tiled=True).astype(F32)


def scattered_gains(grads):
    count = lax.axis_size("shard") * lax.axis_size("ctx")
    kinds = grads.shape[0]
    parts = grads.reshape(kinds, count, -1).transpose(1, 0, 2)
    parts = lax.all_to_all(parts, ALL, split_axis=0, concat_axis=0, tiled=True)
    return jnp.sum(parts, axis=0).T


def swapped(values, groups):
    return lax.all_to_all(
        values, "ctx", split_axis=0, concat_axis=0, tiled=True, axis_index_groups=groups
    )


def plain(tokens, doc_starts, w_qkv, w_out, w_up, w_down, gains, cotangent):
    ctx_size = lax.axis_size("ctx")
    place = lax.axis_index("ctx")
    batch, rows, width = tokens.shape
    count = batch * rows
    docs = doc_starts.shape[2]
    group_count = math.gcd(HEADS, ctx_size)
    runs = ctx_size // group_count
    if runs == 1:
        near = far = None
    else:
        near = [[r * group_count + g for g in range(group_count)] for r in range(runs)]
        far = [[r * group_count + g for r in range(runs)] for g in range(group_count)]
    lanes = width // group_count

    gain_all = lax.all_gather(gains, "shard", axis=0, tiled=True).T.astype(F32)
    columns = picked(w_qkv.reshape(-1, 3, group_count, lanes), lax.rem(place, group_count), 2)
    w_heads = lax.all_gather(columns.reshape(-1, 3 * lanes), "shard", axis=0, tiled=True)
    full_out, full_up, full_down = gathered(w_out), gathered(w_up), gathered(w_down)

    starts = doc_starts[:, 0, :]
    cos_all, sin_all = rope_tables(starts, ctx_size, rows)
    run_first = (place // group_count) * group_count
    info = jnp.concatenate(
        [starts, jnp.broadcast_to(run_first * rows, (batch, 1)).astype(jnp.int32)], axis=1
    )

    x = tokens.reshape(count, width).astype(F32)
    out_grad = cotangent.reshape(count, width).astype(F32)
    normed, norm_one_back = jax.vjp(layer_norm, x, gain_all[0])
    u = normed.astype(BF)
    cos_here, sin_here = (
        lax.dynamic_slice_in_dim(t, run_first, group_count, 0) for t in (cos_all, sin_all)
    )
    u_run = lax.all_gather(u, "ctx", axis=0, axis_index_groups=near)
    qkv = project_plain(u_run, w_heads, cos_here, sin_here)
    if runs == 1:
        keys, k_slot = qkv, 1
    else:
        keys, k_slot = (
            lax.all_gather(qkv[:, 1:], "ctx", axis=0, tiled=True, axis_index_groups=far),
            0,
        )
    held = ()
    for mb in range(batch):
        held = attend(info, docs, mb, qkv, 0, keys, k_slot, k_slot + 1, held)
    attended, attended_low, lse = held
    ob = swapped(attended_low, near).transpose(1, 2, 0, 3).reshape(count, width)
    attn_proj = dot(ob, full_out)
    attn_branch, norm_two_back = jax.vjp(layer_norm, attn_proj, gain_all[1])
    hidden = x + attn_branch
    normed_two, norm_three_back = jax.vjp(layer_norm, hidden, gain_all[2])
    u2 = normed_two.astype(BF)
    up_proj = dot(u2, full_up)
    activated, gelu_back = jax.vjp(gelu_tanh, up_proj)
    g = activated.astype(BF)
    down_proj = dot(g, full_down)
    mlp_branch, norm_four_back = jax.vjp(layer_norm, down_proj, gain_all[3])
    layer_out = (hidden + mlp_branch).astype(BF)

    down_grad, gain_four = norm_four_back(out_grad)
    dmb = down_grad.astype(BF)
    grad_down = scattered(g, dmb)
    (up_grad,) = gelu_back(contract_cols(dmb, full_down))
    dfb = up_grad.astype(BF)
    grad_up = scattered(u2, dfb)
    hidden_add, gain_three = norm_three_back(contract_cols(dfb, full_up))
    dh = out_grad + hidden_add
    attn_grad, gain_two = norm_two_back(dh)
    dab = attn_grad.astype(BF)
    grad_out = scattered(ob, dab)
    dob = contract_cols(dab, full_out).astype(BF)
    dob = swapped(dob.reshape(batch, rows, group_count, lanes).transpose(2, 0, 1, 3), near)
    back = ()
    for mb in range(batch):
        back = attend_back(
            info, docs, mb, qkv, 0, keys, k_slot, k_slot + 1, dob, attended, lse, cos_all, sin_all,
            cos_here, sin_here, back,
        )
    if runs == 1:
        dqkv = back[0]
    else:
        dkv = lax.psum_scatter(
            back[1], "ctx", scatter_dimension=0, tiled=True, axis_index_groups=far
        )
        dqkv = jnp.concatenate([back[0], dkv.astype(BF)], axis=-1)
    dqkv = dqkv.reshape(group_count * count, 3 * lanes)
    du = contract_cols(dqkv, w_heads)
    qkv_part = contract_rows(u_run.reshape(group_count * count, width), dqkv)
    du = lax.psum_scatter(du, "ctx", scatter_dimension=0, tiled=True, axis_index_groups=near)
    own = jnp.zeros((width, 3, group_count, lanes), F32)
    own = lax.dynamic_update_slice_in_dim(
        own, qkv_part.reshape(width, 3, 1, lanes), lax.rem(place, group_count), 2
    )
    grad_qkv = lax.psum_scatter(
        own.reshape(width, 3 * width), ALL, scatter_dimension=0, tiled=True
    )
    input_add, gain_one = norm_one_back(du)
    grad_tokens = dh + input_add
    grad_gains = scattered_gains(jnp.stack([gain_one, gain_two, gain_three, gain_four]))
    return (
        layer_out.reshape(batch, rows, width),
        grad_tokens.reshape(batch, rows, width),
        grad_qkv,
        grad_out,
        grad_up,
        grad_down,
        grad_gains,
    )


def staged(tokens, doc_starts, w_qkv, w_out, w_up, w_down, gains, cotangent):
    ctx_size, shards = lax.axis_size("ctx"), lax.axis_size("shard")
    place = lax.axis_index("ctx")
    batch, rows, width = tokens.shape
    count = batch * rows
    docs = doc_starts.shape[2]
    lanes = width // ctx_size
    kinds = gains.shape[1]
    x = tokens.reshape(count, width)
    cot = cotangent.reshape(count, width)
    split = lambda w: w.reshape(ctx_size, -1, w.shape[1])
    own_out, own_up, own_down = split(w_out), split(w_up), split(w_down)

    starts = doc_starts[:, 0, :]
    cos_all, sin_all = rope_tables(starts, ctx_size, rows)
    columns = picked(w_qkv.reshape(-1, 3, ctx_size, lanes), place, 2).reshape(-1, 3 * lanes)
    gain_rows = jnp.pad(gains.T, ((0, 8 - kinds), (0, 3 * lanes - gains.shape[0])))
    piece = jnp.concatenate([columns, gain_rows])
    head_parts = [piece] + [sent(piece, turns(k)) for k in range(1, shards)]
    x_parts = spread(x, (cos_all, sin_all, *head_parts[1:]))

    piece = jnp.concatenate([picked(own_out, place, 0), picked(own_up, place, 0)], axis=1)
    piece = after(piece, *head_parts)
    piece_out = picked(own_down, place, 0)

    info = jnp.concatenate([starts, jnp.zeros((batch, 1), jnp.int32)], axis=1)
    qkv, u_run, w_heads, gain_all = project(x_parts, head_parts, cos_all, sin_all)

    far_in = far_rows(piece, qkv)
    half = far_in.shape[2] // 2
    a, b = far_in[:, :, :half], far_in[:, :, half:]
    a_in, b_in = sent(a, flips(2)), sent(b, flips(4))
    held = ()
    for mb in range(batch):
        held = attend(after(info, far_in, *held), docs, mb, qkv, 0, qkv, 1, 2, held)
        if mb == 0:
            a, b = jnp.stack([a, after(a_in, held[2])]), jnp.stack([b, after(b_in, held[2])])
            info = after(info, a, b)
    attended, attended_low, lse = held
    a_in, b_in = sent(a, flips(4)), sent(b, flips(2))
    ob = swapped(attended_low, None)
    a, b = jnp.stack([a, after(a_in, lse)]), jnp.stack([b, after(b_in, lse)])
    in_parts = (a, sent(a, flips(1)), b, sent(b, flips(1)))
    far_out = far_rows(piece_out, a, b)
    half = far_out.shape[2] // 2
    c, d = far_out[:, :, :half], far_out[:, :, half:]
    c_in, d_in = sent(c, flips(2)), sent(d, flips(4))
    c, d = jnp.stack([c, after(c_in, ob)]), jnp.stack([d, after(d_in, ob)])
    c_in, d_in = sent(c, flips(4)), sent(d, flips(2))

    attn, h, g, slope, in_flip, g_flip = mlp_in(
        after(ob, c, d), x, gain_all, own_out, own_up, in_parts
    )
    c, d = jnp.stack([c, after(c_in, h)]), jnp.stack([d, after(d_in, h)])
    out_parts = (c, sent(c, flips(1)), d, sent(d, flips(1)))
    layer_out, dmb, dfb, gain_four = mlp_out(g, slope, h, cot, gain_all, own_down, out_parts)

    dmbs = halves(dmb)
    d_out = first_away(g_flip, dmbs)
    d_core = pair_sent(d_out, 1, 1)
    dh, right_a, right_b, dob = mlp_back(
        after(dfb, *d_out), h, attn, cot, gain_all, gain_four, own_out, own_up, in_parts, ctx_size, batch
    )
    rights = (right_a, right_b)
    d_out = second_away(g_flip, dmbs, pair_after(d_core, dob))
    d_first = pair_sent(d_out, 4, 2)
    dob = swapped(dob, None)
    gain_part = jnp.sum(dob[:, 0, rows : rows + 8, :].astype(F32), axis=0)
    u_out = first_away(in_flip, pair_after(rights, *d_out))
    u_core = pair_sent(u_out, 1, 1)
    back = ()
    for mb in range(batch):
        back = attend_back(
            after(info, *u_out, *back), docs, mb, qkv, 0, qkv, 1, 2, dob, attended, lse, cos_all,
            sin_all, cos_all, sin_all, back,
        )
        if mb == 0:
            u_out = second_away(in_flip, rights, pair_after(u_core, *back))
            u_first = pair_sent(u_out, 4, 2)
            d_out = third_away(g_flip, dmbs, d_core, pair_after(d_first, *u_out))
            d_second = pair_sent(d_out, 2, 4)
            info = after(info, *d_out)
    dqkv = back[0].reshape(ctx_size, count, 3 * lanes)
    du_keep, du_away, qkv_part = tail_products(dqkv, u_run, w_heads, gain_part)
    u_out = third_away(in_flip, rights, u_core, pair_after(u_first, qkv_part))
    u_second = pair_sent(u_out, 2, 4)
    total = last_total(g_flip, dmbs, d_core, d_first, pair_after(d_second, *u_out))
    d_last = lax.all_to_all(total, "shard", split_axis=0, concat_axis=0, tiled=True)
    du_in = sent(after(du_away, total), flips(1))
    qkv_parts = ring_parts(after(qkv_part, total))
    qkv_in = ring_sent(qkv_parts)
    _, y_bit, x_bit, _ = bits()
    kept = summed(du_keep, after(du_in, *qkv_parts)).reshape(2, 2, count, width)
    kept = halves(kept)
    out = picked(kept[0], 1 - y_bit, 0), picked(kept[1], 1 - x_bit, 1)
    kept = picked(kept[0], y_bit, 0), picked(kept[1], x_bit, 1)
    got = pair_sent(out, 4, 2)
    u_parts = ring_parts(
        last_total(in_flip, rights, u_core, u_first, pair_after(u_second, *out))
    )
    u_in = ring_sent(u_parts)
    kept = [summed(*both) for both in zip(kept, pair_after(got, *u_parts))]
    out = picked(kept[0], 1 - x_bit, 0), picked(kept[1], 1 - y_bit, 0)
    kept = picked(kept[0], x_bit, 0), picked(kept[1], y_bit, 0)
    got = pair_sent(out, 2, 4)
    grad_down = jnp.sum(after(d_last, *out).astype(F32), axis=0)
    grad_qkv = ring_total(qkv_parts[0], pair_after(qkv_in, grad_down))
    size = width // shards
    gain_pair = grad_qkv[size : size + 2, : size // ctx_size].T
    qkv_last = swapped(grad_qkv[:size].reshape(ctx_size, -1, 3 * lanes), None)
    grad_tokens = finish_tokens(kept, pair_after(got, grad_qkv), x, dh, gain_all)
    grad_in = ring_total(u_parts[0], pair_after(u_in, grad_tokens))
    grad_qkv = after(qkv_last, grad_in)
    grad_out, grad_up = grad_in[:, :width], grad_in[:, width:]

    grad_qkv = grad_qkv.reshape(ctx_size, -1, 3, lanes).transpose(1, 2, 0, 3)
    grad_qkv = grad_qkv.reshape(-1, 3 * width)

    own_gains = picked(gains.reshape(ctx_size, -1, kinds), place, 0).astype(F32)
    row_sum = lambda weight, grad: jnp.sum(
        picked(split(weight), place, 0).astype(F32) * grad, axis=1
    )
    gain_one = row_sum(w_qkv, grad_qkv) / own_gains[:, 0]
    gain_three = row_sum(w_up, grad_up) / own_gains[:, 2]
    grad_gains = jnp.stack([gain_one, gain_pair[:, 0], gain_three, gain_pair[:, 1]], axis=1)
    return (
        layer_out.reshape(batch, rows, width),
        grad_tokens.reshape(batch, rows, width),
        grad_qkv,
        grad_out,
        grad_up,
        grad_down,
        grad_gains,
    )


def per_device(*args):
    return staged(*args) if cube() else plain(*args)


def solution(mesh):
    return jax.shard_map(
        per_device,
        mesh=mesh,
        in_specs=(
            P(None, ALL, None),
            P(None, "shard", None),
            P("shard", None),
            P("shard", None),
            P("shard", None),
            P("shard", None),
            P("shard", None),
            P(None, ALL, None),
        ),
        out_specs=(
            P(None, ALL, None),
            P(None, ALL, None),
            P(ALL, None),
            P(ALL, None),
            P(ALL, None),
            P(ALL, None),
            P(ALL, None),
        ),
        check_vma=False,
    )
```

```python
import functools
import math

import jax
import jax.numpy as jnp
from jax import lax
from jax.experimental import pallas as pl
from jax.experimental.pallas import tpu as pltpu
from jax.sharding import PartitionSpec as P

HEADS = 16
HDIM = 64
EPSILON = 1e-05
ROPE_BASE = 10000.0
MASKED = -1e30
ALL = ("shard", "ctx")
BF = jnp.bfloat16
F32 = jnp.float32
VMEM_LIMIT = 56 * 1024 * 1024
GAIN_ROWS = 16


def layer_norm(values, gain):
    center = jnp.mean(values, axis=-1, keepdims=True)
    shifted = values - center
    spread = jnp.mean(shifted * shifted, axis=-1, keepdims=True)
    return shifted * lax.rsqrt(spread + EPSILON) * gain


def gelu_tanh(values):
    return jax.nn.gelu(values, approximate=True)


def dot(left, right):
    return jnp.dot(left, right, preferred_element_type=F32)


def contract_rows(left, right):
    return lax.dot_general(left, right, (((0,), (0,)), ((), ())), preferred_element_type=F32)


def contract_cols(left, right):
    return lax.dot_general(left, right, (((1,), (1,)), ((), ())), preferred_element_type=F32)


def rope_tables(doc_starts, blocks, rows):
    half = HDIM // 2
    lane = jnp.arange(2 * HDIM, dtype=jnp.int32)
    freqs = ROPE_BASE ** (-(lane % half).astype(F32) / half)
    sign = jnp.where(lane % HDIM < half, -1.0, 1.0).astype(F32)
    positions = jnp.arange(blocks * rows, dtype=jnp.int32).reshape(blocks, 1, rows)
    latest = jnp.zeros((blocks, doc_starts.shape[0], rows), jnp.int32)
    for d in range(doc_starts.shape[1]):
        start = doc_starts[None, :, d, None]
        latest = jnp.where(positions >= start, jnp.maximum(latest, start), latest)
    angles = (positions - latest).astype(F32)[..., None] * freqs
    return jnp.cos(angles), jnp.sin(angles) * sign


def turned(values, cos_row, sin_row):
    width = values.shape[1]
    half = HDIM // 2
    if width == HDIM:
        swapped = jnp.concatenate([values[:, half:], values[:, :half]], axis=1)
    else:
        lane = lax.broadcasted_iota(jnp.int32, values.shape, 1)
        swapped = jnp.where(
            lane % HDIM < half, pltpu.roll(values, width - half, 1), pltpu.roll(values, half, 1)
        )
    return values * cos_row[:, :width] + swapped * sin_row[:, :width]


def project_rows(u, weight, cos_row, sin_row, lanes):
    full = dot(u, weight)
    parts = [full[:, slot * lanes : (slot + 1) * lanes] for slot in range(3)]
    query = turned(parts[0], cos_row, sin_row) * HDIM ** (-0.5)
    return query, turned(parts[1], cos_row, sin_row), parts[2]


def norm_parts(values):
    shifted = values - jnp.mean(values, axis=-1, keepdims=True)
    scale = lax.rsqrt(jnp.mean(shifted * shifted, axis=-1, keepdims=True) + EPSILON)
    return shifted * scale, scale


def norm_back(grad, normed, scale, gain):
    scaled = grad * gain
    return scale * (
        scaled
        - jnp.mean(scaled, axis=-1, keepdims=True)
        - normed * jnp.mean(scaled * normed, axis=-1, keepdims=True)
    )


def project_kernel(
    shards, where, a0, a1, b0, b1, cos_ref, sin_ref, *rest
):
    part_refs, (out_ref, u_ref, w_ref, gain_ref) = rest[:shards], rest[shards:]
    _, _, batch, rows, lanes = out_ref.shape
    count = batch * rows
    size = w_ref.shape[0] // shards

    @pl.when(pl.program_id(0) == 0)
    def _():
        for k, part_ref in enumerate(part_refs):
            at = pl.multiple_of(lax.rem(where[0] - k + shards, shards) * size, size)
            w_ref[pl.ds(at, size), :] = part_ref[:size, :]
            gain_ref[:, pl.ds(at, size)] = part_ref[size:, :size].astype(F32)

    gain = gain_ref[0:1, :]
    for side, (a, b) in enumerate(((a0, b0), (a1, b1))):
        core = where[3] ^ side
        x = jnp.concatenate([a[...], b[...]], axis=1).astype(F32)
        u = (norm_parts(x)[0] * gain).astype(BF)
        u_ref[core] = u
        cos_row = cos_ref[core].reshape(count, -1)
        sin_row = sin_ref[core].reshape(count, -1)
        for slot, part in enumerate(project_rows(u, w_ref[...], cos_row, sin_row, lanes)):
            out_ref[core, slot] = part.reshape(batch, rows, lanes).astype(BF)


def project(parts, weight_parts, cos_all, sin_all):
    a, b = parts[0], parts[2]
    count, half = a.shape[2:]
    shards = len(weight_parts)
    size, columns = weight_parts[0].shape
    width = 2 * half
    kinds = size - width // shards
    lanes = columns // 3
    blocks, batch, rows, _ = cos_all.shape
    a_spec = pl.BlockSpec(
        (None, None, count, half), lambda t, w: ((t // 2) ^ w[1], (t % 2) ^ w[2], 0, 0)
    )
    b_spec = pl.BlockSpec(
        (None, None, count, half), lambda t, w: ((t % 2) ^ w[2], (t // 2) ^ w[1], 0, 0)
    )
    table = pl.BlockSpec((2, batch, rows, 2 * HDIM), lambda t, w: (t, 0, 0, 0))
    whole = lambda shape: pl.BlockSpec(shape, lambda t, w: (0, 0))
    return pl.pallas_call(
        functools.partial(project_kernel, shards),
        out_shape=(
            jax.ShapeDtypeStruct((blocks, 3, batch, rows, lanes), BF),
            jax.ShapeDtypeStruct((blocks, count, width), BF),
            jax.ShapeDtypeStruct((width, columns), BF),
            jax.ShapeDtypeStruct((kinds, width), F32),
        ),
        grid_spec=pltpu.PrefetchScalarGridSpec(
            num_scalar_prefetch=1,
            grid=(4,),
            in_specs=[a_spec, a_spec, b_spec, b_spec, table, table]
            + [whole((size, columns))] * shards,
            out_specs=(
                pl.BlockSpec((2, 3, batch, rows, lanes), lambda t, w: (t, 0, 0, 0, 0)),
                pl.BlockSpec((2, count, width), lambda t, w: (t, 0, 0)),
                whole((width, columns)),
                whole((kinds, width)),
            ),
        ),
        compiler_params=pltpu.CompilerParams(vmem_limit_bytes=VMEM_LIMIT),
        name="project",
    )(where(), *parts, cos_all, sin_all, *weight_parts)


def project_plain(u_run, weight, cos_run, sin_run):
    blocks, batch, rows, _ = cos_run.shape
    lanes = weight.shape[1] // 3
    full = dot(u_run.reshape(-1, weight.shape[0]), weight).reshape(blocks, batch, rows, 3, -1, HDIM)
    half = HDIM // 2
    cosine, sine = (t[..., None, half:HDIM] for t in (cos_run, sin_run))

    def turn(values):
        first, second = values[..., :half], values[..., half:]
        return jnp.concatenate(
            [first * cosine - second * sine, second * cosine + first * sine], axis=-1
        )

    parts = [turn(full[..., 0, :, :]) * HDIM ** (-0.5), turn(full[..., 1, :, :]), full[..., 2, :, :]]
    return jnp.stack([p.reshape(blocks, batch, rows, lanes).astype(BF) for p in parts], axis=1)


def starts_row(info_ref, mb, docs, positions):
    latest = jnp.zeros_like(positions)
    for d in range(docs):
        start = info_ref[mb, d]
        latest = jnp.where(positions >= start, jnp.maximum(latest, start), latest)
    return latest


def start_scalar(info_ref, mb, docs, position):
    latest = jnp.int32(0)
    for d in range(docs):
        start = info_ref[mb, d]
        latest = jnp.where(position >= start, jnp.maximum(latest, start), latest)
    return latest


def attend_kernel(docs, heads, mb, info_ref, q_ref, k_ref, v_ref, *rest):
    o_ref, ob_ref, lse_ref = rest[-3:]
    i = pl.program_id(0)
    per, rows, lanes = q_ref.shape
    block = per * rows
    first = info_ref[mb, docs] + i * block
    low = start_scalar(info_ref, mb, docs, first) // block
    diag = first // block
    q_pos = first + lax.broadcasted_iota(jnp.int32, (1, block), 1)
    q_start = starts_row(info_ref, mb, docs, q_pos)
    q_all = q_ref[...].reshape(block, lanes)
    queries = [q_all[:, h * HDIM : (h + 1) * HDIM] for h in range(heads)]

    def visit(step, state):
        j = diag - step
        k_all = k_ref[pl.ds(j * per, per)].reshape(block, lanes)
        v_flip = v_ref[pl.ds(j * per, per)].reshape(block, lanes).astype(F32).T.astype(BF)
        k_pos = j * block + lax.broadcasted_iota(jnp.int32, (block, 1), 0)
        allowed = (k_pos >= q_start) & (k_pos <= q_pos)
        out = []
        for h in range(heads):
            peak, total, acc = state[h]
            scores = contract_cols(k_all[:, h * HDIM : (h + 1) * HDIM], queries[h])
            scores = jnp.where(allowed, scores, MASKED)
            new_peak = jnp.maximum(peak, jnp.max(scores, axis=0, keepdims=True))
            decay = jnp.exp(peak - new_peak)
            weights = jnp.exp(scores - new_peak)
            total = total * decay + jnp.sum(weights, axis=0, keepdims=True)
            acc = acc * decay + dot(v_flip[h * HDIM : (h + 1) * HDIM], weights.astype(BF))
            out.append((new_peak, total, acc))
        return tuple(out)

    start = tuple(
        (
            jnp.full((1, block), MASKED, F32),
            jnp.zeros((1, block), F32),
            jnp.zeros((HDIM, block), F32),
        )
        for _ in range(heads)
    )
    state = lax.fori_loop(0, diag - low + 1, visit, start)
    flipped = jnp.concatenate([acc / total for _, total, acc in state], axis=0)
    attended = flipped.T
    o_ref[...] = attended.reshape(per, rows, lanes)
    ob_ref[...] = attended.astype(BF).reshape(per, rows, lanes)
    lse_ref[...] = jnp.concatenate([peak + jnp.log(total) for peak, total, _ in state], axis=0)


def attend(info, docs, mb, queries, q_slot, keys, k_slot, v_slot, earlier=()):
    group_count, _, batch, rows, lanes = queries.shape
    blocks_all = keys.shape[0]
    heads = lanes // HDIM
    per = math.gcd(group_count, max(1, 256 // rows))
    q_blocks = group_count // per
    spec = pl.BlockSpec((per, None, None, rows, lanes), lambda i, info: (i, q_slot, mb, 0, 0))
    kv_spec = lambda slot: pl.BlockSpec(
        (blocks_all, None, None, rows, lanes), lambda i, info: (0, slot, mb, 0, 0)
    )
    o_spec = pl.BlockSpec((per, None, rows, lanes), lambda i, info: (i, mb, 0, 0))
    return pl.pallas_call(
        functools.partial(attend_kernel, docs, heads, mb),
        out_shape=(
            jax.ShapeDtypeStruct((group_count, batch, rows, lanes), F32),
            jax.ShapeDtypeStruct((group_count, batch, rows, lanes), BF),
            jax.ShapeDtypeStruct((batch, heads, group_count * rows), F32),
        ),
        grid_spec=pltpu.PrefetchScalarGridSpec(
            num_scalar_prefetch=1,
            grid=(q_blocks,),
            in_specs=[spec, kv_spec(k_slot), kv_spec(v_slot)]
            + [pl.BlockSpec(memory_space=pl.ANY)] * len(earlier),
            out_specs=(
                o_spec,
                o_spec,
                pl.BlockSpec((None, heads, per * rows), lambda i, info: (mb, 0, i)),
            ),
        ),
        input_output_aliases={4 + n: n for n in range(len(earlier))},
        compiler_params=pltpu.CompilerParams(vmem_limit_bytes=VMEM_LIMIT),
        name="attend",
    )(info, queries, keys, keys, *earlier)


def attend_back_kernel(
    docs, heads, per, merged, mb, info_ref, q_ref, k_ref, v_ref, do_ref, o_ref, lse_ref, cosq_ref,
    sinq_ref, cosk_ref, sink_ref, *rest
):
    j = pl.program_id(0)
    out_ref, dq_acc, delta_ref = rest[-3:]
    dq_ref = None if merged else rest[-4]
    group_count, rows, lanes = q_ref.shape
    block = per * rows
    q_blocks = group_count // per
    base = info_ref[mb, docs] // block

    def lanes_of(i):
        return pl.ds(pl.multiple_of(i * block, block), block)

    @pl.when(j == 0)
    def _():
        dq_acc[...] = jnp.zeros_like(dq_acc)

        def fill(i, carry):
            here = pl.ds(i * per, per)
            prod = do_ref[here].reshape(block, lanes).astype(F32) * o_ref[here].reshape(
                block, lanes
            )
            flipped = prod.T
            delta_ref[:, lanes_of(i)] = jnp.concatenate(
                [
                    jnp.sum(flipped[h * HDIM : (h + 1) * HDIM], axis=0, keepdims=True)
                    for h in range(heads)
                ],
                axis=0,
            )
            return carry

        lax.fori_loop(0, q_blocks, fill, 0)

    k_first = j * block
    last = k_first + block - 1
    end = base * block + group_count * rows
    for d in range(docs):
        start = info_ref[mb, d]
        end = jnp.where(start > last, jnp.minimum(end, start), end)
    i_low = jnp.maximum(j - base, 0)
    i_high = jnp.maximum((end - base * block + block - 1) // block, i_low)
    k_pos = k_first + lax.broadcasted_iota(jnp.int32, (block, 1), 0)
    k_all = k_ref[...].reshape(block, lanes)
    v_all = v_ref[...].reshape(block, lanes)
    k_flip = k_all.astype(F32).T.astype(BF)
    heads_of = lambda a: [a[:, h * HDIM : (h + 1) * HDIM] for h in range(heads)]
    k_heads, v_heads = heads_of(k_all), heads_of(v_all)

    def visit(i, state):
        here = pl.ds(i * per, per)
        q_heads = heads_of(q_ref[here].reshape(block, lanes))
        do_heads = heads_of(do_ref[here].reshape(block, lanes))
        q_pos = (base + i) * block + lax.broadcasted_iota(jnp.int32, (1, block), 1)
        q_start = starts_row(info_ref, mb, docs, q_pos)
        allowed = (k_pos >= q_start) & (k_pos <= q_pos)
        lse = lse_ref[:, lanes_of(i)]
        delta = delta_ref[:, lanes_of(i)]
        out = []
        for h in range(heads):
            dk, dv = state[h]
            scores = contract_cols(k_heads[h], q_heads[h])
            weights = jnp.exp(jnp.where(allowed, scores - lse[h : h + 1], MASKED))
            grad_weights = contract_cols(v_heads[h], do_heads[h])
            grad_scores = (weights * (grad_weights - delta[h : h + 1])).astype(BF)
            dv = dv + dot(weights.astype(BF), do_heads[h])
            dk = dk + dot(grad_scores, q_heads[h])
            at = slice(h * HDIM, (h + 1) * HDIM)
            dq_acc[at, lanes_of(i)] += dot(k_flip[at], grad_scores)
            out.append((dk, dv))
        return tuple(out)

    zero = jnp.zeros((block, HDIM), F32)
    state = lax.fori_loop(i_low, i_high, visit, tuple((zero, zero) for _ in range(heads)))
    dk = jnp.concatenate([dk for dk, _ in state], axis=1) if heads > 1 else state[0][0]
    dv = jnp.concatenate([dv for _, dv in state], axis=1) if heads > 1 else state[0][1]
    dk = turned(dk, cosk_ref[...].reshape(block, -1), -sink_ref[...].reshape(block, -1))
    there = pl.ds(j * per, per)
    first = lanes if merged else 0
    out_ref[there, :, first : first + lanes] = dk.reshape(per, rows, lanes).astype(out_ref.dtype)
    out_ref[there, :, first + lanes : first + 2 * lanes] = dv.reshape(per, rows, lanes).astype(
        out_ref.dtype
    )

    @pl.when(j == pl.num_programs(0) - 1)
    def _():
        def finish(i, carry):
            dq = dq_acc[:, lanes_of(i)].T
            at = pl.ds(i * per, per)
            cos_row = cosq_ref[at].reshape(block, -1)
            sin_row = sinq_ref[at].reshape(block, -1)
            dq = turned(dq, cos_row, -sin_row) * HDIM ** (-0.5)
            dq = dq.reshape(per, rows, lanes).astype(BF)
            if merged:
                out_ref[at, :, :lanes] = dq
            else:
                dq_ref[at] = dq
            return carry

        lax.fori_loop(0, q_blocks, finish, 0)


def attend_back(info, docs, mb, queries, q_slot, keys, k_slot, v_slot, grad, attended, lse,
                cos_all, sin_all, cos_here, sin_here, earlier=()):
    group_count, _, batch, rows, lanes = queries.shape
    blocks_all = keys.shape[0]
    merged = blocks_all == group_count
    heads = lanes // HDIM
    per = math.gcd(group_count, max(1, 256 // rows))
    length = group_count * rows
    full = pl.BlockSpec(
        (group_count, None, None, rows, lanes), lambda j, info: (0, q_slot, mb, 0, 0)
    )
    part = lambda slot: pl.BlockSpec(
        (per, None, None, rows, lanes), lambda j, info: (j, slot, mb, 0, 0)
    )
    rows_of_mb = lambda count, width: pl.BlockSpec(
        (count, None, rows, width), lambda j, info: (0, mb, 0, 0)
    )
    table_k = pl.BlockSpec((per, None, rows, 2 * HDIM), lambda j, info: (j, mb, 0, 0))
    if merged:
        out_shape = [jax.ShapeDtypeStruct((group_count, batch, rows, 3 * lanes), BF)]
        out_specs = [rows_of_mb(group_count, 3 * lanes)]
    else:
        out_shape = [
            jax.ShapeDtypeStruct((group_count, batch, rows, lanes), BF),
            jax.ShapeDtypeStruct((blocks_all, batch, rows, 2 * lanes), F32),
        ]
        out_specs = [rows_of_mb(group_count, lanes), rows_of_mb(blocks_all, 2 * lanes)]
    table_q = rows_of_mb(group_count, 2 * HDIM)
    return pl.pallas_call(
        functools.partial(attend_back_kernel, docs, heads, per, merged, mb),
        out_shape=out_shape,
        grid_spec=pltpu.PrefetchScalarGridSpec(
            num_scalar_prefetch=1,
            grid=(blocks_all // per,),
            in_specs=[
                full, part(k_slot), part(v_slot), rows_of_mb(group_count, lanes),
                rows_of_mb(group_count, lanes),
                pl.BlockSpec((None, heads, length), lambda j, info: (mb, 0, 0)),
                table_q, table_q, table_k, table_k,
            ]
            + [pl.BlockSpec(memory_space=pl.ANY)] * len(earlier),
            out_specs=out_specs,
            scratch_shapes=[pltpu.VMEM((lanes, length), F32), pltpu.VMEM((heads, length), F32)],
        ),
        input_output_aliases={11 + n: n for n in range(len(earlier))},
        compiler_params=pltpu.CompilerParams(vmem_limit_bytes=VMEM_LIMIT),
        name="attend_back",
    )(info, queries, keys, keys, grad, attended, lse, cos_here, sin_here, cos_all, sin_all,
      *earlier)


def flips(mask):
    count = lax.axis_size("shard") * lax.axis_size("ctx")
    return [(i, i ^ mask) for i in range(count)]


def turns(by):
    shards, places = lax.axis_size("shard"), lax.axis_size("ctx")
    return [
        (a * places + b, ((a + by) % shards) * places + b)
        for a in range(shards)
        for b in range(places)
    ]


def sent(values, pairs):
    return lax.ppermute(values, ALL, pairs)


def picked(values, index, axis):
    return lax.dynamic_index_in_dim(values, index, axis, keepdims=False)


def cube():
    return lax.axis_size("ctx") == 8 and lax.axis_size("shard") == 4


def bits():
    place = lax.axis_index("ctx")
    return lax.axis_index("shard"), place // 4, place // 2 % 2, place % 2


def where():
    return jnp.stack(bits()).astype(jnp.int32)


def spread(values, early, late):
    half = values.shape[1] // 2
    a, b = values[:, :half], values[:, half:]
    a_in, b_in = sent(a, flips(2)), sent(b, flips(4))
    a, b = jnp.stack([a, after(a_in, *early)]), jnp.stack([b, after(b_in, *early)])
    a = jnp.stack([a, after(sent(a, flips(4)), *late)])
    b = jnp.stack([b, after(sent(b, flips(2)), *late)])
    return a, sent(a, flips(1)), b, sent(b, flips(1))


def ring_parts(values):
    shards = lax.axis_size("shard")
    z = lax.axis_index("shard")
    return [picked(values, lax.rem(z + k, shards), 0) for k in range(shards)]


def ring_sent(parts):
    return [sent(part, turns(k)) for k, part in enumerate(parts) if k]


def ring_total(own, received):
    total = own.astype(F32)
    for part in received:
        total = total + part.astype(F32)
    return total


def fold_first(values):
    low = lax.axis_index("shard") % 2
    return picked(values.reshape(2, 2, *values.shape[1:]), 1 - low, 1)


def fold_second(values, received):
    z = lax.axis_index("shard")
    mine = picked(values.reshape(2, 2, *values.shape[1:]), z % 2, 1)
    return summed(picked(mine, 1 - z // 2, 0), picked(received, 1 - z // 2, 0))


def fold_last(values, received, last):
    z = lax.axis_index("shard")
    parts = picked(values, z, 0), picked(received, z // 2, 0), last
    return sum(part.astype(F32) for part in parts)


def after(values, *earlier):
    return lax.optimization_barrier((values,) + earlier)[0]


def far_rows(piece, *earlier):
    shards = lax.axis_size("shard")
    return jnp.stack([after(sent(piece, turns(k)), *earlier) for k in range(1, shards)])


def copies_in(where, owns, parts, out_ref, sem):
    z, y, x, c = (where[i] for i in range(4))
    shards = out_ref.shape[0]
    half = parts[0].shape[-1]
    groups = [[] for _ in range(shards)]

    def add(k, source, target):
        at = sum(len(group) for group in groups)
        groups[k].append(pltpu.make_async_copy(source, target, sem.at[at]))

    first = 0
    for own in owns:
        add(0, own, out_ref.at[z, :, :, pl.ds(first, own.shape[-1])])
        first += own.shape[-1]
    for k in range(1, shards):
        source = lax.rem(z - k + shards, shards)
        for side in range(2):
            a, b = parts[side], parts[2 + side]
            core = c ^ side
            for p in range(2):
                for q in range(2):
                    at_a = ((y ^ p) * 2 + (x ^ q)) * 2 + core
                    at_b = ((y ^ q) * 2 + (x ^ p)) * 2 + core
                    add(k, a.at[p, q, k - 1], out_ref.at[source, at_a, :, pl.ds(0, half)])
                    add(k, b.at[p, q, k - 1], out_ref.at[source, at_b, :, pl.ds(half, half)])
    for group in groups:
        for copy in group:
            copy.start()
    return groups


def arrived(groups, where):
    shards = len(groups)
    for k, group in enumerate(groups):
        for copy in group:
            copy.wait()
        yield lax.rem(where[0] - k + shards, shards)


def copy_count(shards, owns):
    return owns + 16 * (shards - 1)


def rows_of(w, first, last):
    part = w[:, :, :, first:last]
    return part.reshape(-1, last - first)


def chunk_of(w, z, first, last):
    part = w[z, :, :, first:last]
    return part.reshape(-1, last - first)


def block_at(z, size):
    return pl.ds(pl.multiple_of(z * size, size), size)


def flip_pieces(values, size, out_ref, first):
    tokens, rows = values.shape
    step = max(size, 128)
    for start in range(0, rows, step):
        flip = values[:, start : start + step].astype(F32).T.astype(BF)
        for low in range(0, step, size):
            piece = (start + low) // size
            z, y, x, c = piece // 8, piece // 4 % 2, piece // 2 % 2, piece % 2
            out_ref[c, y, x, z, :, first : first + tokens] = flip[low : low + size]


def mlp_in_kernel(
    where, ob_ref, x_ref, gain_ref, own_out, own_up, a0, a1, b0, b1,
    a_ref, h_ref, g_ref, slope_ref, in_flip, g_flip, w, obl, sem
):
    copies = copies_in(where, (own_out, own_up), (a0, a1, b0, b1), w, sem)
    groups, batch, rows, lanes = ob_ref.shape
    shards = w.shape[0]
    width = x_ref.shape[1]
    count = batch * rows
    size = width // shards
    for mb in range(batch):
        for g in range(groups):
            obl[mb * rows : (mb + 1) * rows, g * lanes : (g + 1) * lanes] = ob_ref[g, mb]
    flip_pieces(obl[...], size // 8, in_flip, count)
    a = None
    for z in arrived(copies, where):
        part = dot(obl[:, block_at(z, size)], chunk_of(w, z, 0, width))
        a = part if a is None else a + part
    a_ref[...] = a
    h = x_ref[...].astype(F32) + norm_parts(a)[0] * gain_ref[1:2, :]
    h_ref[...] = h
    u2 = (norm_parts(h)[0] * gain_ref[2:3, :]).astype(BF)
    flip_pieces(u2, size // 8, in_flip, 0)
    hidden = g_ref.shape[1]
    step = 512
    root = math.sqrt(2.0 / math.pi)
    for first in range(0, hidden, step):
        f = dot(u2, rows_of(w, width + first, width + first + step))
        square = f * f
        bent = jnp.tanh(root * (f + 0.044715 * (square * f)))
        half = 0.5 * (1.0 + bent)
        at = slice(first, first + step)
        g_ref[:, at] = (f * half).astype(BF)
        slope = half + 0.5 * f * (1.0 - bent * bent) * (root * (1.0 + 3 * 0.044715 * square))
        slope_ref[:, at] = slope.astype(BF)
    flip_pieces(g_ref[...], hidden // (8 * shards), g_flip, 0)


def mlp_in(ob, x, gain_all, w_out, w_up, parts):
    shards = lax.axis_size("shard")
    count, width = x.shape
    hidden = w_up.shape[-1]
    pieces, rows = w_out.shape[:2]
    anywhere = pl.BlockSpec(memory_space=pl.ANY)
    local = pl.BlockSpec(memory_space=pltpu.VMEM)
    shape = jax.ShapeDtypeStruct
    return pl.pallas_call(
        mlp_in_kernel,
        out_shape=(
            shape((count, width), F32),
            shape((count, width), F32),
            shape((count, hidden), BF),
            shape((count, hidden), BF),
            shape((2, 2, 2, shards, width // (8 * shards), 2 * count), BF),
            shape((2, 2, 2, shards, hidden // (8 * shards), count), BF),
        ),
        grid_spec=pltpu.PrefetchScalarGridSpec(
            num_scalar_prefetch=1,
            grid=(),
            in_specs=[local] * 3 + [anywhere] * 6,
            out_specs=[local] * 6,
            scratch_shapes=[
                pltpu.VMEM((shards, pieces, rows, width + hidden), BF),
                pltpu.VMEM((count, width), BF),
                pltpu.SemaphoreType.DMA((copy_count(shards, 2),)),
            ],
        ),
        compiler_params=pltpu.CompilerParams(vmem_limit_bytes=VMEM_LIMIT),
        name="mlp_in",
    )(where(), ob, x, gain_all, w_out, w_up, *parts)


def mlp_out_kernel(
    where, g_ref, slope_ref, h_ref, cot_ref, gain_ref, own, a0, a1, b0, b1,
    out_ref, dmb_ref, dfb_ref, gg_ref, w, sem
):
    copies = copies_in(where, (own,), (a0, a1, b0, b1), w, sem)
    shards = w.shape[0]
    width = h_ref.shape[1]
    size = g_ref.shape[1] // shards
    m = None
    for z in arrived(copies, where):
        part = dot(g_ref[:, block_at(z, size)], chunk_of(w, z, 0, width))
        m = part if m is None else m + part
    gain = gain_ref[3:4, :]
    normed, scale = norm_parts(m)
    out_ref[...] = (h_ref[...] + normed * gain).astype(BF)
    dy = cot_ref[...].astype(F32)
    gg_ref[...] = jnp.sum(dy * normed, axis=0, keepdims=True)
    dmb = norm_back(dy, normed, scale, gain).astype(BF)
    dmb_ref[...] = dmb
    for z in range(shards):
        at = slice(z * size, (z + 1) * size)
        dg = contract_cols(dmb, chunk_of(w, z, 0, width))
        dfb_ref[:, at] = (dg * slope_ref[:, at].astype(F32)).astype(BF)


def mlp_out(g, slope, h, cot, gain_all, w_down, parts):
    shards = lax.axis_size("shard")
    count, width = h.shape
    hidden = g.shape[1]
    pieces, rows = w_down.shape[:2]
    anywhere = pl.BlockSpec(memory_space=pl.ANY)
    local = pl.BlockSpec(memory_space=pltpu.VMEM)
    shape = jax.ShapeDtypeStruct
    return pl.pallas_call(
        mlp_out_kernel,
        out_shape=(
            shape((count, width), BF),
            shape((count, width), BF),
            shape((count, hidden), BF),
            shape((1, width), F32),
        ),
        grid_spec=pltpu.PrefetchScalarGridSpec(
            num_scalar_prefetch=1,
            grid=(),
            in_specs=[local] * 5 + [anywhere] * 5,
            out_specs=[local] * 4,
            scratch_shapes=[
                pltpu.VMEM((shards, pieces, rows, width), BF),
                pltpu.SemaphoreType.DMA((copy_count(shards, 1),)),
            ],
        ),
        compiler_params=pltpu.CompilerParams(vmem_limit_bytes=VMEM_LIMIT),
        name="mlp_out",
    )(where(), g, slope, h, cot, gain_all, w_down, *parts)


def mlp_back_kernel(
    where, dfb_ref, h_ref, a_ref, cot_ref, gain_ref, gain_four_ref, own_out, own_up, a0, a1, b0, b1,
    dh_ref, right_a, right_b, dob_ref, w, du2, sem
):
    copies = copies_in(where, (own_out, own_up), (a0, a1, b0, b1), w, sem)
    shards = w.shape[0]
    count, width = h_ref.shape
    size = width // shards
    groups, batch, rows, lanes = dob_ref.shape
    rows -= GAIN_ROWS
    last = w.shape[-1]
    middle = last // 2
    right_a[:count, :width] = jnp.zeros((count, width), BF)
    right_a[count:, width:] = jnp.zeros((count, middle - width), BF)
    right_a[:count, width:] = dfb_ref[:, : middle - width]
    right_b[count:, :] = jnp.zeros((count, middle), BF)
    right_b[:count, :] = dfb_ref[:, middle - width :]
    for z in arrived(copies, where):
        du2[:, block_at(z, size)] = contract_cols(dfb_ref[...], chunk_of(w, z, width, last))
    normed, scale = norm_parts(h_ref[...])
    dh = cot_ref[...].astype(F32) + norm_back(du2[...], normed, scale, gain_ref[2:3, :])
    dh_ref[...] = dh
    normed, scale = norm_parts(a_ref[...])
    gains = (jnp.sum(dh * normed, axis=0, keepdims=True), gain_four_ref[...])
    step = lanes // shards
    blank = jnp.zeros((GAIN_ROWS - len(gains), lanes), F32)
    for g in range(groups):
        lines = [
            jnp.concatenate(
                [line[:, z * size + g * step : z * size + (g + 1) * step] for z in range(shards)],
                axis=1,
            )
            for line in gains
        ]
        block = jnp.concatenate(lines + [blank], axis=0).astype(BF)
        for mb in range(batch):
            dob_ref[g, mb, rows:, :] = block
    dab = norm_back(dh, normed, scale, gain_ref[1:2, :]).astype(BF)
    right_a[count:, :width] = dab
    for z in range(shards):
        dob = contract_cols(dab, chunk_of(w, z, 0, width)).astype(BF)
        for part in range(size // lanes):
            for mb in range(batch):
                dob_ref[z * (size // lanes) + part, mb, :rows] = dob[
                    mb * rows : (mb + 1) * rows, part * lanes : (part + 1) * lanes
                ]


def mlp_back(dfb, h, a, cot, gain_all, gain_four, w_out, w_up, parts, groups, batch):
    shards = lax.axis_size("shard")
    count, width = h.shape
    hidden = dfb.shape[1]
    pieces, rows = w_out.shape[:2]
    anywhere = pl.BlockSpec(memory_space=pl.ANY)
    local = pl.BlockSpec(memory_space=pltpu.VMEM)
    shape = jax.ShapeDtypeStruct
    return pl.pallas_call(
        mlp_back_kernel,
        out_shape=(
            shape((count, width), F32),
            shape((2 * count, (width + hidden) // 2), BF),
            shape((2 * count, (width + hidden) // 2), BF),
            shape((groups, batch, count // batch + GAIN_ROWS, width // groups), BF),
        ),
        grid_spec=pltpu.PrefetchScalarGridSpec(
            num_scalar_prefetch=1,
            grid=(),
            in_specs=[local] * 6 + [anywhere] * 6,
            out_specs=[local] * 4,
            scratch_shapes=[
                pltpu.VMEM((shards, pieces, rows, width + hidden), BF),
                pltpu.VMEM((count, width), F32),
                pltpu.SemaphoreType.DMA((copy_count(shards, 2),)),
            ],
        ),
        compiler_params=pltpu.CompilerParams(vmem_limit_bytes=VMEM_LIMIT),
        name="mlp_back",
    )(where(), dfb, h, a, cot, gain_all, gain_four, w_out, w_up, *parts)


def tail_kernel(where, dqkv_ref, u_ref, w_ref, gain_ref, keep_ref, away_ref, grad_ref):
    core = where[3]
    shards = grad_ref.shape[0]
    size = w_ref.shape[0] // shards
    step = gain_ref.shape[1] // shards
    total = None
    for pair in range(dqkv_ref.shape[0] // 2):
        for side, out_ref in enumerate((keep_ref, away_ref)):
            block = 2 * pair + (core ^ side)
            dqkv = dqkv_ref[block]
            out_ref[pair] = contract_cols(dqkv, w_ref[...]).astype(BF)
            part = dot(dqkv.astype(F32).T.astype(BF), u_ref[block])
            total = part if total is None else total + part
    blank = jnp.zeros((gain_ref.shape[0], grad_ref.shape[2] - step), F32)
    for z in range(shards):
        grad_ref[z, :size] = total[:, z * size : (z + 1) * size].T.astype(BF)
        gains = gain_ref[:, z * step : (z + 1) * step]
        grad_ref[z, size:] = jnp.concatenate([gains, blank], axis=1).astype(BF)


def tail_products(dqkv, u_run, w_heads, gain_part):
    blocks, count, columns = dqkv.shape
    width = w_heads.shape[0]
    shards = lax.axis_size("shard")
    local = pl.BlockSpec(memory_space=pltpu.VMEM)
    rows = jax.ShapeDtypeStruct((blocks // 2, count, width), BF)
    return pl.pallas_call(
        tail_kernel,
        out_shape=(
            rows,
            rows,
            jax.ShapeDtypeStruct((shards, width // shards + gain_part.shape[0], columns), BF),
        ),
        grid_spec=pltpu.PrefetchScalarGridSpec(
            num_scalar_prefetch=1, grid=(), in_specs=[local] * 4, out_specs=[local] * 3
        ),
        compiler_params=pltpu.CompilerParams(vmem_limit_bytes=VMEM_LIMIT),
        name="tail_products",
    )(where(), dqkv, u_run, w_heads, gain_part)


def finish_kernel(keep_a, keep_b, got_a, got_b, x_ref, dh_ref, gain_ref, out_ref):
    parts = ((keep_a, got_a), (keep_b, got_b))
    du = jnp.concatenate([k[...].astype(F32) + g[...].astype(F32) for k, g in parts], axis=1)
    normed, scale = norm_parts(x_ref[...].astype(F32))
    out_ref[...] = dh_ref[...] + norm_back(du, normed, scale, gain_ref[0:1, :])


def finish_tokens(kept, got, x, dh, gain_all):
    local = pl.BlockSpec(memory_space=pltpu.VMEM)
    return pl.pallas_call(
        finish_kernel,
        out_shape=jax.ShapeDtypeStruct(x.shape, F32),
        in_specs=[local] * 7,
        out_specs=local,
        compiler_params=pltpu.CompilerParams(vmem_limit_bytes=VMEM_LIMIT),
        name="finish_tokens",
    )(*kept, *got, x, dh, gain_all)


def product(left, right, *addends):
    total = dot(left.reshape(-1, left.shape[-1]), right)
    total = total.reshape(*left.shape[:-1], right.shape[1])
    for addend in addends:
        total = total + addend.astype(F32)
    return total.astype(BF)


def halves(values):
    half = values.shape[-1] // 2
    return values[..., :half], values[..., half:]


def at(values, y, x):
    return picked(picked(values, y, 0), x, 0)


def first_away(left, rights):
    left = picked(left, 1 - bits()[3], 0)
    return [product(left, right) for right in rights]


def second_away(left, rights, core_in):
    _, y, x, c = bits()
    left = picked(left, c, 0)
    return (
        product(picked(left, 1 - y, 0), rights[0], picked(core_in[0], 1 - y, 0)),
        product(picked(left, 1 - x, 1), rights[1], picked(core_in[1], 1 - x, 1)),
    )


def third_away(left, rights, core_in, first_in):
    _, y, x, c = bits()
    left = picked(left, c, 0)
    return (
        product(
            at(left, y, 1 - x), rights[0], at(core_in[0], y, 1 - x), picked(first_in[0], 1 - x, 0)
        ),
        product(
            at(left, 1 - y, x), rights[1], at(core_in[1], 1 - y, x), picked(first_in[1], 1 - y, 0)
        ),
    )


def last_total(left, rights, core_in, first_in, second_in):
    _, y, x, c = bits()
    left = at(picked(left, c, 0), y, x)
    own = (x, y)
    parts = [
        product(left, rights[n], at(core_in[n], y, x), picked(first_in[n], own[n], 0), second_in[n])
        for n in range(2)
    ]
    return jnp.concatenate(parts, axis=-1)


def pair_sent(parts, first, second):
    return sent(parts[0], flips(first)), sent(parts[1], flips(second))


def pair_after(parts, *earlier):
    return tuple(after(part, *earlier) for part in parts)


def summed(left, right):
    return (left.astype(F32) + right.astype(F32)).astype(BF)


def gathered(weight):
    size = weight.shape[0] // lax.axis_size("ctx")
    piece = lax.dynamic_slice_in_dim(weight, lax.axis_index("ctx") * size, size, 0)
    return lax.all_gather(piece, ALL, axis=0, tiled=True)


def scattered(left, right):
    total = contract_rows(left, right).astype(BF)
    return lax.psum_scatter(total, ALL, scatter_dimension=0, tiled=True).astype(F32)


def scattered_gains(grads):
    count = lax.axis_size("shard") * lax.axis_size("ctx")
    kinds = grads.shape[0]
    parts = grads.reshape(kinds, count, -1).transpose(1, 0, 2)
    parts = lax.all_to_all(parts, ALL, split_axis=0, concat_axis=0, tiled=True)
    return jnp.sum(parts, axis=0).T


def swapped(values, groups):
    return lax.all_to_all(
        values, "ctx", split_axis=0, concat_axis=0, tiled=True, axis_index_groups=groups
    )


def plain(tokens, doc_starts, w_qkv, w_out, w_up, w_down, gains, cotangent):
    ctx_size = lax.axis_size("ctx")
    place = lax.axis_index("ctx")
    batch, rows, width = tokens.shape
    count = batch * rows
    docs = doc_starts.shape[2]
    group_count = math.gcd(HEADS, ctx_size)
    runs = ctx_size // group_count
    if runs == 1:
        near = far = None
    else:
        near = [[r * group_count + g for g in range(group_count)] for r in range(runs)]
        far = [[r * group_count + g for r in range(runs)] for g in range(group_count)]
    lanes = width // group_count

    gain_all = lax.all_gather(gains, "shard", axis=0, tiled=True).T.astype(F32)
    columns = picked(w_qkv.reshape(-1, 3, group_count, lanes), lax.rem(place, group_count), 2)
    w_heads = lax.all_gather(columns.reshape(-1, 3 * lanes), "shard", axis=0, tiled=True)
    full_out, full_up, full_down = gathered(w_out), gathered(w_up), gathered(w_down)

    starts = doc_starts[:, 0, :]
    cos_all, sin_all = rope_tables(starts, ctx_size, rows)
    run_first = (place // group_count) * group_count
    info = jnp.concatenate(
        [starts, jnp.broadcast_to(run_first * rows, (batch, 1)).astype(jnp.int32)], axis=1
    )

    x = tokens.reshape(count, width).astype(F32)
    out_grad = cotangent.reshape(count, width).astype(F32)
    normed, norm_one_back = jax.vjp(layer_norm, x, gain_all[0])
    u = normed.astype(BF)
    cos_here, sin_here = (
        lax.dynamic_slice_in_dim(t, run_first, group_count, 0) for t in (cos_all, sin_all)
    )
    u_run = lax.all_gather(u, "ctx", axis=0, axis_index_groups=near)
    qkv = project_plain(u_run, w_heads, cos_here, sin_here)
    if runs == 1:
        keys, k_slot = qkv, 1
    else:
        keys, k_slot = (
            lax.all_gather(qkv[:, 1:], "ctx", axis=0, tiled=True, axis_index_groups=far),
            0,
        )
    held = ()
    for mb in range(batch):
        held = attend(info, docs, mb, qkv, 0, keys, k_slot, k_slot + 1, held)
    attended, attended_low, lse = held
    ob = swapped(attended_low, near).transpose(1, 2, 0, 3).reshape(count, width)
    attn_proj = dot(ob, full_out)
    attn_branch, norm_two_back = jax.vjp(layer_norm, attn_proj, gain_all[1])
    hidden = x + attn_branch
    normed_two, norm_three_back = jax.vjp(layer_norm, hidden, gain_all[2])
    u2 = normed_two.astype(BF)
    up_proj = dot(u2, full_up)
    activated, gelu_back = jax.vjp(gelu_tanh, up_proj)
    g = activated.astype(BF)
    down_proj = dot(g, full_down)
    mlp_branch, norm_four_back = jax.vjp(layer_norm, down_proj, gain_all[3])
    layer_out = (hidden + mlp_branch).astype(BF)

    down_grad, gain_four = norm_four_back(out_grad)
    dmb = down_grad.astype(BF)
    grad_down = scattered(g, dmb)
    (up_grad,) = gelu_back(contract_cols(dmb, full_down))
    dfb = up_grad.astype(BF)
    grad_up = scattered(u2, dfb)
    hidden_add, gain_three = norm_three_back(contract_cols(dfb, full_up))
    dh = out_grad + hidden_add
    attn_grad, gain_two = norm_two_back(dh)
    dab = attn_grad.astype(BF)
    grad_out = scattered(ob, dab)
    dob = contract_cols(dab, full_out).astype(BF)
    dob = swapped(dob.reshape(batch, rows, group_count, lanes).transpose(2, 0, 1, 3), near)
    back = ()
    for mb in range(batch):
        back = attend_back(
            info, docs, mb, qkv, 0, keys, k_slot, k_slot + 1, dob, attended, lse, cos_all, sin_all,
            cos_here, sin_here, back,
        )
    if runs == 1:
        dqkv = back[0]
    else:
        dkv = lax.psum_scatter(
            back[1], "ctx", scatter_dimension=0, tiled=True, axis_index_groups=far
        )
        dqkv = jnp.concatenate([back[0], dkv.astype(BF)], axis=-1)
    dqkv = dqkv.reshape(group_count * count, 3 * lanes)
    du = contract_cols(dqkv, w_heads)
    qkv_part = contract_rows(u_run.reshape(group_count * count, width), dqkv)
    du = lax.psum_scatter(du, "ctx", scatter_dimension=0, tiled=True, axis_index_groups=near)
    own = jnp.zeros((width, 3, group_count, lanes), F32)
    own = lax.dynamic_update_slice_in_dim(
        own, qkv_part.reshape(width, 3, 1, lanes), lax.rem(place, group_count), 2
    )
    grad_qkv = lax.psum_scatter(
        own.reshape(width, 3 * width), ALL, scatter_dimension=0, tiled=True
    )
    input_add, gain_one = norm_one_back(du)
    grad_tokens = dh + input_add
    grad_gains = scattered_gains(jnp.stack([gain_one, gain_two, gain_three, gain_four]))
    return (
        layer_out.reshape(batch, rows, width),
        grad_tokens.reshape(batch, rows, width),
        grad_qkv,
        grad_out,
        grad_up,
        grad_down,
        grad_gains,
    )


def staged(tokens, doc_starts, w_qkv, w_out, w_up, w_down, gains, cotangent):
    ctx_size, shards = lax.axis_size("ctx"), lax.axis_size("shard")
    place = lax.axis_index("ctx")
    batch, rows, width = tokens.shape
    count = batch * rows
    docs = doc_starts.shape[2]
    lanes = width // ctx_size
    kinds = gains.shape[1]
    x = tokens.reshape(count, width)
    cot = cotangent.reshape(count, width)
    split = lambda w: w.reshape(ctx_size, -1, w.shape[1])
    own_out, own_up, own_down = split(w_out), split(w_up), split(w_down)

    starts = doc_starts[:, 0, :]
    cos_all, sin_all = rope_tables(starts, ctx_size, rows)
    columns = picked(w_qkv.reshape(-1, 3, ctx_size, lanes), place, 2).reshape(-1, 3 * lanes)
    gain_rows = jnp.pad(gains.T, ((0, 8 - kinds), (0, 3 * lanes - gains.shape[0])))
    piece = jnp.concatenate([columns, gain_rows])
    head_parts = [piece] + [sent(piece, turns(k)) for k in range(1, shards)]

    piece = jnp.concatenate([picked(own_out, place, 0), picked(own_up, place, 0)], axis=1)
    piece = after(piece, cos_all, sin_all, *head_parts)
    far_in = [sent(piece, turns(k)) for k in range(1, shards)]
    x_parts = spread(x, (cos_all, sin_all, *head_parts[1:]), (far_in[0], far_in[-1]))

    info = jnp.concatenate([starts, jnp.zeros((batch, 1), jnp.int32)], axis=1)
    qkv, u_run, w_heads, gain_all = project(x_parts, head_parts, cos_all, sin_all)

    far_in = jnp.stack([after(part, qkv) for part in far_in])
    piece_out = after(picked(own_down, place, 0), far_in)
    half = far_in.shape[2] // 2
    a, b = far_in[:, :, :half], far_in[:, :, half:]
    a_in, b_in = sent(a, flips(2)), sent(b, flips(4))
    held = ()
    for mb in range(batch):
        held = attend(after(info, far_in, *held), docs, mb, qkv, 0, qkv, 1, 2, held)
        if mb == 0:
            a, b = jnp.stack([a, after(a_in, held[2])]), jnp.stack([b, after(b_in, held[2])])
            info = after(info, a, b)
    attended, attended_low, lse = held
    a_in, b_in = sent(a, flips(4)), sent(b, flips(2))
    ob = swapped(attended_low, None)
    far_out = far_rows(piece_out, lse)
    half = far_out.shape[2] // 2
    c, d = far_out[:, :, :half], far_out[:, :, half:]
    c_in, d_in = sent(c, flips(2)), sent(d, flips(4))
    a, b = jnp.stack([a, after(a_in, c, d)]), jnp.stack([b, after(b_in, c, d)])
    in_parts = (a, sent(a, flips(1)), b, sent(b, flips(1)))
    c, d = jnp.stack([c, after(c_in, a, b, ob)]), jnp.stack([d, after(d_in, a, b, ob)])
    c_in, d_in = sent(c, flips(4)), sent(d, flips(2))

    attn, h, g, slope, in_flip, g_flip = mlp_in(
        after(ob, c, d), x, gain_all, own_out, own_up, in_parts
    )
    c, d = jnp.stack([c, after(c_in, h)]), jnp.stack([d, after(d_in, h)])
    out_parts = (c, sent(c, flips(1)), d, sent(d, flips(1)))
    layer_out, dmb, dfb, gain_four = mlp_out(g, slope, h, cot, gain_all, own_down, out_parts)

    dmbs = halves(dmb)
    d_out = first_away(g_flip, dmbs)
    d_core = pair_sent(d_out, 1, 1)
    dh, right_a, right_b, dob = mlp_back(
        after(dfb, *d_out), h, attn, cot, gain_all, gain_four, own_out, own_up, in_parts, ctx_size, batch
    )
    rights = (right_a, right_b)
    d_out = second_away(g_flip, dmbs, pair_after(d_core, dob))
    d_first = pair_sent(d_out, 4, 2)
    dob = swapped(dob, None)
    gain_part = jnp.sum(dob[:, 0, rows : rows + 8, :].astype(F32), axis=0)
    u_out = first_away(in_flip, pair_after(rights, *d_out))
    u_core = pair_sent(u_out, 1, 1)
    back = ()
    for mb in range(batch):
        back = attend_back(
            after(info, *u_out, *back), docs, mb, qkv, 0, qkv, 1, 2, dob, attended, lse, cos_all,
            sin_all, cos_all, sin_all, back,
        )
        if mb == 0:
            u_out = second_away(in_flip, rights, pair_after(u_core, *back))
            u_first = pair_sent(u_out, 4, 2)
            d_out = third_away(g_flip, dmbs, d_core, pair_after(d_first, *u_out))
            d_second = pair_sent(d_out, 2, 4)
            info = after(info, *d_out)
    dqkv = back[0].reshape(ctx_size, count, 3 * lanes)
    du_keep, du_away, qkv_part = tail_products(dqkv, u_run, w_heads, gain_part)
    u_out = third_away(in_flip, rights, u_core, pair_after(u_first, qkv_part))
    u_second = pair_sent(u_out, 2, 4)
    total = last_total(g_flip, dmbs, d_core, d_first, pair_after(d_second, *u_out))
    d_near = fold_first(total)
    d_near_in = sent(d_near, flips(8))
    du_in = sent(after(du_away, d_near), flips(1))
    q_near = fold_first(after(qkv_part, d_near))
    q_near_in = sent(q_near, flips(8))
    _, y_bit, x_bit, _ = bits()
    kept = summed(du_keep, after(du_in, q_near)).reshape(2, 2, count, width)
    kept = halves(kept)
    out = picked(kept[0], 1 - y_bit, 0), picked(kept[1], 1 - x_bit, 1)
    kept = picked(kept[0], y_bit, 0), picked(kept[1], x_bit, 1)
    got = pair_sent(out, 4, 2)
    u_total = last_total(in_flip, rights, u_core, u_first, pair_after(u_second, *out))
    u_near = fold_first(u_total)
    u_near_in = sent(u_near, flips(8))
    q_next = fold_second(qkv_part, after(q_near_in, u_near))
    q_next_in = sent(q_next, flips(16))
    d_next = fold_second(total, after(d_near_in, q_next))
    d_next_in = sent(d_next, flips(16))
    kept = [summed(*both) for both in zip(kept, pair_after(got, d_next))]
    out = picked(kept[0], 1 - x_bit, 0), picked(kept[1], 1 - y_bit, 0)
    kept = picked(kept[0], x_bit, 0), picked(kept[1], y_bit, 0)
    got = pair_sent(out, 2, 4)
    grad_qkv = fold_last(qkv_part, q_near_in, after(q_next_in, *out))
    size = width // shards
    gain_pair = grad_qkv[size : size + 2, : size // ctx_size].T
    qkv_last = swapped(grad_qkv[:size].reshape(ctx_size, -1, 3 * lanes), None)
    u_next = fold_second(u_total, after(u_near_in, grad_qkv))
    u_next_in = sent(u_next, flips(16))
    grad_tokens = finish_tokens(kept, pair_after(got, u_next), x, dh, gain_all)
    grad_down = fold_last(total, d_near_in, after(d_next_in, grad_tokens))
    grad_in = fold_last(u_total, u_near_in, after(u_next_in, grad_down))
    grad_qkv = after(qkv_last, grad_in)
    grad_out, grad_up = grad_in[:, :width], grad_in[:, width:]

    grad_qkv = grad_qkv.reshape(ctx_size, -1, 3, lanes).transpose(1, 2, 0, 3)
    grad_qkv = grad_qkv.reshape(-1, 3 * width)

    own_gains = picked(gains.reshape(ctx_size, -1, kinds), place, 0).astype(F32)
    row_sum = lambda weight, grad: jnp.sum(
        picked(split(weight), place, 0).astype(F32) * grad, axis=1
    )
    gain_one = row_sum(w_qkv, grad_qkv) / own_gains[:, 0]
    gain_three = row_sum(w_up, grad_up) / own_gains[:, 2]
    grad_gains = jnp.stack([gain_one, gain_pair[:, 0], gain_three, gain_pair[:, 1]], axis=1)
    return (
        layer_out.reshape(batch, rows, width),
        grad_tokens.reshape(batch, rows, width),
        grad_qkv,
        grad_out,
        grad_up,
        grad_down,
        grad_gains,
    )


def per_device(*args):
    return staged(*args) if cube() else plain(*args)


def solution(mesh):
    return jax.shard_map(
        per_device,
        mesh=mesh,
        in_specs=(
            P(None, ALL, None),
            P(None, "shard", None),
            P("shard", None),
            P("shard", None),
            P("shard", None),
            P("shard", None),
            P("shard", None),
            P(None, ALL, None),
        ),
        out_specs=(
            P(None, ALL, None),
            P(None, ALL, None),
            P(ALL, None),
            P(ALL, None),
            P(ALL, None),
            P(ALL, None),
            P(ALL, None),
        ),
        check_vma=False,
    )
```

```python
import functools
import math

import jax
import jax.numpy as jnp
from jax import lax
from jax.experimental import pallas as pl
from jax.experimental.pallas import tpu as pltpu
from jax.sharding import PartitionSpec as P

HEADS = 16
HDIM = 64
EPSILON = 1e-05
ROPE_BASE = 10000.0
MASKED = -1e30
ALL = ("shard", "ctx")
BF = jnp.bfloat16
F32 = jnp.float32
VMEM_LIMIT = 56 * 1024 * 1024
GAIN_ROWS = 16


def layer_norm(values, gain):
    center = jnp.mean(values, axis=-1, keepdims=True)
    shifted = values - center
    spread = jnp.mean(shifted * shifted, axis=-1, keepdims=True)
    return shifted * lax.rsqrt(spread + EPSILON) * gain


def gelu_tanh(values):
    return jax.nn.gelu(values, approximate=True)


def dot(left, right):
    return jnp.dot(left, right, preferred_element_type=F32)


def contract_rows(left, right):
    return lax.dot_general(left, right, (((0,), (0,)), ((), ())), preferred_element_type=F32)


def contract_cols(left, right):
    return lax.dot_general(left, right, (((1,), (1,)), ((), ())), preferred_element_type=F32)


def rope_tables(doc_starts, blocks, rows):
    half = HDIM // 2
    lane = jnp.arange(2 * HDIM, dtype=jnp.int32)
    freqs = ROPE_BASE ** (-(lane % half).astype(F32) / half)
    sign = jnp.where(lane % HDIM < half, -1.0, 1.0).astype(F32)
    positions = jnp.arange(blocks * rows, dtype=jnp.int32).reshape(blocks, 1, rows)
    latest = jnp.zeros((blocks, doc_starts.shape[0], rows), jnp.int32)
    for d in range(doc_starts.shape[1]):
        start = doc_starts[None, :, d, None]
        latest = jnp.where(positions >= start, jnp.maximum(latest, start), latest)
    angles = (positions - latest).astype(F32)[..., None] * freqs
    return jnp.cos(angles), jnp.sin(angles) * sign


def turned(values, cos_row, sin_row):
    width = values.shape[1]
    half = HDIM // 2
    if width == HDIM:
        swapped = jnp.concatenate([values[:, half:], values[:, :half]], axis=1)
    else:
        lane = lax.broadcasted_iota(jnp.int32, values.shape, 1)
        swapped = jnp.where(
            lane % HDIM < half, pltpu.roll(values, width - half, 1), pltpu.roll(values, half, 1)
        )
    return values * cos_row[:, :width] + swapped * sin_row[:, :width]


def project_rows(u, weight, cos_row, sin_row, lanes):
    full = dot(u, weight)
    parts = [full[:, slot * lanes : (slot + 1) * lanes] for slot in range(3)]
    query = turned(parts[0], cos_row, sin_row) * HDIM ** (-0.5)
    return query, turned(parts[1], cos_row, sin_row), parts[2]


def norm_parts(values):
    shifted = values - jnp.mean(values, axis=-1, keepdims=True)
    scale = lax.rsqrt(jnp.mean(shifted * shifted, axis=-1, keepdims=True) + EPSILON)
    return shifted * scale, scale


def norm_back(grad, normed, scale, gain):
    scaled = grad * gain
    return scale * (
        scaled
        - jnp.mean(scaled, axis=-1, keepdims=True)
        - normed * jnp.mean(scaled * normed, axis=-1, keepdims=True)
    )


def project_kernel(
    shards, where, a0, a1, b0, b1, cos_ref, sin_ref, *rest
):
    part_refs, (out_ref, u_ref, w_ref, gain_ref) = rest[:shards], rest[shards:]
    _, _, batch, rows, lanes = out_ref.shape
    count = batch * rows
    size = w_ref.shape[0] // shards

    @pl.when(pl.program_id(0) == 0)
    def _():
        for k, part_ref in enumerate(part_refs):
            at = pl.multiple_of(lax.rem(where[0] - k + shards, shards) * size, size)
            w_ref[pl.ds(at, size), :] = part_ref[:size, :]
            gain_ref[:, pl.ds(at, size)] = part_ref[size:, :size].astype(F32)

    gain = gain_ref[0:1, :]
    for side, (a, b) in enumerate(((a0, b0), (a1, b1))):
        core = where[3] ^ side
        x = jnp.concatenate([a[...], b[...]], axis=1).astype(F32)
        u = (norm_parts(x)[0] * gain).astype(BF)
        u_ref[core] = u
        cos_row = cos_ref[core].reshape(count, -1)
        sin_row = sin_ref[core].reshape(count, -1)
        for slot, part in enumerate(project_rows(u, w_ref[...], cos_row, sin_row, lanes)):
            out_ref[core, slot] = part.reshape(batch, rows, lanes).astype(BF)


def project(parts, weight_parts, cos_all, sin_all):
    a, b = parts[0], parts[2]
    count, half = a.shape[2:]
    shards = len(weight_parts)
    size, columns = weight_parts[0].shape
    width = 2 * half
    kinds = size - width // shards
    lanes = columns // 3
    blocks, batch, rows, _ = cos_all.shape
    a_spec = pl.BlockSpec(
        (None, None, count, half), lambda t, w: ((t // 2) ^ w[1], (t % 2) ^ w[2], 0, 0)
    )
    b_spec = pl.BlockSpec(
        (None, None, count, half), lambda t, w: ((t % 2) ^ w[2], (t // 2) ^ w[1], 0, 0)
    )
    table = pl.BlockSpec((2, batch, rows, 2 * HDIM), lambda t, w: (t, 0, 0, 0))
    whole = lambda shape: pl.BlockSpec(shape, lambda t, w: (0, 0))
    return pl.pallas_call(
        functools.partial(project_kernel, shards),
        out_shape=(
            jax.ShapeDtypeStruct((blocks, 3, batch, rows, lanes), BF),
            jax.ShapeDtypeStruct((blocks, count, width), BF),
            jax.ShapeDtypeStruct((width, columns), BF),
            jax.ShapeDtypeStruct((kinds, width), F32),
        ),
        grid_spec=pltpu.PrefetchScalarGridSpec(
            num_scalar_prefetch=1,
            grid=(4,),
            in_specs=[a_spec, a_spec, b_spec, b_spec, table, table]
            + [whole((size, columns))] * shards,
            out_specs=(
                pl.BlockSpec((2, 3, batch, rows, lanes), lambda t, w: (t, 0, 0, 0, 0)),
                pl.BlockSpec((2, count, width), lambda t, w: (t, 0, 0)),
                whole((width, columns)),
                whole((kinds, width)),
            ),
        ),
        compiler_params=pltpu.CompilerParams(vmem_limit_bytes=VMEM_LIMIT),
        name="project",
    )(where(), *parts, cos_all, sin_all, *weight_parts)


def project_plain(u_run, weight, cos_run, sin_run):
    blocks, batch, rows, _ = cos_run.shape
    lanes = weight.shape[1] // 3
    full = dot(u_run.reshape(-1, weight.shape[0]), weight).reshape(blocks, batch, rows, 3, -1, HDIM)
    half = HDIM // 2
    cosine, sine = (t[..., None, half:HDIM] for t in (cos_run, sin_run))

    def turn(values):
        first, second = values[..., :half], values[..., half:]
        return jnp.concatenate(
            [first * cosine - second * sine, second * cosine + first * sine], axis=-1
        )

    parts = [turn(full[..., 0, :, :]) * HDIM ** (-0.5), turn(full[..., 1, :, :]), full[..., 2, :, :]]
    return jnp.stack([p.reshape(blocks, batch, rows, lanes).astype(BF) for p in parts], axis=1)


def starts_row(info_ref, mb, docs, positions):
    latest = jnp.zeros_like(positions)
    for d in range(docs):
        start = info_ref[mb, d]
        latest = jnp.where(positions >= start, jnp.maximum(latest, start), latest)
    return latest


def start_scalar(info_ref, mb, docs, position):
    latest = jnp.int32(0)
    for d in range(docs):
        start = info_ref[mb, d]
        latest = jnp.where(position >= start, jnp.maximum(latest, start), latest)
    return latest


def attend_kernel(docs, heads, mb, info_ref, q_ref, k_ref, v_ref, *rest):
    o_ref, ob_ref, lse_ref = rest[-3:]
    i = pl.program_id(0)
    per, rows, lanes = q_ref.shape
    block = per * rows
    first = info_ref[mb, docs] + i * block
    low = start_scalar(info_ref, mb, docs, first) // block
    diag = first // block
    q_pos = first + lax.broadcasted_iota(jnp.int32, (1, block), 1)
    q_start = starts_row(info_ref, mb, docs, q_pos)
    q_all = q_ref[...].reshape(block, lanes)
    queries = [q_all[:, h * HDIM : (h + 1) * HDIM] for h in range(heads)]

    def visit(step, state):
        j = diag - step
        k_all = k_ref[pl.ds(j * per, per)].reshape(block, lanes)
        v_flip = v_ref[pl.ds(j * per, per)].reshape(block, lanes).astype(F32).T.astype(BF)
        k_pos = j * block + lax.broadcasted_iota(jnp.int32, (block, 1), 0)
        allowed = (k_pos >= q_start) & (k_pos <= q_pos)
        out = []
        for h in range(heads):
            peak, total, acc = state[h]
            scores = contract_cols(k_all[:, h * HDIM : (h + 1) * HDIM], queries[h])
            scores = jnp.where(allowed, scores, MASKED)
            new_peak = jnp.maximum(peak, jnp.max(scores, axis=0, keepdims=True))
            decay = jnp.exp(peak - new_peak)
            weights = jnp.exp(scores - new_peak)
            total = total * decay + jnp.sum(weights, axis=0, keepdims=True)
            acc = acc * decay + dot(v_flip[h * HDIM : (h + 1) * HDIM], weights.astype(BF))
            out.append((new_peak, total, acc))
        return tuple(out)

    start = tuple(
        (
            jnp.full((1, block), MASKED, F32),
            jnp.zeros((1, block), F32),
            jnp.zeros((HDIM, block), F32),
        )
        for _ in range(heads)
    )
    state = lax.fori_loop(0, diag - low + 1, visit, start)
    flipped = jnp.concatenate([acc / total for _, total, acc in state], axis=0)
    attended = flipped.T
    o_ref[...] = attended.reshape(per, rows, lanes)
    ob_ref[...] = attended.astype(BF).reshape(per, rows, lanes)
    lse_ref[...] = jnp.concatenate([peak + jnp.log(total) for peak, total, _ in state], axis=0)


def attend(info, docs, mb, queries, q_slot, keys, k_slot, v_slot, earlier=()):
    group_count, _, batch, rows, lanes = queries.shape
    blocks_all = keys.shape[0]
    heads = lanes // HDIM
    per = math.gcd(group_count, max(1, 512 // rows))
    q_blocks = group_count // per
    spec = pl.BlockSpec((per, None, None, rows, lanes), lambda i, info: (i, q_slot, mb, 0, 0))
    kv_spec = lambda slot: pl.BlockSpec(
        (blocks_all, None, None, rows, lanes), lambda i, info: (0, slot, mb, 0, 0)
    )
    o_spec = pl.BlockSpec((per, None, rows, lanes), lambda i, info: (i, mb, 0, 0))
    return pl.pallas_call(
        functools.partial(attend_kernel, docs, heads, mb),
        out_shape=(
            jax.ShapeDtypeStruct((group_count, batch, rows, lanes), F32),
            jax.ShapeDtypeStruct((group_count, batch, rows, lanes), BF),
            jax.ShapeDtypeStruct((batch, heads, group_count * rows), F32),
        ),
        grid_spec=pltpu.PrefetchScalarGridSpec(
            num_scalar_prefetch=1,
            grid=(q_blocks,),
            in_specs=[spec, kv_spec(k_slot), kv_spec(v_slot)]
            + [pl.BlockSpec(memory_space=pl.ANY)] * len(earlier),
            out_specs=(
                o_spec,
                o_spec,
                pl.BlockSpec((None, heads, per * rows), lambda i, info: (mb, 0, i)),
            ),
        ),
        input_output_aliases={4 + n: n for n in range(len(earlier))},
        compiler_params=pltpu.CompilerParams(vmem_limit_bytes=VMEM_LIMIT),
        name="attend",
    )(info, queries, keys, keys, *earlier)


def attend_back_kernel(
    docs, heads, per, merged, mb, info_ref, q_ref, k_ref, v_ref, do_ref, o_ref, lse_ref, cosq_ref,
    sinq_ref, cosk_ref, sink_ref, *rest
):
    j = pl.program_id(0)
    out_ref, dq_acc, delta_ref = rest[-3:]
    dq_ref = None if merged else rest[-4]
    group_count, rows, lanes = q_ref.shape
    block = per * rows
    q_blocks = group_count // per
    base = info_ref[mb, docs] // block

    def lanes_of(i):
        return pl.ds(pl.multiple_of(i * block, block), block)

    @pl.when(j == 0)
    def _():
        dq_acc[...] = jnp.zeros_like(dq_acc)

        def fill(i, carry):
            here = pl.ds(i * per, per)
            prod = do_ref[here].reshape(block, lanes).astype(F32) * o_ref[here].reshape(
                block, lanes
            )
            flipped = prod.T
            delta_ref[:, lanes_of(i)] = jnp.concatenate(
                [
                    jnp.sum(flipped[h * HDIM : (h + 1) * HDIM], axis=0, keepdims=True)
                    for h in range(heads)
                ],
                axis=0,
            )
            return carry

        lax.fori_loop(0, q_blocks, fill, 0)

    k_first = j * block
    last = k_first + block - 1
    end = base * block + group_count * rows
    for d in range(docs):
        start = info_ref[mb, d]
        end = jnp.where(start > last, jnp.minimum(end, start), end)
    i_low = jnp.maximum(j - base, 0)
    i_high = jnp.maximum((end - base * block + block - 1) // block, i_low)
    k_pos = k_first + lax.broadcasted_iota(jnp.int32, (block, 1), 0)
    k_all = k_ref[...].reshape(block, lanes)
    v_all = v_ref[...].reshape(block, lanes)
    k_flip = k_all.astype(F32).T.astype(BF)
    heads_of = lambda a: [a[:, h * HDIM : (h + 1) * HDIM] for h in range(heads)]
    k_heads, v_heads = heads_of(k_all), heads_of(v_all)

    def visit(i, state):
        here = pl.ds(i * per, per)
        q_heads = heads_of(q_ref[here].reshape(block, lanes))
        do_heads = heads_of(do_ref[here].reshape(block, lanes))
        q_pos = (base + i) * block + lax.broadcasted_iota(jnp.int32, (1, block), 1)
        q_start = starts_row(info_ref, mb, docs, q_pos)
        allowed = (k_pos >= q_start) & (k_pos <= q_pos)
        lse = lse_ref[:, lanes_of(i)]
        delta = delta_ref[:, lanes_of(i)]
        out = []
        for h in range(heads):
            dk, dv = state[h]
            scores = contract_cols(k_heads[h], q_heads[h])
            weights = jnp.exp(jnp.where(allowed, scores - lse[h : h + 1], MASKED))
            grad_weights = contract_cols(v_heads[h], do_heads[h])
            grad_scores = (weights * (grad_weights - delta[h : h + 1])).astype(BF)
            dv = dv + dot(weights.astype(BF), do_heads[h])
            dk = dk + dot(grad_scores, q_heads[h])
            at = slice(h * HDIM, (h + 1) * HDIM)
            dq_acc[at, lanes_of(i)] += dot(k_flip[at], grad_scores)
            out.append((dk, dv))
        return tuple(out)

    zero = jnp.zeros((block, HDIM), F32)
    state = lax.fori_loop(i_low, i_high, visit, tuple((zero, zero) for _ in range(heads)))
    dk = jnp.concatenate([dk for dk, _ in state], axis=1) if heads > 1 else state[0][0]
    dv = jnp.concatenate([dv for _, dv in state], axis=1) if heads > 1 else state[0][1]
    dk = turned(dk, cosk_ref[...].reshape(block, -1), -sink_ref[...].reshape(block, -1))
    there = pl.ds(j * per, per)
    first = lanes if merged else 0
    out_ref[there, :, first : first + lanes] = dk.reshape(per, rows, lanes).astype(out_ref.dtype)
    out_ref[there, :, first + lanes : first + 2 * lanes] = dv.reshape(per, rows, lanes).astype(
        out_ref.dtype
    )

    @pl.when(j == pl.num_programs(0) - 1)
    def _():
        def finish(i, carry):
            dq = dq_acc[:, lanes_of(i)].T
            at = pl.ds(i * per, per)
            cos_row = cosq_ref[at].reshape(block, -1)
            sin_row = sinq_ref[at].reshape(block, -1)
            dq = turned(dq, cos_row, -sin_row) * HDIM ** (-0.5)
            dq = dq.reshape(per, rows, lanes).astype(BF)
            if merged:
                out_ref[at, :, :lanes] = dq
            else:
                dq_ref[at] = dq
            return carry

        lax.fori_loop(0, q_blocks, finish, 0)


def attend_back(info, docs, mb, queries, q_slot, keys, k_slot, v_slot, grad, attended, lse,
                cos_all, sin_all, cos_here, sin_here, earlier=()):
    group_count, _, batch, rows, lanes = queries.shape
    blocks_all = keys.shape[0]
    merged = blocks_all == group_count
    heads = lanes // HDIM
    per = math.gcd(group_count, max(1, 512 // rows))
    length = group_count * rows
    full = pl.BlockSpec(
        (group_count, None, None, rows, lanes), lambda j, info: (0, q_slot, mb, 0, 0)
    )
    part = lambda slot: pl.BlockSpec(
        (per, None, None, rows, lanes), lambda j, info: (j, slot, mb, 0, 0)
    )
    rows_of_mb = lambda count, width: pl.BlockSpec(
        (count, None, rows, width), lambda j, info: (0, mb, 0, 0)
    )
    table_k = pl.BlockSpec((per, None, rows, 2 * HDIM), lambda j, info: (j, mb, 0, 0))
    if merged:
        out_shape = [jax.ShapeDtypeStruct((group_count, batch, rows, 3 * lanes), BF)]
        out_specs = [rows_of_mb(group_count, 3 * lanes)]
    else:
        out_shape = [
            jax.ShapeDtypeStruct((group_count, batch, rows, lanes), BF),
            jax.ShapeDtypeStruct((blocks_all, batch, rows, 2 * lanes), F32),
        ]
        out_specs = [rows_of_mb(group_count, lanes), rows_of_mb(blocks_all, 2 * lanes)]
    table_q = rows_of_mb(group_count, 2 * HDIM)
    return pl.pallas_call(
        functools.partial(attend_back_kernel, docs, heads, per, merged, mb),
        out_shape=out_shape,
        grid_spec=pltpu.PrefetchScalarGridSpec(
            num_scalar_prefetch=1,
            grid=(blocks_all // per,),
            in_specs=[
                full, part(k_slot), part(v_slot), rows_of_mb(group_count, lanes),
                rows_of_mb(group_count, lanes),
                pl.BlockSpec((None, heads, length), lambda j, info: (mb, 0, 0)),
                table_q, table_q, table_k, table_k,
            ]
            + [pl.BlockSpec(memory_space=pl.ANY)] * len(earlier),
            out_specs=out_specs,
            scratch_shapes=[pltpu.VMEM((lanes, length), F32), pltpu.VMEM((heads, length), F32)],
        ),
        input_output_aliases={11 + n: n for n in range(len(earlier))},
        compiler_params=pltpu.CompilerParams(vmem_limit_bytes=VMEM_LIMIT),
        name="attend_back",
    )(info, queries, keys, keys, grad, attended, lse, cos_here, sin_here, cos_all, sin_all,
      *earlier)


def flips(mask):
    count = lax.axis_size("shard") * lax.axis_size("ctx")
    return [(i, i ^ mask) for i in range(count)]


def turns(by):
    shards, places = lax.axis_size("shard"), lax.axis_size("ctx")
    return [
        (a * places + b, ((a + by) % shards) * places + b)
        for a in range(shards)
        for b in range(places)
    ]


def sent(values, pairs):
    return lax.ppermute(values, ALL, pairs)


def picked(values, index, axis):
    return lax.dynamic_index_in_dim(values, index, axis, keepdims=False)


def cube():
    return lax.axis_size("ctx") == 8 and lax.axis_size("shard") == 4


def bits():
    place = lax.axis_index("ctx")
    return lax.axis_index("shard"), place // 4, place // 2 % 2, place % 2


def where():
    return jnp.stack(bits()).astype(jnp.int32)


def spread(values, early, late):
    half = values.shape[1] // 2
    a, b = values[:, :half], values[:, half:]
    a_in, b_in = sent(a, flips(2)), sent(b, flips(4))
    a, b = jnp.stack([a, after(a_in, *early)]), jnp.stack([b, after(b_in, *early)])
    a = jnp.stack([a, after(sent(a, flips(4)), *late)])
    b = jnp.stack([b, after(sent(b, flips(2)), *late)])
    return a, sent(a, flips(1)), b, sent(b, flips(1))


def ring_parts(values):
    shards = lax.axis_size("shard")
    z = lax.axis_index("shard")
    return [picked(values, lax.rem(z + k, shards), 0) for k in range(shards)]


def ring_sent(parts):
    return [sent(part, turns(k)) for k, part in enumerate(parts) if k]


def ring_total(own, received):
    total = own.astype(F32)
    for part in received:
        total = total + part.astype(F32)
    return total


def fold_first(values):
    low = lax.axis_index("shard") % 2
    return picked(values.reshape(2, 2, *values.shape[1:]), 1 - low, 1)


def fold_second(values, received):
    z = lax.axis_index("shard")
    mine = picked(values.reshape(2, 2, *values.shape[1:]), z % 2, 1)
    return summed(picked(mine, 1 - z // 2, 0), picked(received, 1 - z // 2, 0))


def fold_last(values, received, last):
    z = lax.axis_index("shard")
    parts = picked(values, z, 0), picked(received, z // 2, 0), last
    return sum(part.astype(F32) for part in parts)


def after(values, *earlier):
    return lax.optimization_barrier((values,) + earlier)[0]


def far_rows(piece, *earlier):
    shards = lax.axis_size("shard")
    return jnp.stack([after(sent(piece, turns(k)), *earlier) for k in range(1, shards)])


def copies_in(where, owns, parts, out_ref, sem):
    z, y, x, c = (where[i] for i in range(4))
    shards = out_ref.shape[0]
    half = parts[0].shape[-1]
    groups = [[] for _ in range(shards)]

    def add(k, source, target):
        at = sum(len(group) for group in groups)
        groups[k].append(pltpu.make_async_copy(source, target, sem.at[at]))

    first = 0
    for own in owns:
        add(0, own, out_ref.at[z, :, :, pl.ds(first, own.shape[-1])])
        first += own.shape[-1]
    for k in range(1, shards):
        source = lax.rem(z - k + shards, shards)
        for side in range(2):
            a, b = parts[side], parts[2 + side]
            core = c ^ side
            for p in range(2):
                for q in range(2):
                    at_a = ((y ^ p) * 2 + (x ^ q)) * 2 + core
                    at_b = ((y ^ q) * 2 + (x ^ p)) * 2 + core
                    add(k, a.at[p, q, k - 1], out_ref.at[source, at_a, :, pl.ds(0, half)])
                    add(k, b.at[p, q, k - 1], out_ref.at[source, at_b, :, pl.ds(half, half)])
    for group in groups:
        for copy in group:
            copy.start()
    return groups


def arrived(groups, where):
    shards = len(groups)
    for k, group in enumerate(groups):
        for copy in group:
            copy.wait()
        yield lax.rem(where[0] - k + shards, shards)


def copy_count(shards, owns):
    return owns + 16 * (shards - 1)


def rows_of(w, first, last):
    part = w[:, :, :, first:last]
    return part.reshape(-1, last - first)


def chunk_of(w, z, first, last):
    part = w[z, :, :, first:last]
    return part.reshape(-1, last - first)


def block_at(z, size):
    return pl.ds(pl.multiple_of(z * size, size), size)


def flip_pieces(values, size, out_ref, first):
    tokens, rows = values.shape
    step = max(size, 128)
    for start in range(0, rows, step):
        flip = values[:, start : start + step].astype(F32).T.astype(BF)
        for low in range(0, step, size):
            piece = (start + low) // size
            z, y, x, c = piece // 8, piece // 4 % 2, piece // 2 % 2, piece % 2
            out_ref[c, y, x, z, :, first : first + tokens] = flip[low : low + size]


def mlp_in_kernel(
    where, ob_ref, x_ref, gain_ref, own_out, own_up, a0, a1, b0, b1,
    a_ref, h_ref, g_ref, slope_ref, in_flip, g_flip, w, obl, sem
):
    copies = copies_in(where, (own_out, own_up), (a0, a1, b0, b1), w, sem)
    groups, batch, rows, lanes = ob_ref.shape
    shards = w.shape[0]
    width = x_ref.shape[1]
    count = batch * rows
    size = width // shards
    for mb in range(batch):
        for g in range(groups):
            obl[mb * rows : (mb + 1) * rows, g * lanes : (g + 1) * lanes] = ob_ref[g, mb]
    flip_pieces(obl[...], size // 8, in_flip, count)
    a = None
    for z in arrived(copies, where):
        part = dot(obl[:, block_at(z, size)], chunk_of(w, z, 0, width))
        a = part if a is None else a + part
    a_ref[...] = a
    h = x_ref[...].astype(F32) + norm_parts(a)[0] * gain_ref[1:2, :]
    h_ref[...] = h
    u2 = (norm_parts(h)[0] * gain_ref[2:3, :]).astype(BF)
    flip_pieces(u2, size // 8, in_flip, 0)
    hidden = g_ref.shape[1]
    step = 512
    root = math.sqrt(2.0 / math.pi)
    for first in range(0, hidden, step):
        f = dot(u2, rows_of(w, width + first, width + first + step))
        square = f * f
        bent = jnp.tanh(root * (f + 0.044715 * (square * f)))
        half = 0.5 * (1.0 + bent)
        at = slice(first, first + step)
        g_ref[:, at] = (f * half).astype(BF)
        slope = half + 0.5 * f * (1.0 - bent * bent) * (root * (1.0 + 3 * 0.044715 * square))
        slope_ref[:, at] = slope.astype(BF)
    flip_pieces(g_ref[...], hidden // (8 * shards), g_flip, 0)


def mlp_in(ob, x, gain_all, w_out, w_up, parts):
    shards = lax.axis_size("shard")
    count, width = x.shape
    hidden = w_up.shape[-1]
    pieces, rows = w_out.shape[:2]
    anywhere = pl.BlockSpec(memory_space=pl.ANY)
    local = pl.BlockSpec(memory_space=pltpu.VMEM)
    shape = jax.ShapeDtypeStruct
    return pl.pallas_call(
        mlp_in_kernel,
        out_shape=(
            shape((count, width), F32),
            shape((count, width), F32),
            shape((count, hidden), BF),
            shape((count, hidden), BF),
            shape((2, 2, 2, shards, width // (8 * shards), 2 * count), BF),
            shape((2, 2, 2, shards, hidden // (8 * shards), count), BF),
        ),
        grid_spec=pltpu.PrefetchScalarGridSpec(
            num_scalar_prefetch=1,
            grid=(),
            in_specs=[local] * 3 + [anywhere] * 6,
            out_specs=[local] * 6,
            scratch_shapes=[
                pltpu.VMEM((shards, pieces, rows, width + hidden), BF),
                pltpu.VMEM((count, width), BF),
                pltpu.SemaphoreType.DMA((copy_count(shards, 2),)),
            ],
        ),
        compiler_params=pltpu.CompilerParams(vmem_limit_bytes=VMEM_LIMIT),
        name="mlp_in",
    )(where(), ob, x, gain_all, w_out, w_up, *parts)


def mlp_out_kernel(
    where, g_ref, slope_ref, h_ref, cot_ref, gain_ref, own, a0, a1, b0, b1,
    out_ref, dmb_ref, dfb_ref, gg_ref, w, sem
):
    copies = copies_in(where, (own,), (a0, a1, b0, b1), w, sem)
    shards = w.shape[0]
    width = h_ref.shape[1]
    size = g_ref.shape[1] // shards
    m = None
    for z in arrived(copies, where):
        part = dot(g_ref[:, block_at(z, size)], chunk_of(w, z, 0, width))
        m = part if m is None else m + part
    gain = gain_ref[3:4, :]
    normed, scale = norm_parts(m)
    out_ref[...] = (h_ref[...] + normed * gain).astype(BF)
    dy = cot_ref[...].astype(F32)
    gg_ref[...] = jnp.sum(dy * normed, axis=0, keepdims=True)
    dmb = norm_back(dy, normed, scale, gain).astype(BF)
    dmb_ref[...] = dmb
    for z in range(shards):
        at = slice(z * size, (z + 1) * size)
        dg = contract_cols(dmb, chunk_of(w, z, 0, width))
        dfb_ref[:, at] = (dg * slope_ref[:, at].astype(F32)).astype(BF)


def mlp_out(g, slope, h, cot, gain_all, w_down, parts):
    shards = lax.axis_size("shard")
    count, width = h.shape
    hidden = g.shape[1]
    pieces, rows = w_down.shape[:2]
    anywhere = pl.BlockSpec(memory_space=pl.ANY)
    local = pl.BlockSpec(memory_space=pltpu.VMEM)
    shape = jax.ShapeDtypeStruct
    return pl.pallas_call(
        mlp_out_kernel,
        out_shape=(
            shape((count, width), BF),
            shape((count, width), BF),
            shape((count, hidden), BF),
            shape((1, width), F32),
        ),
        grid_spec=pltpu.PrefetchScalarGridSpec(
            num_scalar_prefetch=1,
            grid=(),
            in_specs=[local] * 5 + [anywhere] * 5,
            out_specs=[local] * 4,
            scratch_shapes=[
                pltpu.VMEM((shards, pieces, rows, width), BF),
                pltpu.SemaphoreType.DMA((copy_count(shards, 1),)),
            ],
        ),
        compiler_params=pltpu.CompilerParams(vmem_limit_bytes=VMEM_LIMIT),
        name="mlp_out",
    )(where(), g, slope, h, cot, gain_all, w_down, *parts)


def mlp_back_kernel(
    where, dfb_ref, h_ref, a_ref, cot_ref, gain_ref, gain_four_ref, own_out, own_up, a0, a1, b0, b1,
    dh_ref, right_a, right_b, dob_ref, w, du2, sem
):
    copies = copies_in(where, (own_out, own_up), (a0, a1, b0, b1), w, sem)
    shards = w.shape[0]
    count, width = h_ref.shape
    size = width // shards
    groups, batch, rows, lanes = dob_ref.shape
    rows -= GAIN_ROWS
    last = w.shape[-1]
    middle = last // 2
    right_a[:count, :width] = jnp.zeros((count, width), BF)
    right_a[count:, width:] = jnp.zeros((count, middle - width), BF)
    right_a[:count, width:] = dfb_ref[:, : middle - width]
    right_b[count:, :] = jnp.zeros((count, middle), BF)
    right_b[:count, :] = dfb_ref[:, middle - width :]
    for z in arrived(copies, where):
        du2[:, block_at(z, size)] = contract_cols(dfb_ref[...], chunk_of(w, z, width, last))
    normed, scale = norm_parts(h_ref[...])
    dh = cot_ref[...].astype(F32) + norm_back(du2[...], normed, scale, gain_ref[2:3, :])
    dh_ref[...] = dh
    normed, scale = norm_parts(a_ref[...])
    gains = (jnp.sum(dh * normed, axis=0, keepdims=True), gain_four_ref[...])
    step = lanes // shards
    blank = jnp.zeros((GAIN_ROWS - len(gains), lanes), F32)
    for g in range(groups):
        lines = [
            jnp.concatenate(
                [line[:, z * size + g * step : z * size + (g + 1) * step] for z in range(shards)],
                axis=1,
            )
            for line in gains
        ]
        block = jnp.concatenate(lines + [blank], axis=0).astype(BF)
        for mb in range(batch):
            dob_ref[g, mb, rows:, :] = block
    dab = norm_back(dh, normed, scale, gain_ref[1:2, :]).astype(BF)
    right_a[count:, :width] = dab
    for z in range(shards):
        dob = contract_cols(dab, chunk_of(w, z, 0, width)).astype(BF)
        for part in range(size // lanes):
            for mb in range(batch):
                dob_ref[z * (size // lanes) + part, mb, :rows] = dob[
                    mb * rows : (mb + 1) * rows, part * lanes : (part + 1) * lanes
                ]


def mlp_back(dfb, h, a, cot, gain_all, gain_four, w_out, w_up, parts, groups, batch):
    shards = lax.axis_size("shard")
    count, width = h.shape
    hidden = dfb.shape[1]
    pieces, rows = w_out.shape[:2]
    anywhere = pl.BlockSpec(memory_space=pl.ANY)
    local = pl.BlockSpec(memory_space=pltpu.VMEM)
    shape = jax.ShapeDtypeStruct
    return pl.pallas_call(
        mlp_back_kernel,
        out_shape=(
            shape((count, width), F32),
            shape((2 * count, (width + hidden) // 2), BF),
            shape((2 * count, (width + hidden) // 2), BF),
            shape((groups, batch, count // batch + GAIN_ROWS, width // groups), BF),
        ),
        grid_spec=pltpu.PrefetchScalarGridSpec(
            num_scalar_prefetch=1,
            grid=(),
            in_specs=[local] * 6 + [anywhere] * 6,
            out_specs=[local] * 4,
            scratch_shapes=[
                pltpu.VMEM((shards, pieces, rows, width + hidden), BF),
                pltpu.VMEM((count, width), F32),
                pltpu.SemaphoreType.DMA((copy_count(shards, 2),)),
            ],
        ),
        compiler_params=pltpu.CompilerParams(vmem_limit_bytes=VMEM_LIMIT),
        name="mlp_back",
    )(where(), dfb, h, a, cot, gain_all, gain_four, w_out, w_up, *parts)


def tail_kernel(where, dqkv_ref, u_ref, w_ref, gain_ref, keep_ref, away_ref, grad_ref):
    core = where[3]
    shards = grad_ref.shape[0]
    size = w_ref.shape[0] // shards
    step = gain_ref.shape[1] // shards
    total = None
    for pair in range(dqkv_ref.shape[0] // 2):
        for side, out_ref in enumerate((keep_ref, away_ref)):
            block = 2 * pair + (core ^ side)
            dqkv = dqkv_ref[block]
            out_ref[pair] = contract_cols(dqkv, w_ref[...]).astype(BF)
            part = dot(dqkv.astype(F32).T.astype(BF), u_ref[block])
            total = part if total is None else total + part
    blank = jnp.zeros((gain_ref.shape[0], grad_ref.shape[2] - step), F32)
    for z in range(shards):
        grad_ref[z, :size] = total[:, z * size : (z + 1) * size].T.astype(BF)
        gains = gain_ref[:, z * step : (z + 1) * step]
        grad_ref[z, size:] = jnp.concatenate([gains, blank], axis=1).astype(BF)


def tail_products(dqkv, u_run, w_heads, gain_part):
    blocks, count, columns = dqkv.shape
    width = w_heads.shape[0]
    shards = lax.axis_size("shard")
    local = pl.BlockSpec(memory_space=pltpu.VMEM)
    rows = jax.ShapeDtypeStruct((blocks // 2, count, width), BF)
    return pl.pallas_call(
        tail_kernel,
        out_shape=(
            rows,
            rows,
            jax.ShapeDtypeStruct((shards, width // shards + gain_part.shape[0], columns), BF),
        ),
        grid_spec=pltpu.PrefetchScalarGridSpec(
            num_scalar_prefetch=1, grid=(), in_specs=[local] * 4, out_specs=[local] * 3
        ),
        compiler_params=pltpu.CompilerParams(vmem_limit_bytes=VMEM_LIMIT),
        name="tail_products",
    )(where(), dqkv, u_run, w_heads, gain_part)


def finish_kernel(keep_a, keep_b, got_a, got_b, x_ref, dh_ref, gain_ref, out_ref):
    parts = ((keep_a, got_a), (keep_b, got_b))
    du = jnp.concatenate([k[...].astype(F32) + g[...].astype(F32) for k, g in parts], axis=1)
    normed, scale = norm_parts(x_ref[...].astype(F32))
    out_ref[...] = dh_ref[...] + norm_back(du, normed, scale, gain_ref[0:1, :])


def finish_tokens(kept, got, x, dh, gain_all):
    local = pl.BlockSpec(memory_space=pltpu.VMEM)
    return pl.pallas_call(
        finish_kernel,
        out_shape=jax.ShapeDtypeStruct(x.shape, F32),
        in_specs=[local] * 7,
        out_specs=local,
        compiler_params=pltpu.CompilerParams(vmem_limit_bytes=VMEM_LIMIT),
        name="finish_tokens",
    )(*kept, *got, x, dh, gain_all)


def product(left, right, *addends):
    total = dot(left.reshape(-1, left.shape[-1]), right)
    total = total.reshape(*left.shape[:-1], right.shape[1])
    for addend in addends:
        total = total + addend.astype(F32)
    return total.astype(BF)


def halves(values):
    half = values.shape[-1] // 2
    return values[..., :half], values[..., half:]


def at(values, y, x):
    return picked(picked(values, y, 0), x, 0)


def first_away(left, rights):
    left = picked(left, 1 - bits()[3], 0)
    return [product(left, right) for right in rights]


def second_away(left, rights, core_in):
    _, y, x, c = bits()
    left = picked(left, c, 0)
    return (
        product(picked(left, 1 - y, 0), rights[0], picked(core_in[0], 1 - y, 0)),
        product(picked(left, 1 - x, 1), rights[1], picked(core_in[1], 1 - x, 1)),
    )


def third_away(left, rights, core_in, first_in):
    _, y, x, c = bits()
    left = picked(left, c, 0)
    return (
        product(
            at(left, y, 1 - x), rights[0], at(core_in[0], y, 1 - x), picked(first_in[0], 1 - x, 0)
        ),
        product(
            at(left, 1 - y, x), rights[1], at(core_in[1], 1 - y, x), picked(first_in[1], 1 - y, 0)
        ),
    )


def last_total(left, rights, core_in, first_in, second_in):
    _, y, x, c = bits()
    left = at(picked(left, c, 0), y, x)
    own = (x, y)
    parts = [
        product(left, rights[n], at(core_in[n], y, x), picked(first_in[n], own[n], 0), second_in[n])
        for n in range(2)
    ]
    return jnp.concatenate(parts, axis=-1)


def pair_sent(parts, first, second):
    return sent(parts[0], flips(first)), sent(parts[1], flips(second))


def pair_after(parts, *earlier):
    return tuple(after(part, *earlier) for part in parts)


def summed(left, right):
    return (left.astype(F32) + right.astype(F32)).astype(BF)


def gathered(weight):
    size = weight.shape[0] // lax.axis_size("ctx")
    piece = lax.dynamic_slice_in_dim(weight, lax.axis_index("ctx") * size, size, 0)
    return lax.all_gather(piece, ALL, axis=0, tiled=True)


def scattered(left, right):
    total = contract_rows(left, right).astype(BF)
    return lax.psum_scatter(total, ALL, scatter_dimension=0, tiled=True).astype(F32)


def scattered_gains(grads):
    count = lax.axis_size("shard") * lax.axis_size("ctx")
    kinds = grads.shape[0]
    parts = grads.reshape(kinds, count, -1).transpose(1, 0, 2)
    parts = lax.all_to_all(parts, ALL, split_axis=0, concat_axis=0, tiled=True)
    return jnp.sum(parts, axis=0).T


def swapped(values, groups):
    return lax.all_to_all(
        values, "ctx", split_axis=0, concat_axis=0, tiled=True, axis_index_groups=groups
    )


def plain(tokens, doc_starts, w_qkv, w_out, w_up, w_down, gains, cotangent):
    ctx_size = lax.axis_size("ctx")
    place = lax.axis_index("ctx")
    batch, rows, width = tokens.shape
    count = batch * rows
    docs = doc_starts.shape[2]
    group_count = math.gcd(HEADS, ctx_size)
    runs = ctx_size // group_count
    if runs == 1:
        near = far = None
    else:
        near = [[r * group_count + g for g in range(group_count)] for r in range(runs)]
        far = [[r * group_count + g for r in range(runs)] for g in range(group_count)]
    lanes = width // group_count

    gain_all = lax.all_gather(gains, "shard", axis=0, tiled=True).T.astype(F32)
    columns = picked(w_qkv.reshape(-1, 3, group_count, lanes), lax.rem(place, group_count), 2)
    w_heads = lax.all_gather(columns.reshape(-1, 3 * lanes), "shard", axis=0, tiled=True)
    full_out, full_up, full_down = gathered(w_out), gathered(w_up), gathered(w_down)

    starts = doc_starts[:, 0, :]
    cos_all, sin_all = rope_tables(starts, ctx_size, rows)
    run_first = (place // group_count) * group_count
    info = jnp.concatenate(
        [starts, jnp.broadcast_to(run_first * rows, (batch, 1)).astype(jnp.int32)], axis=1
    )

    x = tokens.reshape(count, width).astype(F32)
    out_grad = cotangent.reshape(count, width).astype(F32)
    normed, norm_one_back = jax.vjp(layer_norm, x, gain_all[0])
    u = normed.astype(BF)
    cos_here, sin_here = (
        lax.dynamic_slice_in_dim(t, run_first, group_count, 0) for t in (cos_all, sin_all)
    )
    u_run = lax.all_gather(u, "ctx", axis=0, axis_index_groups=near)
    qkv = project_plain(u_run, w_heads, cos_here, sin_here)
    if runs == 1:
        keys, k_slot = qkv, 1
    else:
        keys, k_slot = (
            lax.all_gather(qkv[:, 1:], "ctx", axis=0, tiled=True, axis_index_groups=far),
            0,
        )
    held = ()
    for mb in range(batch):
        held = attend(info, docs, mb, qkv, 0, keys, k_slot, k_slot + 1, held)
    attended, attended_low, lse = held
    ob = swapped(attended_low, near).transpose(1, 2, 0, 3).reshape(count, width)
    attn_proj = dot(ob, full_out)
    attn_branch, norm_two_back = jax.vjp(layer_norm, attn_proj, gain_all[1])
    hidden = x + attn_branch
    normed_two, norm_three_back = jax.vjp(layer_norm, hidden, gain_all[2])
    u2 = normed_two.astype(BF)
    up_proj = dot(u2, full_up)
    activated, gelu_back = jax.vjp(gelu_tanh, up_proj)
    g = activated.astype(BF)
    down_proj = dot(g, full_down)
    mlp_branch, norm_four_back = jax.vjp(layer_norm, down_proj, gain_all[3])
    layer_out = (hidden + mlp_branch).astype(BF)

    down_grad, gain_four = norm_four_back(out_grad)
    dmb = down_grad.astype(BF)
    grad_down = scattered(g, dmb)
    (up_grad,) = gelu_back(contract_cols(dmb, full_down))
    dfb = up_grad.astype(BF)
    grad_up = scattered(u2, dfb)
    hidden_add, gain_three = norm_three_back(contract_cols(dfb, full_up))
    dh = out_grad + hidden_add
    attn_grad, gain_two = norm_two_back(dh)
    dab = attn_grad.astype(BF)
    grad_out = scattered(ob, dab)
    dob = contract_cols(dab, full_out).astype(BF)
    dob = swapped(dob.reshape(batch, rows, group_count, lanes).transpose(2, 0, 1, 3), near)
    back = ()
    for mb in range(batch):
        back = attend_back(
            info, docs, mb, qkv, 0, keys, k_slot, k_slot + 1, dob, attended, lse, cos_all, sin_all,
            cos_here, sin_here, back,
        )
    if runs == 1:
        dqkv = back[0]
    else:
        dkv = lax.psum_scatter(
            back[1], "ctx", scatter_dimension=0, tiled=True, axis_index_groups=far
        )
        dqkv = jnp.concatenate([back[0], dkv.astype(BF)], axis=-1)
    dqkv = dqkv.reshape(group_count * count, 3 * lanes)
    du = contract_cols(dqkv, w_heads)
    qkv_part = contract_rows(u_run.reshape(group_count * count, width), dqkv)
    du = lax.psum_scatter(du, "ctx", scatter_dimension=0, tiled=True, axis_index_groups=near)
    own = jnp.zeros((width, 3, group_count, lanes), F32)
    own = lax.dynamic_update_slice_in_dim(
        own, qkv_part.reshape(width, 3, 1, lanes), lax.rem(place, group_count), 2
    )
    grad_qkv = lax.psum_scatter(
        own.reshape(width, 3 * width), ALL, scatter_dimension=0, tiled=True
    )
    input_add, gain_one = norm_one_back(du)
    grad_tokens = dh + input_add
    grad_gains = scattered_gains(jnp.stack([gain_one, gain_two, gain_three, gain_four]))
    return (
        layer_out.reshape(batch, rows, width),
        grad_tokens.reshape(batch, rows, width),
        grad_qkv,
        grad_out,
        grad_up,
        grad_down,
        grad_gains,
    )


def staged(tokens, doc_starts, w_qkv, w_out, w_up, w_down, gains, cotangent):
    ctx_size, shards = lax.axis_size("ctx"), lax.axis_size("shard")
    place = lax.axis_index("ctx")
    batch, rows, width = tokens.shape
    count = batch * rows
    docs = doc_starts.shape[2]
    lanes = width // ctx_size
    kinds = gains.shape[1]
    x = tokens.reshape(count, width)
    cot = cotangent.reshape(count, width)
    split = lambda w: w.reshape(ctx_size, -1, w.shape[1])
    own_out, own_up, own_down = split(w_out), split(w_up), split(w_down)

    starts = doc_starts[:, 0, :]
    cos_all, sin_all = rope_tables(starts, ctx_size, rows)
    columns = picked(w_qkv.reshape(-1, 3, ctx_size, lanes), place, 2).reshape(-1, 3 * lanes)
    gain_rows = jnp.pad(gains.T, ((0, 8 - kinds), (0, 3 * lanes - gains.shape[0])))
    piece = jnp.concatenate([columns, gain_rows])
    head_parts = [piece] + [sent(piece, turns(k)) for k in range(1, shards)]

    piece = jnp.concatenate([picked(own_out, place, 0), picked(own_up, place, 0)], axis=1)
    piece = after(piece, cos_all, sin_all, *head_parts)
    far_in = [sent(piece, turns(k)) for k in range(1, shards)]
    x_parts = spread(x, (cos_all, sin_all, *head_parts[1:]), (far_in[0], far_in[-1]))

    info = jnp.concatenate([starts, jnp.zeros((batch, 1), jnp.int32)], axis=1)
    qkv, u_run, w_heads, gain_all = project(x_parts, head_parts, cos_all, sin_all)

    far_in = jnp.stack([after(part, qkv) for part in far_in])
    piece_out = after(picked(own_down, place, 0), far_in)
    half = far_in.shape[2] // 2
    a, b = far_in[:, :, :half], far_in[:, :, half:]
    a_in, b_in = sent(a, flips(2)), sent(b, flips(4))
    held = ()
    for mb in range(batch):
        held = attend(after(info, far_in, *held), docs, mb, qkv, 0, qkv, 1, 2, held)
        if mb == 0:
            a, b = jnp.stack([a, after(a_in, held[2])]), jnp.stack([b, after(b_in, held[2])])
            info = after(info, a, b)
    attended, attended_low, lse = held
    a_in, b_in = sent(a, flips(4)), sent(b, flips(2))
    ob = swapped(attended_low, None)
    far_out = far_rows(piece_out, lse)
    half = far_out.shape[2] // 2
    c, d = far_out[:, :, :half], far_out[:, :, half:]
    c_in, d_in = sent(c, flips(2)), sent(d, flips(4))
    a, b = jnp.stack([a, after(a_in, c, d, ob)]), jnp.stack([b, after(b_in, c, d, ob)])
    in_parts = (a, sent(a, flips(1)), b, sent(b, flips(1)))
    c, d = jnp.stack([c, after(c_in, a, b, ob)]), jnp.stack([d, after(d_in, a, b, ob)])
    c_in, d_in = sent(c, flips(4)), sent(d, flips(2))

    attn, h, g, slope, in_flip, g_flip = mlp_in(
        after(ob, c, d), x, gain_all, own_out, own_up, in_parts
    )
    c, d = jnp.stack([c, after(c_in, h)]), jnp.stack([d, after(d_in, h)])
    out_parts = (c, sent(c, flips(1)), d, sent(d, flips(1)))
    layer_out, dmb, dfb, gain_four = mlp_out(g, slope, h, cot, gain_all, own_down, out_parts)

    dmbs = halves(dmb)
    d_out = first_away(g_flip, dmbs)
    d_core = pair_sent(d_out, 1, 1)
    dh, right_a, right_b, dob = mlp_back(
        after(dfb, *d_out), h, attn, cot, gain_all, gain_four, own_out, own_up, in_parts, ctx_size, batch
    )
    rights = (right_a, right_b)
    d_out = second_away(g_flip, dmbs, pair_after(d_core, dob))
    d_first = pair_sent(d_out, 4, 2)
    dob = swapped(dob, None)
    gain_part = jnp.sum(dob[:, 0, rows : rows + 8, :].astype(F32), axis=0)
    u_out = first_away(in_flip, pair_after(rights, *d_out))
    u_core = pair_sent(u_out, 1, 1)
    back = ()
    for mb in range(batch):
        back = attend_back(
            after(info, *u_out, *back), docs, mb, qkv, 0, qkv, 1, 2, dob, attended, lse, cos_all,
            sin_all, cos_all, sin_all, back,
        )
        if mb == 0:
            u_out = second_away(in_flip, rights, pair_after(u_core, *back))
            u_first = pair_sent(u_out, 4, 2)
            d_out = third_away(g_flip, dmbs, d_core, pair_after(d_first, *u_out))
            d_second = pair_sent(d_out, 2, 4)
            info = after(info, *d_out)
    dqkv = back[0].reshape(ctx_size, count, 3 * lanes)
    du_keep, du_away, qkv_part = tail_products(dqkv, u_run, w_heads, gain_part)
    u_out = third_away(in_flip, rights, u_core, pair_after(u_first, qkv_part))
    u_second = pair_sent(u_out, 2, 4)
    total = last_total(g_flip, dmbs, d_core, d_first, pair_after(d_second, *u_out))
    d_near = fold_first(total)
    d_near_in = sent(d_near, flips(8))
    du_in = sent(after(du_away, d_near), flips(1))
    q_near = fold_first(after(qkv_part, d_near))
    q_near_in = sent(q_near, flips(8))
    _, y_bit, x_bit, _ = bits()
    kept = summed(du_keep, after(du_in, q_near)).reshape(2, 2, count, width)
    kept = halves(kept)
    out = picked(kept[0], 1 - y_bit, 0), picked(kept[1], 1 - x_bit, 1)
    kept = picked(kept[0], y_bit, 0), picked(kept[1], x_bit, 1)
    got = pair_sent(out, 4, 2)
    u_total = last_total(in_flip, rights, u_core, u_first, pair_after(u_second, *out))
    u_near = fold_first(u_total)
    u_near_in = sent(u_near, flips(8))
    q_next = fold_second(qkv_part, after(q_near_in, u_near))
    q_next_in = sent(q_next, flips(16))
    d_next = fold_second(total, after(d_near_in, q_next))
    d_next_in = sent(d_next, flips(16))
    kept = [summed(*both) for both in zip(kept, pair_after(got, d_next))]
    out = picked(kept[0], 1 - x_bit, 0), picked(kept[1], 1 - y_bit, 0)
    kept = picked(kept[0], x_bit, 0), picked(kept[1], y_bit, 0)
    got = pair_sent(out, 2, 4)
    grad_qkv = fold_last(qkv_part, q_near_in, after(q_next_in, *out))
    size = width // shards
    gain_pair = grad_qkv[size : size + 2, : size // ctx_size].T
    qkv_last = swapped(grad_qkv[:size].reshape(ctx_size, -1, 3 * lanes), None)
    u_next = fold_second(u_total, after(u_near_in, grad_qkv))
    u_next_in = sent(u_next, flips(16))
    grad_tokens = finish_tokens(kept, pair_after(got, u_next), x, dh, gain_all)
    grad_down = fold_last(total, d_near_in, after(d_next_in, grad_tokens))
    grad_in = fold_last(u_total, u_near_in, after(u_next_in, grad_down))
    grad_qkv = after(qkv_last, grad_in)
    grad_out, grad_up = grad_in[:, :width], grad_in[:, width:]

    grad_qkv = grad_qkv.reshape(ctx_size, -1, 3, lanes).transpose(1, 2, 0, 3)
    grad_qkv = grad_qkv.reshape(-1, 3 * width)

    own_gains = picked(gains.reshape(ctx_size, -1, kinds), place, 0).astype(F32)
    row_sum = lambda weight, grad: jnp.sum(
        picked(split(weight), place, 0).astype(F32) * grad, axis=1
    )
    gain_one = row_sum(w_qkv, grad_qkv) / own_gains[:, 0]
    gain_three = row_sum(w_up, grad_up) / own_gains[:, 2]
    grad_gains = jnp.stack([gain_one, gain_pair[:, 0], gain_three, gain_pair[:, 1]], axis=1)
    return (
        layer_out.reshape(batch, rows, width),
        grad_tokens.reshape(batch, rows, width),
        grad_qkv,
        grad_out,
        grad_up,
        grad_down,
        grad_gains,
    )


def per_device(*args):
    return staged(*args) if cube() else plain(*args)


def solution(mesh):
    return jax.shard_map(
        per_device,
        mesh=mesh,
        in_specs=(
            P(None, ALL, None),
            P(None, "shard", None),
            P("shard", None),
            P("shard", None),
            P("shard", None),
            P("shard", None),
            P("shard", None),
            P(None, ALL, None),
        ),
        out_specs=(
            P(None, ALL, None),
            P(None, ALL, None),
            P(ALL, None),
            P(ALL, None),
            P(ALL, None),
            P(ALL, None),
            P(ALL, None),
        ),
        check_vma=False,
    )
```

```python
import functools
import math

import jax
import jax.numpy as jnp
from jax import lax
from jax.experimental import pallas as pl
from jax.experimental.pallas import tpu as pltpu
from jax.sharding import PartitionSpec as P

HEADS = 16
HDIM = 64
EPSILON = 1e-05
ROPE_BASE = 10000.0
MASKED = -1e30
ALL = ("shard", "ctx")
BF = jnp.bfloat16
F32 = jnp.float32
VMEM_LIMIT = 56 * 1024 * 1024
GAIN_ROWS = 16


def layer_norm(values, gain):
    center = jnp.mean(values, axis=-1, keepdims=True)
    shifted = values - center
    spread = jnp.mean(shifted * shifted, axis=-1, keepdims=True)
    return shifted * lax.rsqrt(spread + EPSILON) * gain


def gelu_tanh(values):
    return jax.nn.gelu(values, approximate=True)


def dot(left, right):
    return jnp.dot(left, right, preferred_element_type=F32)


def contract_rows(left, right):
    return lax.dot_general(left, right, (((0,), (0,)), ((), ())), preferred_element_type=F32)


def contract_cols(left, right):
    return lax.dot_general(left, right, (((1,), (1,)), ((), ())), preferred_element_type=F32)


def rope_tables(doc_starts, blocks, rows):
    half = HDIM // 2
    lane = jnp.arange(2 * HDIM, dtype=jnp.int32)
    freqs = ROPE_BASE ** (-(lane % half).astype(F32) / half)
    sign = jnp.where(lane % HDIM < half, -1.0, 1.0).astype(F32)
    positions = jnp.arange(blocks * rows, dtype=jnp.int32).reshape(blocks, 1, rows)
    latest = jnp.zeros((blocks, doc_starts.shape[0], rows), jnp.int32)
    for d in range(doc_starts.shape[1]):
        start = doc_starts[None, :, d, None]
        latest = jnp.where(positions >= start, jnp.maximum(latest, start), latest)
    angles = (positions - latest).astype(F32)[..., None] * freqs
    return jnp.cos(angles), jnp.sin(angles) * sign


def turned(values, cos_row, sin_row):
    width = values.shape[1]
    half = HDIM // 2
    if width == HDIM:
        swapped = jnp.concatenate([values[:, half:], values[:, :half]], axis=1)
    else:
        lane = lax.broadcasted_iota(jnp.int32, values.shape, 1)
        swapped = jnp.where(
            lane % HDIM < half, pltpu.roll(values, width - half, 1), pltpu.roll(values, half, 1)
        )
    return values * cos_row[:, :width] + swapped * sin_row[:, :width]


def project_rows(u, weight, cos_row, sin_row, lanes):
    full = dot(u, weight)
    parts = [full[:, slot * lanes : (slot + 1) * lanes] for slot in range(3)]
    query = turned(parts[0], cos_row, sin_row) * HDIM ** (-0.5)
    return query, turned(parts[1], cos_row, sin_row), parts[2]


def norm_parts(values):
    shifted = values - jnp.mean(values, axis=-1, keepdims=True)
    scale = lax.rsqrt(jnp.mean(shifted * shifted, axis=-1, keepdims=True) + EPSILON)
    return shifted * scale, scale


def norm_back(grad, normed, scale, gain):
    scaled = grad * gain
    return scale * (
        scaled
        - jnp.mean(scaled, axis=-1, keepdims=True)
        - normed * jnp.mean(scaled * normed, axis=-1, keepdims=True)
    )


def project_kernel(
    shards, where, a0, a1, b0, b1, cos_ref, sin_ref, *rest
):
    part_refs, (out_ref, u_ref, w_ref, gain_ref) = rest[:shards], rest[shards:]
    _, _, batch, rows, lanes = out_ref.shape
    count = batch * rows
    size = w_ref.shape[0] // shards

    @pl.when(pl.program_id(0) == 0)
    def _():
        for k, part_ref in enumerate(part_refs):
            at = pl.multiple_of(lax.rem(where[0] - k + shards, shards) * size, size)
            w_ref[pl.ds(at, size), :] = part_ref[:size, :]
            gain_ref[:, pl.ds(at, size)] = part_ref[size:, :size].astype(F32)

    gain = gain_ref[0:1, :]
    for side, (a, b) in enumerate(((a0, b0), (a1, b1))):
        core = where[3] ^ side
        x = jnp.concatenate([a[...], b[...]], axis=1).astype(F32)
        u = (norm_parts(x)[0] * gain).astype(BF)
        u_ref[core] = u
        cos_row = cos_ref[core].reshape(count, -1)
        sin_row = sin_ref[core].reshape(count, -1)
        for slot, part in enumerate(project_rows(u, w_ref[...], cos_row, sin_row, lanes)):
            out_ref[core, slot] = part.reshape(batch, rows, lanes).astype(BF)


def project(parts, weight_parts, cos_all, sin_all):
    a, b = parts[0], parts[2]
    count, half = a.shape[2:]
    shards = len(weight_parts)
    size, columns = weight_parts[0].shape
    width = 2 * half
    kinds = size - width // shards
    lanes = columns // 3
    blocks, batch, rows, _ = cos_all.shape
    a_spec = pl.BlockSpec(
        (None, None, count, half), lambda t, w: ((t // 2) ^ w[1], (t % 2) ^ w[2], 0, 0)
    )
    b_spec = pl.BlockSpec(
        (None, None, count, half), lambda t, w: ((t % 2) ^ w[2], (t // 2) ^ w[1], 0, 0)
    )
    table = pl.BlockSpec((2, batch, rows, 2 * HDIM), lambda t, w: (t, 0, 0, 0))
    whole = lambda shape: pl.BlockSpec(shape, lambda t, w: (0, 0))
    return pl.pallas_call(
        functools.partial(project_kernel, shards),
        out_shape=(
            jax.ShapeDtypeStruct((blocks, 3, batch, rows, lanes), BF),
            jax.ShapeDtypeStruct((blocks, count, width), BF),
            jax.ShapeDtypeStruct((width, columns), BF),
            jax.ShapeDtypeStruct((kinds, width), F32),
        ),
        grid_spec=pltpu.PrefetchScalarGridSpec(
            num_scalar_prefetch=1,
            grid=(4,),
            in_specs=[a_spec, a_spec, b_spec, b_spec, table, table]
            + [whole((size, columns))] * shards,
            out_specs=(
                pl.BlockSpec((2, 3, batch, rows, lanes), lambda t, w: (t, 0, 0, 0, 0)),
                pl.BlockSpec((2, count, width), lambda t, w: (t, 0, 0)),
                whole((width, columns)),
                whole((kinds, width)),
            ),
        ),
        compiler_params=pltpu.CompilerParams(vmem_limit_bytes=VMEM_LIMIT),
        name="project",
    )(where(), *parts, cos_all, sin_all, *weight_parts)


def project_plain(u_run, weight, cos_run, sin_run):
    blocks, batch, rows, _ = cos_run.shape
    lanes = weight.shape[1] // 3
    full = dot(u_run.reshape(-1, weight.shape[0]), weight).reshape(blocks, batch, rows, 3, -1, HDIM)
    half = HDIM // 2
    cosine, sine = (t[..., None, half:HDIM] for t in (cos_run, sin_run))

    def turn(values):
        first, second = values[..., :half], values[..., half:]
        return jnp.concatenate(
            [first * cosine - second * sine, second * cosine + first * sine], axis=-1
        )

    parts = [turn(full[..., 0, :, :]) * HDIM ** (-0.5), turn(full[..., 1, :, :]), full[..., 2, :, :]]
    return jnp.stack([p.reshape(blocks, batch, rows, lanes).astype(BF) for p in parts], axis=1)


def starts_row(info_ref, mb, docs, positions):
    latest = jnp.zeros_like(positions)
    for d in range(docs):
        start = info_ref[mb, d]
        latest = jnp.where(positions >= start, jnp.maximum(latest, start), latest)
    return latest


def start_scalar(info_ref, mb, docs, position):
    latest = jnp.int32(0)
    for d in range(docs):
        start = info_ref[mb, d]
        latest = jnp.where(position >= start, jnp.maximum(latest, start), latest)
    return latest


def attend_kernel(docs, heads, mb, info_ref, q_ref, k_ref, v_ref, *rest):
    o_ref, ob_ref, lse_ref = rest[-3:]
    i = pl.program_id(0)
    per, rows, lanes = q_ref.shape
    block = per * rows
    first = info_ref[mb, docs] + i * block
    low = start_scalar(info_ref, mb, docs, first) // block
    diag = first // block
    q_pos = first + lax.broadcasted_iota(jnp.int32, (1, block), 1)
    q_start = starts_row(info_ref, mb, docs, q_pos)
    q_all = q_ref[...].reshape(block, lanes)
    queries = [q_all[:, h * HDIM : (h + 1) * HDIM] for h in range(heads)]

    def visit(step, state):
        j = diag - step
        k_all = k_ref[pl.ds(j * per, per)].reshape(block, lanes)
        v_flip = v_ref[pl.ds(j * per, per)].reshape(block, lanes).astype(F32).T.astype(BF)
        k_pos = j * block + lax.broadcasted_iota(jnp.int32, (block, 1), 0)
        allowed = (k_pos >= q_start) & (k_pos <= q_pos)
        out = []
        for h in range(heads):
            peak, total, acc = state[h]
            scores = contract_cols(k_all[:, h * HDIM : (h + 1) * HDIM], queries[h])
            scores = jnp.where(allowed, scores, MASKED)
            new_peak = jnp.maximum(peak, jnp.max(scores, axis=0, keepdims=True))
            decay = jnp.exp(peak - new_peak)
            weights = jnp.exp(scores - new_peak)
            total = total * decay + jnp.sum(weights, axis=0, keepdims=True)
            acc = acc * decay + dot(v_flip[h * HDIM : (h + 1) * HDIM], weights.astype(BF))
            out.append((new_peak, total, acc))
        return tuple(out)

    start = tuple(
        (
            jnp.full((1, block), MASKED, F32),
            jnp.zeros((1, block), F32),
            jnp.zeros((HDIM, block), F32),
        )
        for _ in range(heads)
    )
    state = lax.fori_loop(0, diag - low + 1, visit, start)
    flipped = jnp.concatenate([acc / total for _, total, acc in state], axis=0)
    attended = flipped.T
    o_ref[...] = attended.reshape(per, rows, lanes)
    ob_ref[...] = attended.astype(BF).reshape(per, rows, lanes)
    lse_ref[...] = jnp.concatenate([peak + jnp.log(total) for peak, total, _ in state], axis=0)


def attend(info, docs, mb, queries, q_slot, keys, k_slot, v_slot, earlier=()):
    group_count, _, batch, rows, lanes = queries.shape
    blocks_all = keys.shape[0]
    heads = lanes // HDIM
    per = math.gcd(group_count, max(1, 512 // rows))
    q_blocks = group_count // per
    spec = pl.BlockSpec((per, None, None, rows, lanes), lambda i, info: (i, q_slot, mb, 0, 0))
    kv_spec = lambda slot: pl.BlockSpec(
        (blocks_all, None, None, rows, lanes), lambda i, info: (0, slot, mb, 0, 0)
    )
    o_spec = pl.BlockSpec((per, None, rows, lanes), lambda i, info: (i, mb, 0, 0))
    return pl.pallas_call(
        functools.partial(attend_kernel, docs, heads, mb),
        out_shape=(
            jax.ShapeDtypeStruct((group_count, batch, rows, lanes), F32),
            jax.ShapeDtypeStruct((group_count, batch, rows, lanes), BF),
            jax.ShapeDtypeStruct((batch, heads, group_count * rows), F32),
        ),
        grid_spec=pltpu.PrefetchScalarGridSpec(
            num_scalar_prefetch=1,
            grid=(q_blocks,),
            in_specs=[spec, kv_spec(k_slot), kv_spec(v_slot)]
            + [pl.BlockSpec(memory_space=pl.ANY)] * len(earlier),
            out_specs=(
                o_spec,
                o_spec,
                pl.BlockSpec((None, heads, per * rows), lambda i, info: (mb, 0, i)),
            ),
        ),
        input_output_aliases={4 + n: n for n in range(len(earlier))},
        compiler_params=pltpu.CompilerParams(vmem_limit_bytes=VMEM_LIMIT),
        name="attend",
    )(info, queries, keys, keys, *earlier)


def attend_back_kernel(
    docs, heads, per, merged, mb, info_ref, q_ref, k_ref, v_ref, do_ref, o_ref, lse_ref, cosq_ref,
    sinq_ref, cosk_ref, sink_ref, *rest
):
    j = pl.program_id(0)
    out_ref, dq_acc, delta_ref = rest[-3:]
    dq_ref = None if merged else rest[-4]
    group_count, rows, lanes = q_ref.shape
    block = per * rows
    q_blocks = group_count // per
    base = info_ref[mb, docs] // block

    def lanes_of(i):
        return pl.ds(pl.multiple_of(i * block, block), block)

    @pl.when(j == 0)
    def _():
        dq_acc[...] = jnp.zeros_like(dq_acc)

        def fill(i, carry):
            here = pl.ds(i * per, per)
            prod = do_ref[here].reshape(block, lanes).astype(F32) * o_ref[here].reshape(
                block, lanes
            )
            flipped = prod.T
            delta_ref[:, lanes_of(i)] = jnp.concatenate(
                [
                    jnp.sum(flipped[h * HDIM : (h + 1) * HDIM], axis=0, keepdims=True)
                    for h in range(heads)
                ],
                axis=0,
            )
            return carry

        lax.fori_loop(0, q_blocks, fill, 0)

    k_first = j * block
    last = k_first + block - 1
    end = base * block + group_count * rows
    for d in range(docs):
        start = info_ref[mb, d]
        end = jnp.where(start > last, jnp.minimum(end, start), end)
    i_low = jnp.maximum(j - base, 0)
    i_high = jnp.maximum((end - base * block + block - 1) // block, i_low)
    k_pos = k_first + lax.broadcasted_iota(jnp.int32, (block, 1), 0)
    k_all = k_ref[...].reshape(block, lanes)
    v_all = v_ref[...].reshape(block, lanes)
    k_flip = k_all.astype(F32).T.astype(BF)
    heads_of = lambda a: [a[:, h * HDIM : (h + 1) * HDIM] for h in range(heads)]
    k_heads, v_heads = heads_of(k_all), heads_of(v_all)

    def visit(i, state):
        here = pl.ds(i * per, per)
        q_heads = heads_of(q_ref[here].reshape(block, lanes))
        do_heads = heads_of(do_ref[here].reshape(block, lanes))
        q_pos = (base + i) * block + lax.broadcasted_iota(jnp.int32, (1, block), 1)
        q_start = starts_row(info_ref, mb, docs, q_pos)
        allowed = (k_pos >= q_start) & (k_pos <= q_pos)
        lse = lse_ref[:, lanes_of(i)]
        delta = delta_ref[:, lanes_of(i)]
        out = []
        for h in range(heads):
            dk, dv = state[h]
            scores = contract_cols(k_heads[h], q_heads[h])
            weights = jnp.exp(jnp.where(allowed, scores - lse[h : h + 1], MASKED))
            grad_weights = contract_cols(v_heads[h], do_heads[h])
            grad_scores = (weights * (grad_weights - delta[h : h + 1])).astype(BF)
            dv = dv + dot(weights.astype(BF), do_heads[h])
            dk = dk + dot(grad_scores, q_heads[h])
            at = slice(h * HDIM, (h + 1) * HDIM)
            dq_acc[at, lanes_of(i)] += dot(k_flip[at], grad_scores)
            out.append((dk, dv))
        return tuple(out)

    zero = jnp.zeros((block, HDIM), F32)
    state = lax.fori_loop(i_low, i_high, visit, tuple((zero, zero) for _ in range(heads)))
    dk = jnp.concatenate([dk for dk, _ in state], axis=1) if heads > 1 else state[0][0]
    dv = jnp.concatenate([dv for _, dv in state], axis=1) if heads > 1 else state[0][1]
    dk = turned(dk, cosk_ref[...].reshape(block, -1), -sink_ref[...].reshape(block, -1))
    there = pl.ds(j * per, per)
    first = lanes if merged else 0
    out_ref[there, :, first : first + lanes] = dk.reshape(per, rows, lanes).astype(out_ref.dtype)
    out_ref[there, :, first + lanes : first + 2 * lanes] = dv.reshape(per, rows, lanes).astype(
        out_ref.dtype
    )

    @pl.when(j == pl.num_programs(0) - 1)
    def _():
        def finish(i, carry):
            dq = dq_acc[:, lanes_of(i)].T
            at = pl.ds(i * per, per)
            cos_row = cosq_ref[at].reshape(block, -1)
            sin_row = sinq_ref[at].reshape(block, -1)
            dq = turned(dq, cos_row, -sin_row) * HDIM ** (-0.5)
            dq = dq.reshape(per, rows, lanes).astype(BF)
            if merged:
                out_ref[at, :, :lanes] = dq
            else:
                dq_ref[at] = dq
            return carry

        lax.fori_loop(0, q_blocks, finish, 0)


def attend_back(info, docs, mb, queries, q_slot, keys, k_slot, v_slot, grad, attended, lse,
                cos_all, sin_all, cos_here, sin_here, earlier=()):
    group_count, _, batch, rows, lanes = queries.shape
    blocks_all = keys.shape[0]
    merged = blocks_all == group_count
    heads = lanes // HDIM
    per = math.gcd(group_count, max(1, 512 // rows))
    length = group_count * rows
    full = pl.BlockSpec(
        (group_count, None, None, rows, lanes), lambda j, info: (0, q_slot, mb, 0, 0)
    )
    part = lambda slot: pl.BlockSpec(
        (per, None, None, rows, lanes), lambda j, info: (j, slot, mb, 0, 0)
    )
    rows_of_mb = lambda count, width: pl.BlockSpec(
        (count, None, rows, width), lambda j, info: (0, mb, 0, 0)
    )
    table_k = pl.BlockSpec((per, None, rows, 2 * HDIM), lambda j, info: (j, mb, 0, 0))
    if merged:
        out_shape = [jax.ShapeDtypeStruct((group_count, batch, rows, 3 * lanes), BF)]
        out_specs = [rows_of_mb(group_count, 3 * lanes)]
    else:
        out_shape = [
            jax.ShapeDtypeStruct((group_count, batch, rows, lanes), BF),
            jax.ShapeDtypeStruct((blocks_all, batch, rows, 2 * lanes), F32),
        ]
        out_specs = [rows_of_mb(group_count, lanes), rows_of_mb(blocks_all, 2 * lanes)]
    table_q = rows_of_mb(group_count, 2 * HDIM)
    return pl.pallas_call(
        functools.partial(attend_back_kernel, docs, heads, per, merged, mb),
        out_shape=out_shape,
        grid_spec=pltpu.PrefetchScalarGridSpec(
            num_scalar_prefetch=1,
            grid=(blocks_all // per,),
            in_specs=[
                full, part(k_slot), part(v_slot), rows_of_mb(group_count, lanes),
                rows_of_mb(group_count, lanes),
                pl.BlockSpec((None, heads, length), lambda j, info: (mb, 0, 0)),
                table_q, table_q, table_k, table_k,
            ]
            + [pl.BlockSpec(memory_space=pl.ANY)] * len(earlier),
            out_specs=out_specs,
            scratch_shapes=[pltpu.VMEM((lanes, length), F32), pltpu.VMEM((heads, length), F32)],
        ),
        input_output_aliases={11 + n: n for n in range(len(earlier))},
        compiler_params=pltpu.CompilerParams(vmem_limit_bytes=VMEM_LIMIT),
        name="attend_back",
    )(info, queries, keys, keys, grad, attended, lse, cos_here, sin_here, cos_all, sin_all,
      *earlier)


def flips(mask):
    count = lax.axis_size("shard") * lax.axis_size("ctx")
    return [(i, i ^ mask) for i in range(count)]


def turns(by):
    shards, places = lax.axis_size("shard"), lax.axis_size("ctx")
    return [
        (a * places + b, ((a + by) % shards) * places + b)
        for a in range(shards)
        for b in range(places)
    ]


def sent(values, pairs):
    return lax.ppermute(values, ALL, pairs)


def picked(values, index, axis):
    return lax.dynamic_index_in_dim(values, index, axis, keepdims=False)


def cube():
    return lax.axis_size("ctx") == 8 and lax.axis_size("shard") == 4


def bits():
    place = lax.axis_index("ctx")
    return lax.axis_index("shard"), place // 4, place // 2 % 2, place % 2


def where():
    return jnp.stack(bits()).astype(jnp.int32)


def spread(values, early, late):
    half = values.shape[1] // 2
    a, b = values[:, :half], values[:, half:]
    a_in, b_in = sent(a, flips(2)), sent(b, flips(4))
    a, b = jnp.stack([a, after(a_in, *early)]), jnp.stack([b, after(b_in, *early)])
    a = jnp.stack([a, after(sent(a, flips(4)), *late)])
    b = jnp.stack([b, after(sent(b, flips(2)), *late)])
    return a, sent(a, flips(1)), b, sent(b, flips(1))


def ring_parts(values):
    shards = lax.axis_size("shard")
    z = lax.axis_index("shard")
    return [picked(values, lax.rem(z + k, shards), 0) for k in range(shards)]


def ring_sent(parts):
    return [sent(part, turns(k)) for k, part in enumerate(parts) if k]


def ring_total(own, received):
    total = own.astype(F32)
    for part in received:
        total = total + part.astype(F32)
    return total


def fold_first(values):
    low = lax.axis_index("shard") % 2
    return picked(values.reshape(2, 2, *values.shape[1:]), 1 - low, 1)


def fold_second(values, received):
    z = lax.axis_index("shard")
    mine = picked(values.reshape(2, 2, *values.shape[1:]), z % 2, 1)
    return summed(picked(mine, 1 - z // 2, 0), picked(received, 1 - z // 2, 0))


def fold_last(values, received, last):
    z = lax.axis_index("shard")
    parts = picked(values, z, 0), picked(received, z // 2, 0), last
    return sum(part.astype(F32) for part in parts)


def after(values, *earlier):
    return lax.optimization_barrier((values,) + earlier)[0]


def far_rows(piece, *earlier):
    shards = lax.axis_size("shard")
    return jnp.stack([after(sent(piece, turns(k)), *earlier) for k in range(1, shards)])


def copies_in(where, owns, parts, out_ref, sem):
    z, y, x, c = (where[i] for i in range(4))
    shards = out_ref.shape[0]
    half = parts[0].shape[-1]
    groups = [[] for _ in range(shards)]

    def add(k, source, target):
        at = sum(len(group) for group in groups)
        groups[k].append(pltpu.make_async_copy(source, target, sem.at[at]))

    first = 0
    for own in owns:
        add(0, own, out_ref.at[z, :, :, pl.ds(first, own.shape[-1])])
        first += own.shape[-1]
    for k in range(1, shards):
        source = lax.rem(z - k + shards, shards)
        for side in range(2):
            a, b = parts[side], parts[2 + side]
            core = c ^ side
            for p in range(2):
                for q in range(2):
                    at_a = ((y ^ p) * 2 + (x ^ q)) * 2 + core
                    at_b = ((y ^ q) * 2 + (x ^ p)) * 2 + core
                    add(k, a.at[p, q, k - 1], out_ref.at[source, at_a, :, pl.ds(0, half)])
                    add(k, b.at[p, q, k - 1], out_ref.at[source, at_b, :, pl.ds(half, half)])
    for group in groups:
        for copy in group:
            copy.start()
    return groups


def arrived(groups, where):
    shards = len(groups)
    for k, group in enumerate(groups):
        for copy in group:
            copy.wait()
        yield lax.rem(where[0] - k + shards, shards)


def copy_count(shards, owns):
    return owns + 16 * (shards - 1)


def rows_of(w, first, last):
    part = w[:, :, :, first:last]
    return part.reshape(-1, last - first)


def chunk_of(w, z, first, last):
    part = w[z, :, :, first:last]
    return part.reshape(-1, last - first)


def block_at(z, size):
    return pl.ds(pl.multiple_of(z * size, size), size)


def flip_pieces(values, size, out_ref, first):
    tokens, rows = values.shape
    step = max(size, 128)
    for start in range(0, rows, step):
        flip = values[:, start : start + step].astype(F32).T.astype(BF)
        for low in range(0, step, size):
            piece = (start + low) // size
            z, y, x, c = piece // 8, piece // 4 % 2, piece // 2 % 2, piece % 2
            out_ref[c, y, x, z, :, first : first + tokens] = flip[low : low + size]


def mlp_in_kernel(
    where, ob_ref, x_ref, gain_ref, own_out, own_up, a0, a1, b0, b1,
    a_ref, h_ref, g_ref, slope_ref, in_flip, g_flip, w, obl, sem
):
    copies = copies_in(where, (own_out, own_up), (a0, a1, b0, b1), w, sem)
    groups, batch, rows, lanes = ob_ref.shape
    shards = w.shape[0]
    width = x_ref.shape[1]
    count = batch * rows
    size = width // shards
    for mb in range(batch):
        for g in range(groups):
            obl[mb * rows : (mb + 1) * rows, g * lanes : (g + 1) * lanes] = ob_ref[g, mb]
    flip_pieces(obl[...], size // 8, in_flip, count)
    a = None
    for z in arrived(copies, where):
        part = dot(obl[:, block_at(z, size)], chunk_of(w, z, 0, width))
        a = part if a is None else a + part
    a_ref[...] = a
    h = x_ref[...].astype(F32) + norm_parts(a)[0] * gain_ref[1:2, :]
    h_ref[...] = h
    u2 = (norm_parts(h)[0] * gain_ref[2:3, :]).astype(BF)
    flip_pieces(u2, size // 8, in_flip, 0)
    hidden = g_ref.shape[1]
    step = 512
    root = math.sqrt(2.0 / math.pi)
    for first in range(0, hidden, step):
        f = dot(u2, rows_of(w, width + first, width + first + step))
        square = f * f
        bent = jnp.tanh(root * (f + 0.044715 * (square * f)))
        half = 0.5 * (1.0 + bent)
        at = slice(first, first + step)
        g_ref[:, at] = (f * half).astype(BF)
        slope = half + 0.5 * f * (1.0 - bent * bent) * (root * (1.0 + 3 * 0.044715 * square))
        slope_ref[:, at] = slope.astype(BF)
    flip_pieces(g_ref[...], hidden // (8 * shards), g_flip, 0)


def mlp_in(ob, x, gain_all, w_out, w_up, parts):
    shards = lax.axis_size("shard")
    count, width = x.shape
    hidden = w_up.shape[-1]
    pieces, rows = w_out.shape[:2]
    anywhere = pl.BlockSpec(memory_space=pl.ANY)
    local = pl.BlockSpec(memory_space=pltpu.VMEM)
    shape = jax.ShapeDtypeStruct
    return pl.pallas_call(
        mlp_in_kernel,
        out_shape=(
            shape((count, width), F32),
            shape((count, width), F32),
            shape((count, hidden), BF),
            shape((count, hidden), BF),
            shape((2, 2, 2, shards, width // (8 * shards), 2 * count), BF),
            shape((2, 2, 2, shards, hidden // (8 * shards), count), BF),
        ),
        grid_spec=pltpu.PrefetchScalarGridSpec(
            num_scalar_prefetch=1,
            grid=(),
            in_specs=[local] * 3 + [anywhere] * 6,
            out_specs=[local] * 6,
            scratch_shapes=[
                pltpu.VMEM((shards, pieces, rows, width + hidden), BF),
                pltpu.VMEM((count, width), BF),
                pltpu.SemaphoreType.DMA((copy_count(shards, 2),)),
            ],
        ),
        compiler_params=pltpu.CompilerParams(vmem_limit_bytes=VMEM_LIMIT),
        name="mlp_in",
    )(where(), ob, x, gain_all, w_out, w_up, *parts)


def mlp_out_kernel(
    where, g_ref, slope_ref, h_ref, cot_ref, gain_ref, own, a0, a1, b0, b1,
    out_ref, dmb_ref, dfb_ref, gg_ref, w, sem
):
    copies = copies_in(where, (own,), (a0, a1, b0, b1), w, sem)
    shards = w.shape[0]
    width = h_ref.shape[1]
    size = g_ref.shape[1] // shards
    m = None
    for z in arrived(copies, where):
        part = dot(g_ref[:, block_at(z, size)], chunk_of(w, z, 0, width))
        m = part if m is None else m + part
    gain = gain_ref[3:4, :]
    normed, scale = norm_parts(m)
    out_ref[...] = (h_ref[...] + normed * gain).astype(BF)
    dy = cot_ref[...].astype(F32)
    gg_ref[...] = jnp.sum(dy * normed, axis=0, keepdims=True)
    dmb = norm_back(dy, normed, scale, gain).astype(BF)
    dmb_ref[...] = dmb
    for z in range(shards):
        at = slice(z * size, (z + 1) * size)
        dg = contract_cols(dmb, chunk_of(w, z, 0, width))
        dfb_ref[:, at] = (dg * slope_ref[:, at].astype(F32)).astype(BF)


def mlp_out(g, slope, h, cot, gain_all, w_down, parts):
    shards = lax.axis_size("shard")
    count, width = h.shape
    hidden = g.shape[1]
    pieces, rows = w_down.shape[:2]
    anywhere = pl.BlockSpec(memory_space=pl.ANY)
    local = pl.BlockSpec(memory_space=pltpu.VMEM)
    shape = jax.ShapeDtypeStruct
    return pl.pallas_call(
        mlp_out_kernel,
        out_shape=(
            shape((count, width), BF),
            shape((count, width), BF),
            shape((count, hidden), BF),
            shape((1, width), F32),
        ),
        grid_spec=pltpu.PrefetchScalarGridSpec(
            num_scalar_prefetch=1,
            grid=(),
            in_specs=[local] * 5 + [anywhere] * 5,
            out_specs=[local] * 4,
            scratch_shapes=[
                pltpu.VMEM((shards, pieces, rows, width), BF),
                pltpu.SemaphoreType.DMA((copy_count(shards, 1),)),
            ],
        ),
        compiler_params=pltpu.CompilerParams(vmem_limit_bytes=VMEM_LIMIT),
        name="mlp_out",
    )(where(), g, slope, h, cot, gain_all, w_down, *parts)


def mlp_back_kernel(
    where, dfb_ref, h_ref, a_ref, cot_ref, gain_ref, gain_four_ref, own_out, own_up, a0, a1, b0, b1,
    dh_ref, right_a, right_b, dob_ref, w, du2, sem
):
    copies = copies_in(where, (own_out, own_up), (a0, a1, b0, b1), w, sem)
    shards = w.shape[0]
    count, width = h_ref.shape
    size = width // shards
    groups, batch, rows, lanes = dob_ref.shape
    rows -= GAIN_ROWS
    last = w.shape[-1]
    middle = last // 2
    right_a[:count, :width] = jnp.zeros((count, width), BF)
    right_a[count:, width:] = jnp.zeros((count, middle - width), BF)
    right_a[:count, width:] = dfb_ref[:, : middle - width]
    right_b[count:, :] = jnp.zeros((count, middle), BF)
    right_b[:count, :] = dfb_ref[:, middle - width :]
    for z in arrived(copies, where):
        du2[:, block_at(z, size)] = contract_cols(dfb_ref[...], chunk_of(w, z, width, last))
    normed, scale = norm_parts(h_ref[...])
    dh = cot_ref[...].astype(F32) + norm_back(du2[...], normed, scale, gain_ref[2:3, :])
    dh_ref[...] = dh
    normed, scale = norm_parts(a_ref[...])
    gains = (jnp.sum(dh * normed, axis=0, keepdims=True), gain_four_ref[...])
    step = lanes // shards
    blank = jnp.zeros((GAIN_ROWS - len(gains), lanes), F32)
    for g in range(groups):
        lines = [
            jnp.concatenate(
                [line[:, z * size + g * step : z * size + (g + 1) * step] for z in range(shards)],
                axis=1,
            )
            for line in gains
        ]
        block = jnp.concatenate(lines + [blank], axis=0).astype(BF)
        for mb in range(batch):
            dob_ref[g, mb, rows:, :] = block
    dab = norm_back(dh, normed, scale, gain_ref[1:2, :]).astype(BF)
    right_a[count:, :width] = dab
    for z in range(shards):
        dob = contract_cols(dab, chunk_of(w, z, 0, width)).astype(BF)
        for part in range(size // lanes):
            for mb in range(batch):
                dob_ref[z * (size // lanes) + part, mb, :rows] = dob[
                    mb * rows : (mb + 1) * rows, part * lanes : (part + 1) * lanes
                ]


def mlp_back(dfb, h, a, cot, gain_all, gain_four, w_out, w_up, parts, groups, batch):
    shards = lax.axis_size("shard")
    count, width = h.shape
    hidden = dfb.shape[1]
    pieces, rows = w_out.shape[:2]
    anywhere = pl.BlockSpec(memory_space=pl.ANY)
    local = pl.BlockSpec(memory_space=pltpu.VMEM)
    shape = jax.ShapeDtypeStruct
    return pl.pallas_call(
        mlp_back_kernel,
        out_shape=(
            shape((count, width), F32),
            shape((2 * count, (width + hidden) // 2), BF),
            shape((2 * count, (width + hidden) // 2), BF),
            shape((groups, batch, count // batch + GAIN_ROWS, width // groups), BF),
        ),
        grid_spec=pltpu.PrefetchScalarGridSpec(
            num_scalar_prefetch=1,
            grid=(),
            in_specs=[local] * 6 + [anywhere] * 6,
            out_specs=[local] * 4,
            scratch_shapes=[
                pltpu.VMEM((shards, pieces, rows, width + hidden), BF),
                pltpu.VMEM((count, width), F32),
                pltpu.SemaphoreType.DMA((copy_count(shards, 2),)),
            ],
        ),
        compiler_params=pltpu.CompilerParams(vmem_limit_bytes=VMEM_LIMIT),
        name="mlp_back",
    )(where(), dfb, h, a, cot, gain_all, gain_four, w_out, w_up, *parts)


def tail_kernel(where, dqkv_ref, u_ref, w_ref, gain_ref, keep_ref, away_ref, grad_ref):
    core = where[3]
    shards = grad_ref.shape[0]
    size = w_ref.shape[0] // shards
    step = gain_ref.shape[1] // shards
    total = None
    for pair in range(dqkv_ref.shape[0] // 2):
        for side, out_ref in enumerate((keep_ref, away_ref)):
            block = 2 * pair + (core ^ side)
            dqkv = dqkv_ref[block]
            out_ref[pair] = contract_cols(dqkv, w_ref[...]).astype(BF)
            part = dot(dqkv.astype(F32).T.astype(BF), u_ref[block])
            total = part if total is None else total + part
    blank = jnp.zeros((gain_ref.shape[0], grad_ref.shape[2] - step), F32)
    for z in range(shards):
        grad_ref[z, :size] = total[:, z * size : (z + 1) * size].T.astype(BF)
        gains = gain_ref[:, z * step : (z + 1) * step]
        grad_ref[z, size:] = jnp.concatenate([gains, blank], axis=1).astype(BF)


def tail_products(dqkv, u_run, w_heads, gain_part):
    blocks, count, columns = dqkv.shape
    width = w_heads.shape[0]
    shards = lax.axis_size("shard")
    local = pl.BlockSpec(memory_space=pltpu.VMEM)
    rows = jax.ShapeDtypeStruct((blocks // 2, count, width), BF)
    return pl.pallas_call(
        tail_kernel,
        out_shape=(
            rows,
            rows,
            jax.ShapeDtypeStruct((shards, width // shards + gain_part.shape[0], columns), BF),
        ),
        grid_spec=pltpu.PrefetchScalarGridSpec(
            num_scalar_prefetch=1, grid=(), in_specs=[local] * 4, out_specs=[local] * 3
        ),
        compiler_params=pltpu.CompilerParams(vmem_limit_bytes=VMEM_LIMIT),
        name="tail_products",
    )(where(), dqkv, u_run, w_heads, gain_part)


def finish_kernel(keep_a, keep_b, got_a, got_b, x_ref, dh_ref, gain_ref, out_ref):
    parts = ((keep_a, got_a), (keep_b, got_b))
    du = jnp.concatenate([k[...].astype(F32) + g[...].astype(F32) for k, g in parts], axis=1)
    normed, scale = norm_parts(x_ref[...].astype(F32))
    out_ref[...] = dh_ref[...] + norm_back(du, normed, scale, gain_ref[0:1, :])


def finish_tokens(kept, got, x, dh, gain_all):
    local = pl.BlockSpec(memory_space=pltpu.VMEM)
    return pl.pallas_call(
        finish_kernel,
        out_shape=jax.ShapeDtypeStruct(x.shape, F32),
        in_specs=[local] * 7,
        out_specs=local,
        compiler_params=pltpu.CompilerParams(vmem_limit_bytes=VMEM_LIMIT),
        name="finish_tokens",
    )(*kept, *got, x, dh, gain_all)


def product(left, right, *addends):
    total = dot(left.reshape(-1, left.shape[-1]), right)
    total = total.reshape(*left.shape[:-1], right.shape[1])
    for addend in addends:
        total = total + addend.astype(F32)
    return total.astype(BF)


def halves(values):
    half = values.shape[-1] // 2
    return values[..., :half], values[..., half:]


def at(values, y, x):
    return picked(picked(values, y, 0), x, 0)


def first_away(left, rights):
    left = picked(left, 1 - bits()[3], 0)
    return [product(left, right) for right in rights]


def second_away(left, rights, core_in):
    _, y, x, c = bits()
    left = picked(left, c, 0)
    return (
        product(picked(left, 1 - y, 0), rights[0], picked(core_in[0], 1 - y, 0)),
        product(picked(left, 1 - x, 1), rights[1], picked(core_in[1], 1 - x, 1)),
    )


def third_away(left, rights, core_in, first_in):
    _, y, x, c = bits()
    left = picked(left, c, 0)
    return (
        product(
            at(left, y, 1 - x), rights[0], at(core_in[0], y, 1 - x), picked(first_in[0], 1 - x, 0)
        ),
        product(
            at(left, 1 - y, x), rights[1], at(core_in[1], 1 - y, x), picked(first_in[1], 1 - y, 0)
        ),
    )


def last_total(left, rights, core_in, first_in, second_in):
    _, y, x, c = bits()
    left = at(picked(left, c, 0), y, x)
    own = (x, y)
    parts = [
        product(left, rights[n], at(core_in[n], y, x), picked(first_in[n], own[n], 0), second_in[n])
        for n in range(2)
    ]
    return jnp.concatenate(parts, axis=-1)


def pair_sent(parts, first, second):
    return sent(parts[0], flips(first)), sent(parts[1], flips(second))


def pair_after(parts, *earlier):
    return tuple(after(part, *earlier) for part in parts)


def summed(left, right):
    return (left.astype(F32) + right.astype(F32)).astype(BF)


def gathered(weight):
    size = weight.shape[0] // lax.axis_size("ctx")
    piece = lax.dynamic_slice_in_dim(weight, lax.axis_index("ctx") * size, size, 0)
    return lax.all_gather(piece, ALL, axis=0, tiled=True)


def scattered(left, right):
    total = contract_rows(left, right).astype(BF)
    return lax.psum_scatter(total, ALL, scatter_dimension=0, tiled=True).astype(F32)


def scattered_gains(grads):
    count = lax.axis_size("shard") * lax.axis_size("ctx")
    kinds = grads.shape[0]
    parts = grads.reshape(kinds, count, -1).transpose(1, 0, 2)
    parts = lax.all_to_all(parts, ALL, split_axis=0, concat_axis=0, tiled=True)
    return jnp.sum(parts, axis=0).T


def swapped(values, groups):
    return lax.all_to_all(
        values, "ctx", split_axis=0, concat_axis=0, tiled=True, axis_index_groups=groups
    )


def plain(tokens, doc_starts, w_qkv, w_out, w_up, w_down, gains, cotangent):
    ctx_size = lax.axis_size("ctx")
    place = lax.axis_index("ctx")
    batch, rows, width = tokens.shape
    count = batch * rows
    docs = doc_starts.shape[2]
    group_count = math.gcd(HEADS, ctx_size)
    runs = ctx_size // group_count
    if runs == 1:
        near = far = None
    else:
        near = [[r * group_count + g for g in range(group_count)] for r in range(runs)]
        far = [[r * group_count + g for r in range(runs)] for g in range(group_count)]
    lanes = width // group_count

    gain_all = lax.all_gather(gains, "shard", axis=0, tiled=True).T.astype(F32)
    columns = picked(w_qkv.reshape(-1, 3, group_count, lanes), lax.rem(place, group_count), 2)
    w_heads = lax.all_gather(columns.reshape(-1, 3 * lanes), "shard", axis=0, tiled=True)
    full_out, full_up, full_down = gathered(w_out), gathered(w_up), gathered(w_down)

    starts = doc_starts[:, 0, :]
    cos_all, sin_all = rope_tables(starts, ctx_size, rows)
    run_first = (place // group_count) * group_count
    info = jnp.concatenate(
        [starts, jnp.broadcast_to(run_first * rows, (batch, 1)).astype(jnp.int32)], axis=1
    )

    x = tokens.reshape(count, width).astype(F32)
    out_grad = cotangent.reshape(count, width).astype(F32)
    normed, norm_one_back = jax.vjp(layer_norm, x, gain_all[0])
    u = normed.astype(BF)
    cos_here, sin_here = (
        lax.dynamic_slice_in_dim(t, run_first, group_count, 0) for t in (cos_all, sin_all)
    )
    u_run = lax.all_gather(u, "ctx", axis=0, axis_index_groups=near)
    qkv = project_plain(u_run, w_heads, cos_here, sin_here)
    if runs == 1:
        keys, k_slot = qkv, 1
    else:
        keys, k_slot = (
            lax.all_gather(qkv[:, 1:], "ctx", axis=0, tiled=True, axis_index_groups=far),
            0,
        )
    held = ()
    for mb in range(batch):
        held = attend(info, docs, mb, qkv, 0, keys, k_slot, k_slot + 1, held)
    attended, attended_low, lse = held
    ob = swapped(attended_low, near).transpose(1, 2, 0, 3).reshape(count, width)
    attn_proj = dot(ob, full_out)
    attn_branch, norm_two_back = jax.vjp(layer_norm, attn_proj, gain_all[1])
    hidden = x + attn_branch
    normed_two, norm_three_back = jax.vjp(layer_norm, hidden, gain_all[2])
    u2 = normed_two.astype(BF)
    up_proj = dot(u2, full_up)
    activated, gelu_back = jax.vjp(gelu_tanh, up_proj)
    g = activated.astype(BF)
    down_proj = dot(g, full_down)
    mlp_branch, norm_four_back = jax.vjp(layer_norm, down_proj, gain_all[3])
    layer_out = (hidden + mlp_branch).astype(BF)

    down_grad, gain_four = norm_four_back(out_grad)
    dmb = down_grad.astype(BF)
    grad_down = scattered(g, dmb)
    (up_grad,) = gelu_back(contract_cols(dmb, full_down))
    dfb = up_grad.astype(BF)
    grad_up = scattered(u2, dfb)
    hidden_add, gain_three = norm_three_back(contract_cols(dfb, full_up))
    dh = out_grad + hidden_add
    attn_grad, gain_two = norm_two_back(dh)
    dab = attn_grad.astype(BF)
    grad_out = scattered(ob, dab)
    dob = contract_cols(dab, full_out).astype(BF)
    dob = swapped(dob.reshape(batch, rows, group_count, lanes).transpose(2, 0, 1, 3), near)
    back = ()
    for mb in range(batch):
        back = attend_back(
            info, docs, mb, qkv, 0, keys, k_slot, k_slot + 1, dob, attended, lse, cos_all, sin_all,
            cos_here, sin_here, back,
        )
    if runs == 1:
        dqkv = back[0]
    else:
        dkv = lax.psum_scatter(
            back[1], "ctx", scatter_dimension=0, tiled=True, axis_index_groups=far
        )
        dqkv = jnp.concatenate([back[0], dkv.astype(BF)], axis=-1)
    dqkv = dqkv.reshape(group_count * count, 3 * lanes)
    du = contract_cols(dqkv, w_heads)
    qkv_part = contract_rows(u_run.reshape(group_count * count, width), dqkv)
    du = lax.psum_scatter(du, "ctx", scatter_dimension=0, tiled=True, axis_index_groups=near)
    own = jnp.zeros((width, 3, group_count, lanes), F32)
    own = lax.dynamic_update_slice_in_dim(
        own, qkv_part.reshape(width, 3, 1, lanes), lax.rem(place, group_count), 2
    )
    grad_qkv = lax.psum_scatter(
        own.reshape(width, 3 * width), ALL, scatter_dimension=0, tiled=True
    )
    input_add, gain_one = norm_one_back(du)
    grad_tokens = dh + input_add
    grad_gains = scattered_gains(jnp.stack([gain_one, gain_two, gain_three, gain_four]))
    return (
        layer_out.reshape(batch, rows, width),
        grad_tokens.reshape(batch, rows, width),
        grad_qkv,
        grad_out,
        grad_up,
        grad_down,
        grad_gains,
    )


def staged(tokens, doc_starts, w_qkv, w_out, w_up, w_down, gains, cotangent):
    ctx_size, shards = lax.axis_size("ctx"), lax.axis_size("shard")
    place = lax.axis_index("ctx")
    batch, rows, width = tokens.shape
    count = batch * rows
    docs = doc_starts.shape[2]
    lanes = width // ctx_size
    kinds = gains.shape[1]
    x = tokens.reshape(count, width)
    cot = cotangent.reshape(count, width)
    split = lambda w: w.reshape(ctx_size, -1, w.shape[1])
    own_out, own_up, own_down = split(w_out), split(w_up), split(w_down)

    starts = doc_starts[:, 0, :]
    cos_all, sin_all = rope_tables(starts, ctx_size, rows)
    columns = picked(w_qkv.reshape(-1, 3, ctx_size, lanes), place, 2).reshape(-1, 3 * lanes)
    gain_rows = jnp.pad(gains.T, ((0, 8 - kinds), (0, 3 * lanes - gains.shape[0])))
    piece = jnp.concatenate([columns, gain_rows])
    head_parts = [piece] + [sent(piece, turns(k)) for k in range(1, shards)]

    piece = jnp.concatenate([picked(own_out, place, 0), picked(own_up, place, 0)], axis=1)
    piece = after(piece, cos_all, sin_all, *head_parts)
    far_in = [sent(piece, turns(k)) for k in range(1, shards)]
    x_parts = spread(x, (cos_all, sin_all, *head_parts[1:]), (far_in[0], far_in[-1]))

    info = jnp.concatenate([starts, jnp.zeros((batch, 1), jnp.int32)], axis=1)
    qkv, u_run, w_heads, gain_all = project(x_parts, head_parts, cos_all, sin_all)

    far_in = jnp.stack([after(part, qkv) for part in far_in])
    piece_out = after(picked(own_down, place, 0), far_in)
    half = far_in.shape[2] // 2
    a, b = far_in[:, :, :half], far_in[:, :, half:]
    a_in, b_in = sent(a, flips(2)), sent(b, flips(4))
    held = ()
    for mb in range(batch):
        held = attend(after(info, far_in, *held), docs, mb, qkv, 0, qkv, 1, 2, held)
        if mb == 0:
            a, b = jnp.stack([a, after(a_in, held[2])]), jnp.stack([b, after(b_in, held[2])])
            info = after(info, a, b)
    attended, attended_low, lse = held
    a_in, b_in = sent(a, flips(4)), sent(b, flips(2))
    ob = swapped(attended_low, None)
    far_out = far_rows(piece_out, lse)
    half = far_out.shape[2] // 2
    c, d = far_out[:, :, :half], far_out[:, :, half:]
    c_in, d_in = sent(c, flips(2)), sent(d, flips(4))
    a, b = jnp.stack([a, after(a_in, c, d, ob)]), jnp.stack([b, after(b_in, c, d, ob)])
    in_parts = (a, sent(a, flips(1)), b, sent(b, flips(1)))
    c, d = jnp.stack([c, after(c_in, a, b, ob)]), jnp.stack([d, after(d_in, a, b, ob)])
    c_in, d_in = sent(c, flips(4)), sent(d, flips(2))

    attn, h, g, slope, in_flip, g_flip = mlp_in(
        after(ob, c, d), x, gain_all, own_out, own_up, in_parts
    )
    c, d = jnp.stack([c, after(c_in, h)]), jnp.stack([d, after(d_in, h)])
    out_parts = (c, sent(c, flips(1)), d, sent(d, flips(1)))
    layer_out, dmb, dfb, gain_four = mlp_out(g, slope, h, cot, gain_all, own_down, out_parts)

    dmbs = halves(dmb)
    d_out = first_away(g_flip, dmbs)
    d_core = pair_sent(d_out, 1, 1)
    dh, right_a, right_b, dob = mlp_back(
        after(dfb, *d_out), h, attn, cot, gain_all, gain_four, own_out, own_up, in_parts, ctx_size, batch
    )
    rights = (right_a, right_b)
    d_out = second_away(g_flip, dmbs, pair_after(d_core, dob))
    d_first = pair_sent(d_out, 4, 2)
    dob = swapped(dob, None)
    gain_part = jnp.sum(dob[:, 0, rows : rows + 8, :].astype(F32), axis=0)
    u_rights = pair_after(rights, *d_out)
    u_out = first_away(in_flip, (u_rights[0], after(u_rights[1], dob)))
    u_core = pair_sent(u_out, 1, 1)
    back = ()
    for mb in range(batch):
        back = attend_back(
            after(info, *u_out, *back), docs, mb, qkv, 0, qkv, 1, 2, dob, attended, lse, cos_all,
            sin_all, cos_all, sin_all, back,
        )
        if mb == 0:
            u_out = second_away(in_flip, rights, pair_after(u_core, *back))
            u_first = pair_sent(u_out, 4, 2)
            d_out = third_away(g_flip, dmbs, d_core, pair_after(d_first, *u_out))
            d_second = pair_sent(d_out, 2, 4)
            info = after(info, *d_out)
    dqkv = back[0].reshape(ctx_size, count, 3 * lanes)
    du_keep, du_away, qkv_part = tail_products(dqkv, u_run, w_heads, gain_part)
    u_out = third_away(in_flip, rights, u_core, pair_after(u_first, qkv_part))
    u_second = pair_sent(u_out, 2, 4)
    total = last_total(g_flip, dmbs, d_core, d_first, pair_after(d_second, *u_out))
    d_near = fold_first(total)
    d_near_in = sent(d_near, flips(8))
    du_in = sent(after(du_away, d_near), flips(1))
    q_near = fold_first(after(qkv_part, d_near))
    q_near_in = sent(q_near, flips(8))
    _, y_bit, x_bit, _ = bits()
    kept = summed(du_keep, after(du_in, q_near)).reshape(2, 2, count, width)
    kept = halves(kept)
    out = picked(kept[0], 1 - y_bit, 0), picked(kept[1], 1 - x_bit, 1)
    kept = picked(kept[0], y_bit, 0), picked(kept[1], x_bit, 1)
    got = pair_sent(out, 4, 2)
    u_total = last_total(in_flip, rights, u_core, u_first, pair_after(u_second, *out))
    u_near = fold_first(u_total)
    u_near_in = sent(u_near, flips(8))
    q_next = fold_second(qkv_part, after(q_near_in, u_near))
    q_next_in = sent(q_next, flips(16))
    d_next = fold_second(total, after(d_near_in, q_next))
    d_next_in = sent(d_next, flips(16))
    kept = [summed(*both) for both in zip(kept, pair_after(got, d_next))]
    out = picked(kept[0], 1 - x_bit, 0), picked(kept[1], 1 - y_bit, 0)
    kept = picked(kept[0], x_bit, 0), picked(kept[1], y_bit, 0)
    got = pair_sent(out, 2, 4)
    grad_qkv = fold_last(qkv_part, q_near_in, after(q_next_in, *out))
    size = width // shards
    gain_pair = grad_qkv[size : size + 2, : size // ctx_size].T
    qkv_last = swapped(grad_qkv[:size].reshape(ctx_size, -1, 3 * lanes), None)
    u_next = fold_second(u_total, after(u_near_in, grad_qkv))
    u_next_in = sent(u_next, flips(16))
    grad_tokens = finish_tokens(kept, pair_after(got, u_next), x, dh, gain_all)
    grad_down = fold_last(total, d_near_in, after(d_next_in, grad_tokens))
    grad_in = fold_last(u_total, u_near_in, after(u_next_in, grad_down))
    grad_qkv = after(qkv_last, grad_in)
    grad_out, grad_up = grad_in[:, :width], grad_in[:, width:]

    grad_qkv = grad_qkv.reshape(ctx_size, -1, 3, lanes).transpose(1, 2, 0, 3)
    grad_qkv = grad_qkv.reshape(-1, 3 * width)

    own_gains = picked(gains.reshape(ctx_size, -1, kinds), place, 0).astype(F32)
    row_sum = lambda weight, grad: jnp.sum(
        picked(split(weight), place, 0).astype(F32) * grad, axis=1
    )
    gain_one = row_sum(w_qkv, grad_qkv) / own_gains[:, 0]
    gain_three = row_sum(w_up, grad_up) / own_gains[:, 2]
    grad_gains = jnp.stack([gain_one, gain_pair[:, 0], gain_three, gain_pair[:, 1]], axis=1)
    return (
        layer_out.reshape(batch, rows, width),
        grad_tokens.reshape(batch, rows, width),
        grad_qkv,
        grad_out,
        grad_up,
        grad_down,
        grad_gains,
    )


def per_device(*args):
    return staged(*args) if cube() else plain(*args)


def solution(mesh):
    return jax.shard_map(
        per_device,
        mesh=mesh,
        in_specs=(
            P(None, ALL, None),
            P(None, "shard", None),
            P("shard", None),
            P("shard", None),
            P("shard", None),
            P("shard", None),
            P("shard", None),
            P(None, ALL, None),
        ),
        out_specs=(
            P(None, ALL, None),
            P(None, ALL, None),
            P(ALL, None),
            P(ALL, None),
            P(ALL, None),
            P(ALL, None),
            P(ALL, None),
        ),
        check_vma=False,
    )
```
